128 devices in a mesh: agg: 8 (over y, core), blk: 16 (over x, z).
Axes of the slice: x: 4, y: 4, z: 4, core: 2. Of those that a mesh axis runs over, the one named last changes fastest.
Arguments:
- right_side: float32 [256, 512, 128], P('blk', 'agg'), may hold values from -8 to 8
- coefficient: float32 [256, 512, 128], P('blk', 'agg'), may hold values from 0.05 to 2
Outputs:
- pressure: float32 [256, 512, 128], P('blk', 'agg')
The draws below stay inside these ranges and needn't reach their ends.
All inputs are finite; a program needn't handle non-finite values.
Results may differ from the reference program's by a relative error of at most 0.0001.
Values sent between devices are 32-bit elements; how exact they have to be, the bound alone decides.
No kernel may reach another device: no remote copies, remote signals or barrier semaphores. Data moves between devices by JAX's collectives and lax.ppermute only.
A program may use at most 128 MiB of HBM per device.

```python
import math
import jax
import jax.numpy as jnp

CY = 64
LEVELS = 3
NX = 256
NY = 512
NZ = 128


def block_scale(own_key, shape, split, smallest, top_value):
    gain = 1.0
    for axis_at, blocks in split:
        steps = jax.random.uniform(jax.random.fold_in(jax.random.fold_in(own_key, 6), axis_at), (blocks,), jnp.float32, smallest / len(split), top_value / len(split))
        gain = gain * jnp.repeat(jnp.exp(steps), shape[axis_at] // blocks).reshape((-1,) + (1,) * (len(shape) - 1 - axis_at))
    return gain


def scatter_about(rng, dims, deviation, most, pieces=(), kind=jnp.bfloat16):
    drawn = jax.random.normal(rng, dims, jnp.float32) * deviation
    if len(pieces) > 0:
        drawn = block_scale(rng, dims, pieces, -0.22, 0.18) * drawn
    return jnp.clip(drawn, min=-most, max=most).astype(kind)


def setup_inputs(seed: int = 0) -> dict:
    key_list = jax.random.split(jax.random.key(seed), 3)
    return {
        "right_side": scatter_about(key_list[0], (NX, NY, NZ), 1.0, 8.0, ((0, 16), (1, 8)), jnp.float32),
        "coefficient": jnp.clip(jnp.exp(math.log(2.0) - 3.6888794 * jax.random.uniform(key_list[1], (NX, NY, NZ), jnp.float32) ** block_scale(key_list[1], (NX, NY, NZ), ((0, 16), (1, 8)), -0.2, 0.2)), 0.05, 2.0),
    }


OMEGA = 0.8


def neighbours(v, window):
    nx, ny, nz = v.shape
    p = jnp.pad(v, ((1, 1), (0, 0), (1, 1)))
    total = p[2:, :, 1:-1] + p[:-2, :, 1:-1] + p[1:-1, :, 2:] + p[1:-1, :, :-2]
    if window == 0:
        q = jnp.pad(v, ((0, 0), (1, 1), (0, 0)))
        total = total + q[:, 2:] + q[:, :-2]
    else:
        w = v.reshape(nx, ny // window, window, nz)
        q = jnp.pad(w, ((0, 0), (0, 0), (1, 1), (0, 0)))
        total = total + (q[:, :, 2:] + q[:, :, :-2]).reshape(nx, ny, nz)
    return total


def operate(v, coef, window):
    return (6.0 + coef) * v - neighbours(v, window)


def smooth(v, rhs, coef, window):
    return v + OMEGA * (rhs - operate(v, coef, window)) / (6.0 + coef)


def restrict(v):
    nx, ny, nz = v.shape
    return v.reshape(nx // 2, 2, ny // 2, 2, nz // 2, 2).sum(axis=(1, 3, 5)) * 0.5


def prolong(v):
    return jnp.repeat(jnp.repeat(jnp.repeat(v, 2, axis=0), 2, axis=1), 2, axis=2)


def reference(right_side, coefficient):
    fine = OMEGA * right_side / (6.0 + coefficient)
    fine = smooth(fine, right_side, coefficient, 0)
    resid = right_side - operate(fine, coefficient, 0)
    rhs_list = [right_side]
    coef_list = [coefficient]
    err_list = [fine]
    for level in range(1, LEVELS + 1):
        target = restrict(resid)
        coef = restrict(coef_list[-1])
        err = OMEGA * target / (6.0 + coef)
        if level == LEVELS:
            err = smooth(err, target, coef, CY)
        else:
            resid = target - operate(err, coef, CY)
        rhs_list.append(target)
        coef_list.append(coef)
        err_list.append(err)
    for level in range(LEVELS, 0, -1):
        window = CY if level > 1 else 0
        merged = err_list[level - 1] + prolong(err_list[level])
        err_list[level - 1] = smooth(merged, rhs_list[level - 1], coef_list[level - 1], window)
    return err_list[0]
```

```python
import jax
import jax.numpy as jnp
from jax import lax
from jax.experimental import pallas as pl
from jax.experimental.pallas import tpu as pltpu
from jax.sharding import PartitionSpec as P

OMEGA = 0.8
F32 = jnp.float32
WINDOW = 64
VM = pl.BlockSpec(memory_space=pltpu.VMEM)
SM = pl.BlockSpec(memory_space=pltpu.SMEM)


def shape(*dims):
    return jax.ShapeDtypeStruct(dims, F32)


def call(body, outs, scratch, *args):
    return pl.pallas_call(
        body,
        out_shape=outs,
        in_specs=[SM] + [VM] * (len(args) - 1),
        out_specs=tuple(VM for _ in outs),
        scratch_shapes=[pltpu.VMEM(s, F32) for s in scratch],
        compiler_params=pltpu.CompilerParams(vmem_limit_bytes=56 << 20),
    )(*args)


def iota(rows, axis):
    return lax.broadcasted_iota(jnp.int32, (rows, 128), axis)


def pair_matrix(down):
    i, j = iota(128, 0), iota(128, 1)
    return jnp.where((i >> 1) == j if down else i == (j >> 1), 1.0, 0.0).astype(F32)


def dot(a, m):
    return jnp.dot(a, m, preferred_element_type=F32, precision=lax.Precision.HIGHEST)


def turn(v, by, axis):
    return pltpu.roll(v, by % v.shape[axis], axis)


def z_sum(v):
    lane = iota(v.shape[0], 1)
    below = jnp.where(lane == 0, 0.0, turn(v, 1, 1))
    return below + jnp.where(lane == 127, 0.0, turn(v, -1, 1))


def plane_sum(v):
    return turn(v, 1, 0) + turn(v, -1, 0) + z_sum(v)


def windowed_sum(v, row):
    at = row & (WINDOW - 1)
    below = jnp.where(at == 0, 0.0, turn(v, 1, 0))
    above = jnp.where(at == WINDOW - 1, 0.0, turn(v, -1, 0))
    return below + above + turn(v, 1, 1) + turn(v, -1, 1)


def inside(at, size):
    return (at >= 0) & (at < size)


def row_pairs(ref, k, rows):
    return ref[k, pl.ds(0, rows, stride=2), :] + ref[k, pl.ds(1, rows, stride=2), :]


def spread_rows(ref, k, v):
    rows = v.shape[0]
    ref[k, pl.ds(0, rows, stride=2), :] = v
    ref[k, pl.ds(1, rows, stride=2), :] = v


def down_kernel(
    blocks, aggs,
    at, b, c, xe, xo, ye, yo,
    p0, vown, wown, e1, w1, bc2, se, so,
    v, w, q, bx, cx, rs, b1, c1, r1,
):
    bi, ai = at[0], at[1]
    x_even, y_even = (bi & 1) == 0, (ai & 1) == 0
    y_lo = jnp.where(ai > 0, 1.0, 0.0)
    y_hi = jnp.where(ai < aggs - 1, 1.0, 0.0)

    def put(p, rows, bb, cc, scale):
        ww = scale / (6.0 + cc)
        vv = ww * bb
        w[p, rows], v[p, rows], bx[p, rows], cx[p, rows] = ww, vv, bb, cc
        return vv, ww

    def plane(p, bb, cc, scale):
        out = put(p, pl.ds(8, 64), bb, cc, scale)
        lo = [jnp.where(y_even, yo[k, p], ye[k, p]) for k in (0, 1)]
        hi = [jnp.where(y_even, ye[k, p], yo[k, p]) for k in (0, 1)]
        put(p, pl.ds(4, 4), *lo, scale * y_lo)
        put(p, pl.ds(72, 4), *hi, scale * y_hi)
        return out

    def own(i, carry):
        vown[i], wown[i] = plane(i + 4, b[i], c[i], OMEGA)
        return carry

    def edge(i, carry):
        lo = [jnp.where(x_even, xo[k, i], xe[k, i]) for k in (0, 1)]
        hi = [jnp.where(x_even, xe[k, i], xo[k, i]) for k in (0, 1)]
        plane(i, *lo, jnp.where(bi > 0, OMEGA, 0.0))
        plane(i + 20, *hi, jnp.where(bi < blocks - 1, OMEGA, 0.0))
        return carry

    lax.fori_loop(0, 16, own, 0)
    lax.fori_loop(0, 4, edge, 0)

    def smooth(p, carry):
        vv = v[p]
        qq = 0.4 * vv + w[p] * (v[p - 1] + v[p + 1] + plane_sum(vv))
        q[p] = qq
        return carry

    lax.fori_loop(1, 23, smooth, 0)

    def first(k, carry):
        p0[k] = q[k + 3] + OMEGA * v[k + 3]
        return carry

    lax.fori_loop(0, 18, first, 0)

    half = 0.5 * pair_matrix(True)

    def resid(p):
        return 0.04 * bx[p] + (q[p - 1] + q[p + 1] + plane_sum(q[p]))

    row1 = ai * 32 - 4 + iota(40, 0)
    keep1 = inside(row1, 32 * aggs) & (iota(40, 1) < 64)

    def coarse(k, carry):
        p = 2 + 2 * k
        rs[0] = resid(p) + resid(p + 1)
        rs[1] = cx[p] + cx[p + 1]
        both = jnp.concatenate([row_pairs(rs, 0, 40), row_pairs(rs, 1, 40)], axis=0)
        both = dot(both, half)
        bb, cc = both[:40], both[40:]
        ok = keep1 & inside(bi * 8 + k - 1, 8 * blocks)
        ww = jnp.where(ok, OMEGA / (6.0 + cc), 0.0)
        b1[k], c1[k] = bb, cc
        w1[k + 1] = ww
        e1[k + 1] = jnp.where(ok, ww * bb, 0.0)
        return carry

    lax.fori_loop(0, 10, coarse, 0)

    def resid1(k):
        near = e1[k] + e1[k + 2] + windowed_sum(e1[k + 1], row1)
        return 0.2 * b1[k] + near

    lane16 = iota(16, 1)

    def coarse2(k, carry):
        p = 1 + 2 * k
        r1[0] = resid1(p) + resid1(p + 1)
        r1[1] = c1[p] + c1[p + 1]
        pairs = [r1[i, pl.ds(4, 16, stride=2), :] + r1[i, pl.ds(5, 16, stride=2), :] for i in (0, 1)]
        both = dot(jnp.concatenate(pairs, axis=0), half)
        bb = jnp.where(lane16 < 32, both[:16], 0.0)
        cc = jnp.where(lane16 < 32, both[16:], 0.0)
        mix = bb + turn(cc, 32, 1)
        bc2[k] = mix
        for ref, lo_side in ((se, jnp.logical_not(y_even)), (so, y_even)):
            ref[k, 0:5] = jnp.where(lo_side, mix[0:5], mix[11:16])
            for j in (0, 1):
                n = 2 + 2 * k + j
                ref[k, 5 + j : 6 + j] = jnp.where(lo_side, e1[n, 5:6], e1[n, 34:35])
            ref[k, 7:8] = jnp.zeros((1, 128), F32)
        return carry

    lax.fori_loop(0, 4, coarse2, 0)


def join_kernel(at, bc2, ye, yo, e1, wide, se, so, sf, sg):
    bi, ai = at[0], at[1]
    x_even, y_even = (bi & 1) == 0, (ai & 1) == 0
    low_pair = (bi & 2) == 0
    for k in range(4):
        wide[k] = jnp.zeros((32, 128), F32)
        wide[k, 3:8] = jnp.where(y_even, yo[k, 0:5], ye[k, 0:5])
        wide[k, 8:24] = bc2[k]
        wide[k, 24:29] = jnp.where(y_even, ye[k, 0:5], yo[k, 0:5])
        se[k] = wide[k]
        so[k] = wide[k]
    up, down = e1[8, 4:36], e1[3, 4:36]
    se[4] = jnp.where(x_even, up, down)
    so[4] = jnp.where(x_even, down, up)
    sf[0] = jnp.where(low_pair, wide[3], wide[0])
    sg[0] = jnp.where(low_pair, wide[0], wide[3])


def up_kernel(
    blocks, aggs,
    at, p0, vown, wown, e1in, w1, wide, ye, yo, xe, xo, xf, xg,
    out,
    bc, e2, w2, b2, c2, rs, b3, e3, w3, pe2, m2, t2, e1, pe1, m1, mf,
):
    bi, ai = at[0], at[1]
    x_even, y_even = (bi & 1) == 0, (ai & 1) == 0
    low_pair = (bi & 2) == 0
    half, twice = 0.5 * pair_matrix(True), pair_matrix(False)

    bc[0] = jnp.where(low_pair, xg[0], xf[0])
    bc[13] = jnp.where(low_pair, xf[0], xg[0])
    for k in range(4):
        bc[1 + k] = jnp.where(x_even, xo[k], xe[k])
        bc[5 + k] = wide[k]
        bc[9 + k] = jnp.where(x_even, xe[k], xo[k])

    row2 = ai * 16 - 8 + iota(32, 0)
    lane2 = iota(32, 1) < 32
    keep2 = inside(row2, 16 * aggs) & lane2
    for k in range(14):
        mix = bc[k]
        bb = jnp.where(lane2, mix, 0.0)
        cc = jnp.where(lane2, turn(mix, -32, 1), 0.0)
        ww = jnp.where(keep2 & inside(bi * 4 + k - 5, 4 * blocks), OMEGA / (6.0 + cc), 0.0)
        b2[k], c2[k], w2[k], e2[k] = bb, cc, ww, ww * bb

    def resid2(k):
        return 0.2 * b2[k] + (e2[k - 1] + e2[k + 1] + windowed_sum(e2[k], row2))

    for j in range(6):
        k = 1 + 2 * j
        rs[j] = resid2(k) + resid2(k + 1)
        rs[6 + j] = c2[k] + c2[k + 1]
    both = dot(jnp.concatenate([row_pairs(rs, j, 16) for j in range(12)], axis=0), half)
    row3 = ai * 8 - 4 + iota(16, 0)
    keep3 = inside(row3, 8 * aggs) & (iota(16, 1) < 16)
    for j in range(6):
        bb, cc = both[16 * j : 16 * j + 16], both[96 + 16 * j : 112 + 16 * j]
        ww = jnp.where(keep3 & inside(bi * 2 + j - 2, 2 * blocks), OMEGA / (6.0 + cc), 0.0)
        w3[j], e3[j] = ww, ww * bb
    solved = []
    for j in range(1, 5):
        near = e3[j - 1] + e3[j + 1] + windowed_sum(e3[j], row3)
        solved.append(1.2 * e3[j] + w3[j] * near)
    wider = dot(jnp.concatenate(solved, axis=0), twice)
    for j in range(4):
        spread_rows(pe2, j, wider[16 * j : 16 * j + 16])
    for k in range(3, 11):
        m2[k] = e2[k] + pe2[(k - 3) // 2]
    solved = []
    for k in range(4, 10):
        near = m2[k - 1] + m2[k + 1] + windowed_sum(m2[k], row2)
        solved.append(0.2 * m2[k] + e2[k] + w2[k] * near)
    wider = dot(jnp.concatenate(solved, axis=0), twice)
    for k in range(6):
        t2[k] = wider[32 * k : 32 * k + 32]
        spread_rows(pe1, k, t2[k, 6:26])

    for k in range(1, 11):
        e1[k] = e1in[k]
    for k in (0, 11):
        e1[k] = jnp.zeros((40, 128), F32)
    e1[0, 4:36] = jnp.where(x_even, xo[4], xe[4])
    e1[11, 4:36] = jnp.where(x_even, xe[4], xo[4])
    for n in range(8):
        k, j = n // 2, n % 2
        mine, other = ye[k, 5 + j : 6 + j], yo[k, 5 + j : 6 + j]
        e1[n + 2, 2:3] = jnp.where(y_even, other, mine)
        e1[n + 2, 37:38] = jnp.where(y_even, mine, other)
    for k in range(12):
        m1[k] = e1[k] + pe1[k // 2]
    row1 = ai * 32 - 4 + iota(40, 0)

    def fine(k, carry):
        near = m1[k] + m1[k + 2] + windowed_sum(m1[k + 1], row1)
        v = 0.2 * m1[k + 1] + e1[k + 1] + w1[k + 1] * near
        spread_rows(rs80, k, dot(v, twice))
        return carry

    rs80 = mf.at[pl.ds(18, 10)]
    lax.fori_loop(0, 10, fine, 0)

    def merge(k, carry):
        mf[k] = p0[k] + mf[18 + (k + 1) // 2]
        return carry

    lax.fori_loop(0, 18, merge, 0)

    def last(k, carry):
        m = mf[k + 1]
        near = (plane_sum(m) + mf[k] + mf[k + 2])[8:72]
        out[k] = 0.2 * m[8:72] + vown[k] + wown[k] * near
        return carry

    lax.fori_loop(0, 16, last, 0)


def swaps(size, apart):
    inner = [(i, i ^ apart) for i in range(size)]
    outer = []
    for i in range(apart, size - apart):
        if i & apart:
            outer += [(i, i + apart), (i + apart, i)]
    return inner, outer


def shards(b, c):
    blocks, aggs = lax.axis_size("blk"), lax.axis_size("agg")
    bi, ai = lax.axis_index("blk"), lax.axis_index("agg")
    at = jnp.stack([bi, ai]).astype(jnp.int32)
    x_even, y_even = (bi & 1) == 0, (ai & 1) == 0
    near_in, near_out = swaps(blocks, 1)
    far_in, far_out = swaps(blocks, 2)
    side_in, side_out = swaps(aggs, 1)

    first = jnp.stack([b[:4], c[:4]])
    last = jnp.stack([b[12:], c[12:]])
    xe = lax.ppermute(jnp.where(x_even, last, first), "blk", near_in)
    xo = lax.ppermute(jnp.where(x_even, first, last), "blk", near_out)
    lo, hi = jnp.where(x_even, xo, xe), jnp.where(x_even, xe, xo)

    def rows(cut):
        own = jnp.stack([b[:, cut], c[:, cut]])
        return jnp.concatenate([lo[:, :, cut], own, hi[:, :, cut]], axis=1)

    first, last = rows(slice(0, 4)), rows(slice(60, 64))
    ye = lax.ppermute(jnp.where(y_even, last, first), "agg", side_in)
    yo = lax.ppermute(jnp.where(y_even, first, last), "agg", side_out)

    big, mid = (24, 80, 128), (12, 40, 128)
    p0, vown, wown, e1, w1, bc2, se, so = call(
        lambda *refs: down_kernel(blocks, aggs, *refs),
        (shape(18, 80, 128), shape(16, 64, 128), shape(16, 64, 128), shape(*mid), shape(*mid),
         shape(4, 16, 128), shape(4, 8, 128), shape(4, 8, 128)),
        [big] * 5 + [(2, 80, 128), mid, mid, (2, 40, 128)],
        at, b, c, xe, xo, ye, yo,
    )
    ye = lax.ppermute(se, "agg", side_in)
    yo = lax.ppermute(so, "agg", side_out)
    wide, se, so, sf, sg = call(
        join_kernel,
        (shape(4, 32, 128), shape(5, 32, 128), shape(5, 32, 128), shape(1, 32, 128), shape(1, 32, 128)),
        [],
        at, bc2, ye, yo, e1,
    )
    xe = lax.ppermute(se, "blk", near_in)
    xo = lax.ppermute(so, "blk", near_out)
    xf = lax.ppermute(sf, "blk", far_in)
    xg = lax.ppermute(sg, "blk", far_out)
    small = (14, 32, 128)
    (out,) = call(
        lambda *refs: up_kernel(blocks, aggs, *refs),
        (shape(16, 64, 128),),
        [small] * 5 + [(12, 32, 128), (6, 16, 128), (6, 16, 128), (6, 16, 128), (4, 32, 128),
                       small, (6, 32, 128), mid, (6, 40, 128), mid, (28, 80, 128)],
        at, p0, vown, wown, e1, w1, wide, ye, yo, xe, xo, xf, xg,
    )
    return out


def solution(mesh):
    placed = (P("blk", "agg", None), P("blk", "agg", None))
    return jax.shard_map(
        shards, mesh=mesh, in_specs=placed, out_specs=P("blk", "agg", None), check_vma=False
    )
```

```python
import jax
import jax.numpy as jnp
from jax import lax
from jax.experimental import pallas as pl
from jax.experimental.pallas import tpu as pltpu
from jax.sharding import PartitionSpec as P

OMEGA = 0.8
F32 = jnp.float32
WINDOW = 64
VM = pl.BlockSpec(memory_space=pltpu.VMEM)
SM = pl.BlockSpec(memory_space=pltpu.SMEM)


def shape(*dims):
    return jax.ShapeDtypeStruct(dims, F32)


def call(body, outs, scratch, *args):
    return pl.pallas_call(
        body,
        out_shape=outs,
        in_specs=[SM] + [VM] * (len(args) - 1),
        out_specs=tuple(VM for _ in outs),
        scratch_shapes=[pltpu.VMEM(s, F32) for s in scratch],
        compiler_params=pltpu.CompilerParams(vmem_limit_bytes=56 << 20),
    )(*args)


def iota(rows, axis):
    return lax.broadcasted_iota(jnp.int32, (rows, 128), axis)


def pair_matrix(down):
    i, j = iota(128, 0), iota(128, 1)
    return jnp.where((i >> 1) == j if down else i == (j >> 1), 1.0, 0.0).astype(F32)


def dot(a, m):
    return jnp.dot(a, m, preferred_element_type=F32, precision=lax.Precision.HIGHEST)


def turn(v, by, axis):
    return pltpu.roll(v, by % v.shape[axis], axis)


def z_sum(v):
    lane = iota(v.shape[0], 1)
    below = jnp.where(lane == 0, 0.0, turn(v, 1, 1))
    return below + jnp.where(lane == 127, 0.0, turn(v, -1, 1))


def plane_sum(v):
    return turn(v, 1, 0) + turn(v, -1, 0) + z_sum(v)


def windowed_sum(v, row):
    at = row & (WINDOW - 1)
    below = jnp.where(at == 0, 0.0, turn(v, 1, 0))
    above = jnp.where(at == WINDOW - 1, 0.0, turn(v, -1, 0))
    return below + above + turn(v, 1, 1) + turn(v, -1, 1)


def inside(at, size):
    return (at >= 0) & (at < size)


def row_pairs(ref, k, rows):
    return ref[k, pl.ds(0, rows, stride=2), :] + ref[k, pl.ds(1, rows, stride=2), :]


def spread_rows(ref, k, v):
    rows = v.shape[0]
    ref[k, pl.ds(0, rows, stride=2), :] = v
    ref[k, pl.ds(1, rows, stride=2), :] = v


def down_kernel(
    blocks, aggs,
    at, b, c, xe, xo, ye, yo,
    p0, vown, wown, e1, w1, bc2, se, so,
    v, w, q, bx, cx, rs, b1, c1, r1,
):
    bi, ai = at[0], at[1]
    x_even, y_even = (bi & 1) == 0, (ai & 1) == 0
    y_lo = jnp.where(ai > 0, 1.0, 0.0)
    y_hi = jnp.where(ai < aggs - 1, 1.0, 0.0)

    def put(p, rows, bb, cc, scale):
        ww = scale / (6.0 + cc)
        vv = ww * bb
        w[p, rows], v[p, rows], bx[p, rows], cx[p, rows] = ww, vv, bb, cc
        return vv, ww

    def plane(p, bb, cc, scale):
        out = put(p, pl.ds(8, 64), bb, cc, scale)
        lo = [jnp.where(y_even, yo[k, p], ye[k, p]) for k in (0, 1)]
        hi = [jnp.where(y_even, ye[k, p], yo[k, p]) for k in (0, 1)]
        put(p, pl.ds(4, 4), *lo, scale * y_lo)
        put(p, pl.ds(72, 4), *hi, scale * y_hi)
        return out

    def own(i, carry):
        vown[i], wown[i] = plane(i + 4, b[i], c[i], OMEGA)
        return carry

    def edge(i, carry):
        lo = [jnp.where(x_even, xo[k, i], xe[k, i]) for k in (0, 1)]
        hi = [jnp.where(x_even, xe[k, i], xo[k, i]) for k in (0, 1)]
        plane(i, *lo, jnp.where(bi > 0, OMEGA, 0.0))
        plane(i + 20, *hi, jnp.where(bi < blocks - 1, OMEGA, 0.0))
        return carry

    lax.fori_loop(0, 16, own, 0)
    lax.fori_loop(0, 4, edge, 0)

    def smooth(p, carry):
        vv = v[p]
        qq = 0.4 * vv + w[p] * (v[p - 1] + v[p + 1] + plane_sum(vv))
        q[p] = qq
        return carry

    lax.fori_loop(1, 23, smooth, 0)

    def first(k, carry):
        p0[k] = q[k + 3] + OMEGA * v[k + 3]
        return carry

    lax.fori_loop(0, 18, first, 0)

    half = 0.5 * pair_matrix(True)

    def resid(p):
        return 0.04 * bx[p] + (q[p - 1] + q[p + 1] + plane_sum(q[p]))

    row1 = ai * 32 - 4 + iota(40, 0)
    keep1 = inside(row1, 32 * aggs) & (iota(40, 1) < 64)

    def coarse(k, carry):
        p = 2 + 2 * k
        rs[0] = resid(p) + resid(p + 1)
        rs[1] = cx[p] + cx[p + 1]
        both = jnp.concatenate([row_pairs(rs, 0, 40), row_pairs(rs, 1, 40)], axis=0)
        both = dot(both, half)
        bb, cc = both[:40], both[40:]
        ok = keep1 & inside(bi * 8 + k - 1, 8 * blocks)
        ww = jnp.where(ok, OMEGA / (6.0 + cc), 0.0)
        b1[k], c1[k] = bb, cc
        w1[k + 1] = ww
        e1[k + 1] = jnp.where(ok, ww * bb, 0.0)
        return carry

    lax.fori_loop(0, 10, coarse, 0)

    def resid1(k):
        near = e1[k] + e1[k + 2] + windowed_sum(e1[k + 1], row1)
        return 0.2 * b1[k] + near

    lane16 = iota(16, 1)

    def coarse2(k, carry):
        p = 1 + 2 * k
        r1[0] = resid1(p) + resid1(p + 1)
        r1[1] = c1[p] + c1[p + 1]
        pairs = [r1[i, pl.ds(4, 16, stride=2), :] + r1[i, pl.ds(5, 16, stride=2), :] for i in (0, 1)]
        both = dot(jnp.concatenate(pairs, axis=0), half)
        bb = jnp.where(lane16 < 32, both[:16], 0.0)
        cc = jnp.where(lane16 < 32, both[16:], 0.0)
        mix = bb + turn(cc, 32, 1)
        bc2[k] = mix
        for ref, lo_side in ((se, jnp.logical_not(y_even)), (so, y_even)):
            ref[k, 0:5] = jnp.where(lo_side, mix[0:5], mix[11:16])
            for j in (0, 1):
                n = 2 + 2 * k + j
                ref[k, 5 + j : 6 + j] = jnp.where(lo_side, e1[n, 5:6], e1[n, 34:35])
            ref[k, 7:8] = jnp.zeros((1, 128), F32)
        return carry

    lax.fori_loop(0, 4, coarse2, 0)


def join_kernel(at, bc2, ye, yo, e1, wide, se, so, sf, sg):
    bi, ai = at[0], at[1]
    x_even, y_even = (bi & 1) == 0, (ai & 1) == 0
    low_pair = (bi & 2) == 0
    for k in range(4):
        wide[k] = jnp.zeros((32, 128), F32)
        wide[k, 3:8] = jnp.where(y_even, yo[k, 0:5], ye[k, 0:5])
        wide[k, 8:24] = bc2[k]
        wide[k, 24:29] = jnp.where(y_even, ye[k, 0:5], yo[k, 0:5])
        se[k] = wide[k]
        so[k] = wide[k]
    up, down = e1[8, 4:36], e1[3, 4:36]
    se[4] = jnp.where(x_even, up, down)
    so[4] = jnp.where(x_even, down, up)
    sf[0] = jnp.where(low_pair, wide[3], wide[0])
    sg[0] = jnp.where(low_pair, wide[0], wide[3])


def up_kernel(
    blocks, aggs,
    at, p0, vown, wown, e1in, w1, wide, ye, yo, xe, xo, xf, xg,
    out,
    bc, e2, w2, b2, c2, rs, b3, e3, w3, pe2, m2, t2, e1, pe1, m1, mf,
):
    bi, ai = at[0], at[1]
    x_even, y_even = (bi & 1) == 0, (ai & 1) == 0
    low_pair = (bi & 2) == 0
    half, twice = 0.5 * pair_matrix(True), pair_matrix(False)

    bc[0] = jnp.where(low_pair, xg[0], xf[0])
    bc[13] = jnp.where(low_pair, xf[0], xg[0])
    for k in range(4):
        bc[1 + k] = jnp.where(x_even, xo[k], xe[k])
        bc[5 + k] = wide[k]
        bc[9 + k] = jnp.where(x_even, xe[k], xo[k])

    row2 = ai * 16 - 8 + iota(32, 0)
    lane2 = iota(32, 1) < 32
    keep2 = inside(row2, 16 * aggs) & lane2
    for k in range(14):
        mix = bc[k]
        bb = jnp.where(lane2, mix, 0.0)
        cc = jnp.where(lane2, turn(mix, -32, 1), 0.0)
        ww = jnp.where(keep2 & inside(bi * 4 + k - 5, 4 * blocks), OMEGA / (6.0 + cc), 0.0)
        b2[k], c2[k], w2[k], e2[k] = bb, cc, ww, ww * bb

    def resid2(k):
        return 0.2 * b2[k] + (e2[k - 1] + e2[k + 1] + windowed_sum(e2[k], row2))

    for j in range(6):
        k = 1 + 2 * j
        rs[j] = resid2(k) + resid2(k + 1)
        rs[6 + j] = c2[k] + c2[k + 1]
    both = dot(jnp.concatenate([row_pairs(rs, j, 16) for j in range(12)], axis=0), half)
    row3 = ai * 8 - 4 + iota(16, 0)
    keep3 = inside(row3, 8 * aggs) & (iota(16, 1) < 16)
    for j in range(6):
        bb, cc = both[16 * j : 16 * j + 16], both[96 + 16 * j : 112 + 16 * j]
        ww = jnp.where(keep3 & inside(bi * 2 + j - 2, 2 * blocks), OMEGA / (6.0 + cc), 0.0)
        w3[j], e3[j] = ww, ww * bb
    solved = []
    for j in range(1, 5):
        near = e3[j - 1] + e3[j + 1] + windowed_sum(e3[j], row3)
        solved.append(1.2 * e3[j] + w3[j] * near)
    wider = dot(jnp.concatenate(solved, axis=0), twice)
    for j in range(4):
        spread_rows(pe2, j, wider[16 * j : 16 * j + 16])
    for k in range(3, 11):
        m2[k] = e2[k] + pe2[(k - 3) // 2]
    solved = []
    for k in range(4, 10):
        near = m2[k - 1] + m2[k + 1] + windowed_sum(m2[k], row2)
        solved.append(0.2 * m2[k] + e2[k] + w2[k] * near)
    wider = dot(jnp.concatenate(solved, axis=0), twice)
    for k in range(6):
        t2[k] = wider[32 * k : 32 * k + 32]
        spread_rows(pe1, k, t2[k, 6:26])

    for k in range(1, 11):
        e1[k] = e1in[k]
    for k in (0, 11):
        e1[k] = jnp.zeros((40, 128), F32)
    e1[0, 4:36] = jnp.where(x_even, xo[4], xe[4])
    e1[11, 4:36] = jnp.where(x_even, xe[4], xo[4])
    for n in range(8):
        k, j = n // 2, n % 2
        mine, other = ye[k, 5 + j : 6 + j], yo[k, 5 + j : 6 + j]
        e1[n + 2, 2:3] = jnp.where(y_even, other, mine)
        e1[n + 2, 37:38] = jnp.where(y_even, mine, other)
    for k in range(12):
        m1[k] = e1[k] + pe1[k // 2]
    row1 = ai * 32 - 4 + iota(40, 0)

    def fine(k, carry):
        near = m1[k] + m1[k + 2] + windowed_sum(m1[k + 1], row1)
        v = 0.2 * m1[k + 1] + e1[k + 1] + w1[k + 1] * near
        spread_rows(rs80, k, dot(v, twice))
        return carry

    rs80 = mf.at[pl.ds(18, 10)]
    lax.fori_loop(0, 10, fine, 0)

    def merge(k, carry):
        mf[k] = p0[k] + mf[18 + (k + 1) // 2]
        return carry

    lax.fori_loop(0, 18, merge, 0)

    def last(k, carry):
        m = mf[k + 1]
        near = (plane_sum(m) + mf[k] + mf[k + 2])[8:72]
        out[k] = 0.2 * m[8:72] + vown[k] + wown[k] * near
        return carry

    lax.fori_loop(0, 16, last, 0)


def swaps(size, apart):
    inner, outer = [], []
    for i in range(size):
        inner.append((i, i ^ apart))
        outer.append((i, (i + apart) % size if i & apart else (i - apart) % size))
    return inner, outer


def shards(b, c):
    blocks, aggs = lax.axis_size("blk"), lax.axis_size("agg")
    bi, ai = lax.axis_index("blk"), lax.axis_index("agg")
    at = jnp.stack([bi, ai]).astype(jnp.int32)
    x_even, y_even = (bi & 1) == 0, (ai & 1) == 0
    near_in, near_out = swaps(blocks, 1)
    far_in, far_out = swaps(blocks, 2)
    side_in, side_out = swaps(aggs, 1)

    first = jnp.stack([b[:4], c[:4]])
    last = jnp.stack([b[12:], c[12:]])
    xe = lax.ppermute(jnp.where(x_even, last, first), "blk", near_in)
    xo = lax.ppermute(jnp.where(x_even, first, last), "blk", near_out)
    lo, hi = jnp.where(x_even, xo, xe), jnp.where(x_even, xe, xo)

    def rows(cut):
        own = jnp.stack([b[:, cut], c[:, cut]])
        return jnp.concatenate([lo[:, :, cut], own, hi[:, :, cut]], axis=1)

    first, last = rows(slice(0, 4)), rows(slice(60, 64))
    ye = lax.ppermute(jnp.where(y_even, last, first), "agg", side_in)
    yo = lax.ppermute(jnp.where(y_even, first, last), "agg", side_out)

    big, mid = (24, 80, 128), (12, 40, 128)
    p0, vown, wown, e1, w1, bc2, se, so = call(
        lambda *refs: down_kernel(blocks, aggs, *refs),
        (shape(18, 80, 128), shape(16, 64, 128), shape(16, 64, 128), shape(*mid), shape(*mid),
         shape(4, 16, 128), shape(4, 8, 128), shape(4, 8, 128)),
        [big] * 5 + [(2, 80, 128), mid, mid, (2, 40, 128)],
        at, b, c, xe, xo, ye, yo,
    )
    ye = lax.ppermute(se, "agg", side_in)
    yo = lax.ppermute(so, "agg", side_out)
    wide, se, so, sf, sg = call(
        join_kernel,
        (shape(4, 32, 128), shape(5, 32, 128), shape(5, 32, 128), shape(1, 32, 128), shape(1, 32, 128)),
        [],
        at, bc2, ye, yo, e1,
    )
    xe = lax.ppermute(se, "blk", near_in)
    xo = lax.ppermute(so, "blk", near_out)
    xf = lax.ppermute(sf, "blk", far_in)
    xg = lax.ppermute(sg, "blk", far_out)
    small = (14, 32, 128)
    (out,) = call(
        lambda *refs: up_kernel(blocks, aggs, *refs),
        (shape(16, 64, 128),),
        [small] * 5 + [(12, 32, 128), (6, 16, 128), (6, 16, 128), (6, 16, 128), (4, 32, 128),
                       small, (6, 32, 128), mid, (6, 40, 128), mid, (28, 80, 128)],
        at, p0, vown, wown, e1, w1, wide, ye, yo, xe, xo, xf, xg,
    )
    return out


def solution(mesh):
    placed = (P("blk", "agg", None), P("blk", "agg", None))
    return jax.shard_map(
        shards, mesh=mesh, in_specs=placed, out_specs=P("blk", "agg", None), check_vma=False
    )
```

```python
import jax
import jax.numpy as jnp
from jax import lax
from jax.experimental import pallas as pl
from jax.experimental.pallas import tpu as pltpu
from jax.sharding import PartitionSpec as P

OMEGA = 0.8
F32 = jnp.float32
WINDOW = 64
VM = pl.BlockSpec(memory_space=pltpu.VMEM)
SM = pl.BlockSpec(memory_space=pltpu.SMEM)


def shape(*dims):
    return jax.ShapeDtypeStruct(dims, F32)


def call(body, outs, scratch, *args):
    return pl.pallas_call(
        body,
        out_shape=outs,
        in_specs=[SM] + [VM] * (len(args) - 1),
        out_specs=tuple(VM for _ in outs),
        scratch_shapes=[pltpu.VMEM(s, F32) for s in scratch],
        compiler_params=pltpu.CompilerParams(vmem_limit_bytes=16 << 20),
    )(*args)


def iota(rows, axis):
    return lax.broadcasted_iota(jnp.int32, (rows, 128), axis)


def pair_matrix(down):
    i, j = iota(128, 0), iota(128, 1)
    return jnp.where((i >> 1) == j if down else i == (j >> 1), 1.0, 0.0).astype(F32)


def dot(a, m):
    return jnp.dot(a, m, preferred_element_type=F32, precision=lax.Precision.HIGHEST)


def turn(v, by, axis):
    return pltpu.roll(v, by % v.shape[axis], axis)


def z_sum(v):
    lane = iota(v.shape[0], 1)
    below = jnp.where(lane == 0, 0.0, turn(v, 1, 1))
    return below + jnp.where(lane == 127, 0.0, turn(v, -1, 1))


def plane_sum(v):
    return turn(v, 1, 0) + turn(v, -1, 0) + z_sum(v)


def windowed_sum(v, row):
    at = row & (WINDOW - 1)
    below = jnp.where(at == 0, 0.0, turn(v, 1, 0))
    above = jnp.where(at == WINDOW - 1, 0.0, turn(v, -1, 0))
    return below + above + turn(v, 1, 1) + turn(v, -1, 1)


def inside(at, size):
    return (at >= 0) & (at < size)


def row_pairs(ref, k, rows):
    return ref[k, pl.ds(0, rows, stride=2), :] + ref[k, pl.ds(1, rows, stride=2), :]


def spread_rows(ref, k, v):
    rows = v.shape[0]
    ref[k, pl.ds(0, rows, stride=2), :] = v
    ref[k, pl.ds(1, rows, stride=2), :] = v


def down_kernel(
    blocks, aggs,
    at, b, c, xe, xo, ye, yo,
    p0, vown, wown, e1, w1, bc2, se, so,
    v, w, q, bx, cx, rs, b1, c1, r1,
):
    bi, ai = at[0], at[1]
    x_even, y_even = (bi & 1) == 0, (ai & 1) == 0
    y_lo = jnp.where(ai > 0, 1.0, 0.0)
    y_hi = jnp.where(ai < aggs - 1, 1.0, 0.0)

    def put(p, rows, bb, cc, scale):
        ww = scale / (6.0 + cc)
        vv = ww * bb
        w[p, rows], v[p, rows], bx[p, rows], cx[p, rows] = ww, vv, bb, cc
        return vv, ww

    def plane(p, bb, cc, scale):
        out = put(p, pl.ds(8, 64), bb, cc, scale)
        lo = [jnp.where(y_even, yo[k, p], ye[k, p]) for k in (0, 1)]
        hi = [jnp.where(y_even, ye[k, p], yo[k, p]) for k in (0, 1)]
        put(p, pl.ds(4, 4), *lo, scale * y_lo)
        put(p, pl.ds(72, 4), *hi, scale * y_hi)
        return out

    def own(i, carry):
        vown[i], wown[i] = plane(i + 4, b[i], c[i], OMEGA)
        return carry

    def edge(i, carry):
        lo = [jnp.where(x_even, xo[k, i], xe[k, i]) for k in (0, 1)]
        hi = [jnp.where(x_even, xe[k, i], xo[k, i]) for k in (0, 1)]
        plane(i, *lo, jnp.where(bi > 0, OMEGA, 0.0))
        plane(i + 20, *hi, jnp.where(bi < blocks - 1, OMEGA, 0.0))
        return carry

    lax.fori_loop(0, 16, own, 0)
    lax.fori_loop(0, 4, edge, 0)

    def smooth(p, carry):
        vv = v[p]
        qq = 0.4 * vv + w[p] * (v[p - 1] + v[p + 1] + plane_sum(vv))
        q[p] = qq
        return carry

    lax.fori_loop(1, 23, smooth, 0)

    def first(k, carry):
        p0[k] = q[k + 3] + OMEGA * v[k + 3]
        return carry

    lax.fori_loop(0, 18, first, 0)

    half = 0.5 * pair_matrix(True)

    def resid(p):
        return 0.04 * bx[p] + (q[p - 1] + q[p + 1] + plane_sum(q[p]))

    row1 = ai * 32 - 4 + iota(40, 0)
    keep1 = inside(row1, 32 * aggs) & (iota(40, 1) < 64)

    def coarse(k, carry):
        p = 2 + 2 * k
        rs[0] = resid(p) + resid(p + 1)
        rs[1] = cx[p] + cx[p + 1]
        both = jnp.concatenate([row_pairs(rs, 0, 40), row_pairs(rs, 1, 40)], axis=0)
        both = dot(both, half)
        bb, cc = both[:40], both[40:]
        ok = keep1 & inside(bi * 8 + k - 1, 8 * blocks)
        ww = jnp.where(ok, OMEGA / (6.0 + cc), 0.0)
        b1[k], c1[k] = bb, cc
        w1[k + 1] = ww
        e1[k + 1] = jnp.where(ok, ww * bb, 0.0)
        return carry

    lax.fori_loop(0, 10, coarse, 0)

    def resid1(k):
        near = e1[k] + e1[k + 2] + windowed_sum(e1[k + 1], row1)
        return 0.2 * b1[k] + near

    lane16 = iota(16, 1)

    def coarse2(k, carry):
        p = 1 + 2 * k
        r1[0] = resid1(p) + resid1(p + 1)
        r1[1] = c1[p] + c1[p + 1]
        pairs = [r1[i, pl.ds(4, 16, stride=2), :] + r1[i, pl.ds(5, 16, stride=2), :] for i in (0, 1)]
        both = dot(jnp.concatenate(pairs, axis=0), half)
        bb = jnp.where(lane16 < 32, both[:16], 0.0)
        cc = jnp.where(lane16 < 32, both[16:], 0.0)
        mix = bb + turn(cc, 32, 1)
        bc2[k] = mix
        for ref, lo_side in ((se, jnp.logical_not(y_even)), (so, y_even)):
            ref[k, 0:5] = jnp.where(lo_side, mix[0:5], mix[11:16])
            for j in (0, 1):
                n = 2 + 2 * k + j
                ref[k, 5 + j : 6 + j] = jnp.where(lo_side, e1[n, 5:6], e1[n, 34:35])
            ref[k, 7:8] = jnp.zeros((1, 128), F32)
        return carry

    lax.fori_loop(0, 4, coarse2, 0)


def join_kernel(at, bc2, ye, yo, e1, wide, se, so, sf, sg):
    bi, ai = at[0], at[1]
    x_even, y_even = (bi & 1) == 0, (ai & 1) == 0
    low_pair = (bi & 2) == 0
    for k in range(4):
        wide[k] = jnp.zeros((32, 128), F32)
        wide[k, 3:8] = jnp.where(y_even, yo[k, 0:5], ye[k, 0:5])
        wide[k, 8:24] = bc2[k]
        wide[k, 24:29] = jnp.where(y_even, ye[k, 0:5], yo[k, 0:5])
        se[k] = wide[k]
        so[k] = wide[k]
    up, down = e1[8, 4:36], e1[3, 4:36]
    se[4] = jnp.where(x_even, up, down)
    so[4] = jnp.where(x_even, down, up)
    sf[0] = jnp.where(low_pair, wide[3], wide[0])
    sg[0] = jnp.where(low_pair, wide[0], wide[3])


def up_kernel(
    blocks, aggs,
    at, p0, vown, wown, e1in, w1, wide, ye, yo, xe, xo, xf, xg,
    out,
    bc, e2, w2, b2, c2, rs, b3, e3, w3, pe2, m2, t2, e1, pe1, m1, mf,
):
    bi, ai = at[0], at[1]
    x_even, y_even = (bi & 1) == 0, (ai & 1) == 0
    low_pair = (bi & 2) == 0
    half, twice = 0.5 * pair_matrix(True), pair_matrix(False)

    bc[0] = jnp.where(low_pair, xg[0], xf[0])
    bc[13] = jnp.where(low_pair, xf[0], xg[0])
    for k in range(4):
        bc[1 + k] = jnp.where(x_even, xo[k], xe[k])
        bc[5 + k] = wide[k]
        bc[9 + k] = jnp.where(x_even, xe[k], xo[k])

    row2 = ai * 16 - 8 + iota(32, 0)
    lane2 = iota(32, 1) < 32
    keep2 = inside(row2, 16 * aggs) & lane2
    for k in range(14):
        mix = bc[k]
        bb = jnp.where(lane2, mix, 0.0)
        cc = jnp.where(lane2, turn(mix, -32, 1), 0.0)
        ww = jnp.where(keep2 & inside(bi * 4 + k - 5, 4 * blocks), OMEGA / (6.0 + cc), 0.0)
        b2[k], c2[k], w2[k], e2[k] = bb, cc, ww, ww * bb

    def resid2(k):
        return 0.2 * b2[k] + (e2[k - 1] + e2[k + 1] + windowed_sum(e2[k], row2))

    for j in range(6):
        k = 1 + 2 * j
        rs[j] = resid2(k) + resid2(k + 1)
        rs[6 + j] = c2[k] + c2[k + 1]
    both = dot(jnp.concatenate([row_pairs(rs, j, 16) for j in range(12)], axis=0), half)
    row3 = ai * 8 - 4 + iota(16, 0)
    keep3 = inside(row3, 8 * aggs) & (iota(16, 1) < 16)
    for j in range(6):
        bb, cc = both[16 * j : 16 * j + 16], both[96 + 16 * j : 112 + 16 * j]
        ww = jnp.where(keep3 & inside(bi * 2 + j - 2, 2 * blocks), OMEGA / (6.0 + cc), 0.0)
        w3[j], e3[j] = ww, ww * bb
    solved = []
    for j in range(1, 5):
        near = e3[j - 1] + e3[j + 1] + windowed_sum(e3[j], row3)
        solved.append(1.2 * e3[j] + w3[j] * near)
    wider = dot(jnp.concatenate(solved, axis=0), twice)
    for j in range(4):
        spread_rows(pe2, j, wider[16 * j : 16 * j + 16])
    for k in range(3, 11):
        m2[k] = e2[k] + pe2[(k - 3) // 2]
    solved = []
    for k in range(4, 10):
        near = m2[k - 1] + m2[k + 1] + windowed_sum(m2[k], row2)
        solved.append(0.2 * m2[k] + e2[k] + w2[k] * near)
    wider = dot(jnp.concatenate(solved, axis=0), twice)
    for k in range(6):
        t2[k] = wider[32 * k : 32 * k + 32]
        spread_rows(pe1, k, t2[k, 6:26])

    for k in range(1, 11):
        e1[k] = e1in[k]
    for k in (0, 11):
        e1[k] = jnp.zeros((40, 128), F32)
    e1[0, 4:36] = jnp.where(x_even, xo[4], xe[4])
    e1[11, 4:36] = jnp.where(x_even, xe[4], xo[4])
    for n in range(8):
        k, j = n // 2, n % 2
        mine, other = ye[k, 5 + j : 6 + j], yo[k, 5 + j : 6 + j]
        e1[n + 2, 2:3] = jnp.where(y_even, other, mine)
        e1[n + 2, 37:38] = jnp.where(y_even, mine, other)
    for k in range(12):
        m1[k] = e1[k] + pe1[k // 2]
    row1 = ai * 32 - 4 + iota(40, 0)

    def fine(k, carry):
        near = m1[k] + m1[k + 2] + windowed_sum(m1[k + 1], row1)
        v = 0.2 * m1[k + 1] + e1[k + 1] + w1[k + 1] * near
        spread_rows(rs80, k, dot(v, twice))
        return carry

    rs80 = mf.at[pl.ds(18, 10)]
    lax.fori_loop(0, 10, fine, 0)

    def merge(k, carry):
        mf[k] = p0[k] + mf[18 + (k + 1) // 2]
        return carry

    lax.fori_loop(0, 18, merge, 0)

    def last(k, carry):
        m = mf[k + 1]
        near = (plane_sum(m) + mf[k] + mf[k + 2])[8:72]
        out[k] = 0.2 * m[8:72] + vown[k] + wown[k] * near
        return carry

    lax.fori_loop(0, 16, last, 0)


def swaps(size, apart):
    inner, outer = [], []
    for i in range(size):
        inner.append((i, i ^ apart))
        outer.append((i, (i + apart) % size if i & apart else (i - apart) % size))
    return inner, outer


def shards(b, c):
    blocks, aggs = lax.axis_size("blk"), lax.axis_size("agg")
    bi, ai = lax.axis_index("blk"), lax.axis_index("agg")
    at = jnp.stack([bi, ai]).astype(jnp.int32)
    x_even, y_even = (bi & 1) == 0, (ai & 1) == 0
    near_in, near_out = swaps(blocks, 1)
    far_in, far_out = swaps(blocks, 2)
    side_in, side_out = swaps(aggs, 1)

    first = jnp.stack([b[:4], c[:4]])
    last = jnp.stack([b[12:], c[12:]])
    xe = lax.ppermute(jnp.where(x_even, last, first), "blk", near_in)
    xo = lax.ppermute(jnp.where(x_even, first, last), "blk", near_out)
    lo, hi = jnp.where(x_even, xo, xe), jnp.where(x_even, xe, xo)

    def rows(cut):
        own = jnp.stack([b[:, cut], c[:, cut]])
        return jnp.concatenate([lo[:, :, cut], own, hi[:, :, cut]], axis=1)

    first, last = rows(slice(0, 4)), rows(slice(60, 64))
    ye = lax.ppermute(jnp.where(y_even, last, first), "agg", side_in)
    yo = lax.ppermute(jnp.where(y_even, first, last), "agg", side_out)

    big, mid = (24, 80, 128), (12, 40, 128)
    p0, vown, wown, e1, w1, bc2, se, so = call(
        lambda *refs: down_kernel(blocks, aggs, *refs),
        (shape(18, 80, 128), shape(16, 64, 128), shape(16, 64, 128), shape(*mid), shape(*mid),
         shape(4, 16, 128), shape(4, 8, 128), shape(4, 8, 128)),
        [big] * 5 + [(2, 80, 128), mid, mid, (2, 40, 128)],
        at, b, c, xe, xo, ye, yo,
    )
    ye = lax.ppermute(se, "agg", side_in)
    yo = lax.ppermute(so, "agg", side_out)
    wide, se, so, sf, sg = call(
        join_kernel,
        (shape(4, 32, 128), shape(5, 32, 128), shape(5, 32, 128), shape(1, 32, 128), shape(1, 32, 128)),
        [],
        at, bc2, ye, yo, e1,
    )
    xe = lax.ppermute(se, "blk", near_in)
    xo = lax.ppermute(so, "blk", near_out)
    xf = lax.ppermute(sf, "blk", far_in)
    xg = lax.ppermute(sg, "blk", far_out)
    small = (14, 32, 128)
    (out,) = call(
        lambda *refs: up_kernel(blocks, aggs, *refs),
        (shape(16, 64, 128),),
        [small] * 5 + [(12, 32, 128), (6, 16, 128), (6, 16, 128), (6, 16, 128), (4, 32, 128),
                       small, (6, 32, 128), mid, (6, 40, 128), mid, (28, 80, 128)],
        at, p0, vown, wown, e1, w1, wide, ye, yo, xe, xo, xf, xg,
    )
    return out


def solution(mesh):
    placed = (P("blk", "agg", None), P("blk", "agg", None))
    return jax.shard_map(
        shards, mesh=mesh, in_specs=placed, out_specs=P("blk", "agg", None), check_vma=False
    )
```

```python
import jax
import jax.numpy as jnp
from jax import lax
from jax.experimental import pallas as pl
from jax.experimental.pallas import tpu as pltpu
from jax.sharding import PartitionSpec as P

OMEGA = 0.8
F32 = jnp.float32
WINDOW = 64
VM = pl.BlockSpec(memory_space=pltpu.VMEM)
SM = pl.BlockSpec(memory_space=pltpu.SMEM)


def shape(*dims):
    return jax.ShapeDtypeStruct(dims, F32)


def call(body, outs, scratch, *args):
    return pl.pallas_call(
        body,
        out_shape=outs,
        in_specs=[SM] + [VM] * (len(args) - 1),
        out_specs=tuple(VM for _ in outs),
        scratch_shapes=[pltpu.VMEM(s, F32) for s in scratch],
        compiler_params=pltpu.CompilerParams(vmem_limit_bytes=16 << 20),
    )(*args)


def iota(rows, axis):
    return lax.broadcasted_iota(jnp.int32, (rows, 128), axis)


def pick(kind):
    i, j = iota(128, 0), iota(128, 1)
    if kind == "pairs":
        at = (i >> 1) == j
    elif kind == "beside":
        at = (i >= 2 * j - 1) & (i <= 2 * j + 2)
    else:
        at = i == (j >> 1)
    return jnp.where(at, 1.0, 0.0).astype(jnp.bfloat16)


def halves(a):
    high = a.astype(jnp.bfloat16)
    return [high, (a - high.astype(F32)).astype(jnp.bfloat16)]


def dot(*terms):
    left = jnp.concatenate([h for a, _ in terms for h in halves(a)], axis=1)
    right = jnp.concatenate([m for _, m in terms for _ in (0, 1)], axis=0)
    return jnp.dot(left, right, preferred_element_type=F32)


def turn(v, by, axis):
    return pltpu.roll(v, by % v.shape[axis], axis)


def z_sum(v):
    lane = iota(v.shape[0], 1)
    below = jnp.where(lane == 0, 0.0, turn(v, 1, 1))
    return below + jnp.where(lane == 127, 0.0, turn(v, -1, 1))


def beside(ref, k, v, start, rows):
    return ref[k, pl.ds(start - 1, rows)] + ref[k, pl.ds(start + 1, rows)] + z_sum(v)


def windowed(ref, k, v, rows, at):
    below = jnp.where(at == 0, 0.0, ref[k, pl.ds(7, rows)])
    above = jnp.where(at == WINDOW - 1, 0.0, ref[k, pl.ds(9, rows)])
    return below + above + turn(v, 1, 1) + turn(v, -1, 1)


def inside(at, size):
    return (at >= 0) & (at < size)


def every_other(ref, k, start, rows):
    return ref[k, pl.ds(start, rows, stride=2), :]


def row_pairs(ref, k, start, rows):
    return every_other(ref, k, start, rows) + every_other(ref, k, start + 1, rows)


def gather(both, rest, k, at_both, at_rest, rows, at=None):
    below, above = every_other(both, k, at_both - 1, rows), every_other(both, k, at_both + 2, rows)
    if at is not None:
        below = jnp.where(at == 0, 0.0, below)
        above = jnp.where(at == WINDOW // 2 - 1, 0.0, above)
    own = row_pairs(both, k, at_both, rows)
    return row_pairs(rest, k, at_rest, rows) + own + below + above, own


def down_kernel(
    blocks, aggs,
    at, b, c, xe, xo, ye, yo,
    p0, vown, wown, e1, w1, bc2, se, so,
    v, w, q, bx, cx, own1, rest1, b1, c1, own2, rest2,
):
    bi, ai = at[0], at[1]
    x_even, y_even = (bi & 1) == 0, (ai & 1) == 0
    y_lo = jnp.where(ai > 0, 1.0, 0.0)
    y_hi = jnp.where(ai < aggs - 1, 1.0, 0.0)

    def put(p, rows, bb, cc, scale):
        ww = scale / (6.0 + cc)
        vv = ww * bb
        w[p, rows], v[p, rows], bx[p, rows], cx[p, rows] = ww, vv, bb, cc
        return vv, ww

    def plane(p, bb, cc, scale):
        out = put(p, pl.ds(16, 64), bb, cc, scale)
        lo = [jnp.where(y_even, yo[k, p], ye[k, p]) for k in (0, 1)]
        hi = [jnp.where(y_even, ye[k, p], yo[k, p]) for k in (0, 1)]
        put(p, pl.ds(12, 4), *lo, scale * y_lo)
        put(p, pl.ds(80, 4), *hi, scale * y_hi)
        return out

    def own(k, carry):
        for i in (2 * k, 2 * k + 1):
            vown[i], wown[i] = plane(i + 4, b[i], c[i], OMEGA)
        return carry

    def edge(i, carry):
        lo = [jnp.where(x_even, xo[k, i], xe[k, i]) for k in (0, 1)]
        hi = [jnp.where(x_even, xe[k, i], xo[k, i]) for k in (0, 1)]
        plane(i, *lo, jnp.where(bi > 0, OMEGA, 0.0))
        plane(i + 20, *hi, jnp.where(bi < blocks - 1, OMEGA, 0.0))
        return carry

    lax.fori_loop(0, 8, own, 0)
    lax.fori_loop(0, 4, edge, 0)
    rows = pl.ds(8, 80)

    def smooth(k, carry):
        for p in (1 + 2 * k, 2 + 2 * k):
            vv = v[p, rows]
            near = v[p - 1, rows] + v[p + 1, rows] + beside(v, p, vv, 8, 80)
            qq = 0.4 * vv + w[p, rows] * near
            q[p, rows] = qq
            p0[p] = qq + OMEGA * vv
        return carry

    lax.fori_loop(0, 11, smooth, 0)

    pairs, sides = pick("pairs"), pick("beside")
    row1 = ai * 32 - 4 + iota(40, 0)
    keep1 = inside(row1, 32 * aggs) & (iota(40, 1) < 64)

    def coarse(k, carry):
        p = 2 + 2 * k
        both = q[p, rows] + q[p + 1, rows]
        own1[k, pl.ds(8, 80)] = both
        rest1[k] = 0.04 * (bx[p, rows] + bx[p + 1, rows]) + (both + (q[p - 1, rows] + q[p + 2, rows]))
        cx[k, rows] = cx[p, rows] + cx[p + 1, rows]
        return carry

    lax.fori_loop(0, 10, coarse, 0)

    def coarse_dots(k, carry):
        n = 2 * k
        ends, mids, sums = [], [], []
        for i in (n, n + 1):
            end, mid = gather(own1, rest1, i, 8, 0, 40)
            ends.append(end)
            mids.append(mid)
            sums.append(row_pairs(cx, i, 8, 40))
        bb2 = dot((jnp.concatenate(ends, axis=0), pairs), (jnp.concatenate(mids, axis=0), sides))
        cc2 = dot((jnp.concatenate(sums, axis=0), pairs))
        for i in (0, 1):
            bb, cc = 0.5 * bb2[40 * i : 40 * i + 40], 0.5 * cc2[40 * i : 40 * i + 40]
            ok = keep1 & inside(bi * 8 + n + i - 1, 8 * blocks)
            ww = jnp.where(ok, OMEGA / (6.0 + cc), 0.0)
            b1[n + i], c1[n + i] = bb, cc
            w1[n + i + 1] = ww
            e1[n + i + 1] = jnp.where(ok, ww * bb, 0.0)
        return carry

    lax.fori_loop(0, 5, coarse_dots, 0)

    at2 = (ai * 16 + iota(16, 0)) & (WINDOW // 2 - 1)
    lane16 = iota(16, 1)
    ends, mids, sums = [], [], []
    for k in range(4):
        p = 1 + 2 * k
        both = e1[p + 1] + e1[p + 2]
        own2[k] = both
        rest2[k] = 0.2 * (b1[p] + b1[p + 1]) + (both + (e1[p] + e1[p + 3]))
        end, mid = gather(own2, rest2, k, 4, 4, 16, at2)
        ends.append(end)
        mids.append(mid)
        sums.append(row_pairs(c1, p, 4, 16) + row_pairs(c1, p + 1, 4, 16))
    bb2 = dot((jnp.concatenate(ends, axis=0), pairs), (jnp.concatenate(mids, axis=0), sides))
    cc2 = dot((jnp.concatenate(sums, axis=0), pairs))
    for k in range(4):
        bb = jnp.where(lane16 < 32, 0.5 * bb2[16 * k : 16 * k + 16], 0.0)
        cc = jnp.where(lane16 < 32, 0.5 * cc2[16 * k : 16 * k + 16], 0.0)
        mix = bb + turn(cc, 32, 1)
        bc2[k] = mix
        for ref, lo_side in ((se, jnp.logical_not(y_even)), (so, y_even)):
            ref[k, 0:5] = jnp.where(lo_side, mix[0:5], mix[11:16])
            for j in (0, 1):
                n = 2 + 2 * k + j
                ref[k, 5 + j : 6 + j] = jnp.where(lo_side, e1[n, 5:6], e1[n, 34:35])
            ref[k, 7:8] = jnp.zeros((1, 128), F32)


def join_kernel(at, bc2, ye, yo, e1, wide, se, so, sf, sg):
    bi, ai = at[0], at[1]
    x_even, y_even = (bi & 1) == 0, (ai & 1) == 0
    low_pair = (bi & 2) == 0
    for k in range(4):
        wide[k] = jnp.zeros((32, 128), F32)
        wide[k, 3:8] = jnp.where(y_even, yo[k, 0:5], ye[k, 0:5])
        wide[k, 8:24] = bc2[k]
        wide[k, 24:29] = jnp.where(y_even, ye[k, 0:5], yo[k, 0:5])
        se[k] = wide[k]
        so[k] = wide[k]
    up, down = e1[8, 4:36], e1[3, 4:36]
    se[4] = jnp.where(x_even, up, down)
    so[4] = jnp.where(x_even, down, up)
    sf[0] = jnp.where(low_pair, wide[3], wide[0])
    sg[0] = jnp.where(low_pair, wide[0], wide[3])


def up_kernel(
    blocks, aggs,
    at, p0, vown, wown, e1in, w1, wide, ye, yo, xe, xo, xf, xg,
    out,
    bc, e2, w2, b2, c2, own2, rest2, m2, t2, e1, m1, mf,
):
    bi, ai = at[0], at[1]
    x_even, y_even = (bi & 1) == 0, (ai & 1) == 0
    low_pair = (bi & 2) == 0
    pairs, sides, copies = pick("pairs"), pick("beside"), pick("copies")

    bc[0] = jnp.where(low_pair, xg[0], xf[0])
    bc[13] = jnp.where(low_pair, xf[0], xg[0])
    for k in range(4):
        bc[1 + k] = jnp.where(x_even, xo[k], xe[k])
        bc[5 + k] = wide[k]
        bc[9 + k] = jnp.where(x_even, xe[k], xo[k])

    row2 = ai * 16 - 8 + iota(32, 0)
    lane2 = iota(32, 1) < 32
    keep2 = inside(row2, 16 * aggs) & lane2
    for k in range(14):
        mix = bc[k]
        bb = jnp.where(lane2, mix, 0.0)
        cc = jnp.where(lane2, turn(mix, -32, 1), 0.0)
        ww = jnp.where(keep2 & inside(bi * 4 + k - 5, 4 * blocks), OMEGA / (6.0 + cc), 0.0)
        b2[k], c2[k], w2[k], e2[k] = bb, cc, ww, ww * bb

    row3 = ai * 8 - 4 + iota(16, 0)
    at3 = row3 & (WINDOW // 2 - 1)
    ends, mids, sums = [], [], []
    for j in range(6):
        k = 1 + 2 * j
        both = e2[k] + e2[k + 1]
        own2[j, 8:40] = both
        rest2[j] = 0.2 * (b2[k] + b2[k + 1]) + (both + (e2[k - 1] + e2[k + 2]))
        end, mid = gather(own2, rest2, j, 8, 0, 16, at3)
        ends.append(end)
        mids.append(mid)
        sums.append(row_pairs(c2, k, 0, 16) + row_pairs(c2, k + 1, 0, 16))
    bb3 = dot((jnp.concatenate(ends, axis=0), pairs), (jnp.concatenate(mids, axis=0), sides))
    cc3 = dot((jnp.concatenate(sums, axis=0), pairs))
    keep3 = inside(row3, 8 * aggs) & (iota(16, 1) < 16)
    e3, w3 = [], []
    for j in range(6):
        bb, cc = 0.5 * bb3[16 * j : 16 * j + 16], 0.5 * cc3[16 * j : 16 * j + 16]
        ok = keep3 & inside(bi * 2 + j - 2, 2 * blocks)
        ww = jnp.where(ok, OMEGA / (6.0 + cc), 0.0)
        w3.append(ww)
        e3.append(jnp.where(ok, ww * bb, 0.0))
    solved = []
    for j in range(1, 5):
        v = e3[j]
        near = e3[j - 1] + e3[j + 1] + turn(v, 1, 0) + turn(v, -1, 0) + turn(v, 1, 1) + turn(v, -1, 1)
        solved.append(1.2 * v + w3[j] * near)
    wider = dot((jnp.concatenate(solved, axis=0), copies))
    for k in range(3, 11):
        j = (k - 3) // 2
        for r in (0, 1):
            m2[k, pl.ds(8 + r, 16, stride=2), :] = every_other(e2, k, r, 16) + wider[16 * j : 16 * j + 16]
    at2 = row2 & (WINDOW - 1)
    rows = pl.ds(8, 32)
    solved = []
    for k in range(4, 10):
        v = m2[k, rows]
        near = m2[k - 1, rows] + m2[k + 1, rows] + windowed(m2, k, v, 32, at2)
        solved.append(0.2 * v + e2[k] + w2[k] * near)
    wider = dot((jnp.concatenate(solved, axis=0), copies))
    for k in range(6):
        t2[k] = wider[32 * k : 32 * k + 32]

    for k in range(1, 11):
        e1[k] = e1in[k]
    for k in (0, 11):
        e1[k] = jnp.zeros((40, 128), F32)
    e1[0, 4:36] = jnp.where(x_even, xo[4], xe[4])
    e1[11, 4:36] = jnp.where(x_even, xe[4], xo[4])
    for n in range(8):
        k, j = n // 2, n % 2
        mine, other = ye[k, 5 + j : 6 + j], yo[k, 5 + j : 6 + j]
        e1[n + 2, 2:3] = jnp.where(y_even, other, mine)
        e1[n + 2, 37:38] = jnp.where(y_even, mine, other)
    for k in range(12):
        for r in (0, 1):
            m1[k, pl.ds(8 + r, 20, stride=2), :] = every_other(e1, k, r, 20) + t2[k // 2, 6:26]
    at1 = (ai * 32 - 4 + iota(40, 0)) & (WINDOW - 1)

    def fine(n, carry):
        rows = pl.ds(8, 40)
        solved = []
        for k in (2 * n, 2 * n + 1):
            v = m1[k + 1, rows]
            near = m1[k, rows] + m1[k + 2, rows] + windowed(m1, k + 1, v, 40, at1)
            solved.append(0.2 * v + e1[k + 1] + w1[k + 1] * near)
        wider = dot((jnp.concatenate(solved, axis=0), copies))
        for i in (0, 1):
            for j in (0, 1):
                k = 4 * n + 2 * i + j
                for r in (0, 1):
                    old = p0[k + 2, pl.ds(r, 40, stride=2), :]
                    mf[k, pl.ds(8 + r, 40, stride=2), :] = old + wider[40 * i : 40 * i + 40]
        return carry

    lax.fori_loop(0, 5, fine, 0)

    def last(n, carry):
        rows = pl.ds(16, 64)
        for k in (2 * n, 2 * n + 1):
            m = mf[k + 2, rows]
            near = mf[k + 1, rows] + mf[k + 3, rows] + beside(mf, k + 2, m, 16, 64)
            out[k] = 0.2 * m + vown[k] + wown[k] * near
        return carry

    lax.fori_loop(0, 8, last, 0)


def swaps(size, apart):
    inner, outer = [], []
    for i in range(size):
        inner.append((i, i ^ apart))
        outer.append((i, (i + apart) % size if i & apart else (i - apart) % size))
    return inner, outer


def shards(b, c):
    blocks, aggs = lax.axis_size("blk"), lax.axis_size("agg")
    bi, ai = lax.axis_index("blk"), lax.axis_index("agg")
    at = jnp.stack([bi, ai]).astype(jnp.int32)
    x_even, y_even = (bi & 1) == 0, (ai & 1) == 0
    near_in, near_out = swaps(blocks, 1)
    far_in, far_out = swaps(blocks, 2)
    side_in, side_out = swaps(aggs, 1)

    first = jnp.stack([b[:4], c[:4]])
    last = jnp.stack([b[12:], c[12:]])
    xe = lax.ppermute(jnp.where(x_even, last, first), "blk", near_in)
    xo = lax.ppermute(jnp.where(x_even, first, last), "blk", near_out)
    lo, hi = jnp.where(x_even, xo, xe), jnp.where(x_even, xe, xo)

    def rows(cut):
        own = jnp.stack([b[:, cut], c[:, cut]])
        return jnp.concatenate([lo[:, :, cut], own, hi[:, :, cut]], axis=1)

    first, last = rows(slice(0, 4)), rows(slice(60, 64))
    ye = lax.ppermute(jnp.where(y_even, last, first), "agg", side_in)
    yo = lax.ppermute(jnp.where(y_even, first, last), "agg", side_out)

    big, mid = (24, 96, 128), (12, 40, 128)
    p0, vown, wown, e1, w1, bc2, se, so = call(
        lambda *refs: down_kernel(blocks, aggs, *refs),
        (shape(24, 80, 128), shape(16, 64, 128), shape(16, 64, 128), shape(*mid), shape(*mid),
         shape(4, 16, 128), shape(4, 8, 128), shape(4, 8, 128)),
        [big] * 5 + [(10, 96, 128), (10, 80, 128), mid, mid, (4, 40, 128), (4, 40, 128)],
        at, b, c, xe, xo, ye, yo,
    )
    ye = lax.ppermute(se, "agg", side_in)
    yo = lax.ppermute(so, "agg", side_out)
    wide, se, so, sf, sg = call(
        join_kernel,
        (shape(4, 32, 128), shape(5, 32, 128), shape(5, 32, 128), shape(1, 32, 128), shape(1, 32, 128)),
        [],
        at, bc2, ye, yo, e1,
    )
    xe = lax.ppermute(se, "blk", near_in)
    xo = lax.ppermute(so, "blk", near_out)
    xf = lax.ppermute(sf, "blk", far_in)
    xg = lax.ppermute(sg, "blk", far_out)
    small = (14, 32, 128)
    (out,) = call(
        lambda *refs: up_kernel(blocks, aggs, *refs),
        (shape(16, 64, 128),),
        [small] * 5 + [(6, 48, 128), (6, 32, 128), (14, 48, 128), (6, 32, 128), mid, (12, 56, 128), (20, 96, 128)],
        at, p0, vown, wown, e1, w1, wide, ye, yo, xe, xo, xf, xg,
    )
    return out


def solution(mesh):
    placed = (P("blk", "agg", None), P("blk", "agg", None))
    return jax.shard_map(
        shards, mesh=mesh, in_specs=placed, out_specs=P("blk", "agg", None), check_vma=False
    )
```

```python
import jax
import jax.numpy as jnp
from jax import lax
from jax.experimental import pallas as pl
from jax.experimental.pallas import tpu as pltpu
from jax.sharding import PartitionSpec as P

OMEGA = 0.8
F32 = jnp.float32
WINDOW = 64
VM = pl.BlockSpec(memory_space=pltpu.VMEM)
SM = pl.BlockSpec(memory_space=pltpu.SMEM)


def shape(*dims):
    return jax.ShapeDtypeStruct(dims, F32)


def call(body, outs, scratch, *args):
    return pl.pallas_call(
        body,
        out_shape=outs,
        in_specs=[SM] + [VM] * (len(args) - 1),
        out_specs=tuple(VM for _ in outs),
        scratch_shapes=[pltpu.VMEM(s, F32) for s in scratch],
        compiler_params=pltpu.CompilerParams(vmem_limit_bytes=16 << 20),
    )(*args)


def iota(rows, axis):
    return lax.broadcasted_iota(jnp.int32, (rows, 128), axis)


def pick(kind):
    i, j = iota(128, 0), iota(128, 1)
    if kind == "pairs":
        at = (i >> 1) == j
    elif kind == "beside":
        at = (i >= 2 * j - 1) & (i <= 2 * j + 2) & (j < 64)
    else:
        at = i == (j >> 1)
    return jnp.where(at, 1.0, 0.0).astype(jnp.bfloat16)


def halves(a):
    high = a.astype(jnp.bfloat16)
    return [high, (a - high.astype(F32)).astype(jnp.bfloat16)]


def dot(*terms):
    left = jnp.concatenate([h for a, _ in terms for h in halves(a)], axis=1)
    right = jnp.concatenate([m for _, m in terms for _ in (0, 1)], axis=0)
    return jnp.dot(left, right, preferred_element_type=F32)


def turn(v, by, axis):
    return pltpu.roll(v, by % v.shape[axis], axis)


def z_sum(v):
    lane = iota(v.shape[0], 1)
    below = jnp.where(lane == 0, 0.0, turn(v, 1, 1))
    return below + jnp.where(lane == 127, 0.0, turn(v, -1, 1))


def beside(ref, k, v, start, rows):
    return ref[k, pl.ds(start - 1, rows)] + ref[k, pl.ds(start + 1, rows)] + z_sum(v)


def windowed(ref, k, v, rows, at):
    below = jnp.where(at == 0, 0.0, ref[k, pl.ds(7, rows)])
    above = jnp.where(at == WINDOW - 1, 0.0, ref[k, pl.ds(9, rows)])
    return below + above + turn(v, 1, 1) + turn(v, -1, 1)


def inside(at, size):
    return (at >= 0) & (at < size)


def every_other(ref, k, start, rows):
    return ref[k, pl.ds(start, rows, stride=2), :]


def row_pairs(ref, k, start, rows):
    return every_other(ref, k, start, rows) + every_other(ref, k, start + 1, rows)


def gather(both, rest, k, at_both, at_rest, rows, at=None):
    below, above = every_other(both, k, at_both - 1, rows), every_other(both, k, at_both + 2, rows)
    if at is not None:
        below = jnp.where(at == 0, 0.0, below)
        above = jnp.where(at == WINDOW // 2 - 1, 0.0, above)
    own = row_pairs(both, k, at_both, rows)
    return row_pairs(rest, k, at_rest, rows) + own + below + above, own


def head_kernel(
    aggs,
    at, b, c, ye, yo,
    p0, vown, wown, b1, c1, edge, se, so,
    v, w, q, bx, cx, own1, rest1,
):
    bi, ai = at[0], at[1]
    x_even, y_even = (bi & 1) == 0, (ai & 1) == 0
    y_lo = jnp.where(ai > 0, OMEGA, 0.0)
    y_hi = jnp.where(ai < aggs - 1, OMEGA, 0.0)
    rows = pl.ds(8, 80)

    def put(p, rows, bb, cc, scale):
        ww = scale / (6.0 + cc)
        vv = ww * bb
        w[p, rows], v[p, rows], bx[p, rows], cx[p, rows] = ww, vv, bb, cc
        return vv, ww

    def planes(n, carry):
        for p in (2 * n, 2 * n + 1):
            vown[p], wown[p] = put(p, pl.ds(16, 64), b[p], c[p], OMEGA)
            lo = [jnp.where(y_even, yo[k, p], ye[k, p]) for k in (0, 1)]
            hi = [jnp.where(y_even, ye[k, p], yo[k, p]) for k in (0, 1)]
            put(p, pl.ds(12, 4), *lo, y_lo)
            put(p, pl.ds(80, 4), *hi, y_hi)
        return carry

    lax.fori_loop(0, 8, planes, 0)

    def smooth(n, carry):
        for p in (1 + 2 * n, 2 + 2 * n):
            vv = v[p, rows]
            near = v[p - 1, rows] + v[p + 1, rows] + beside(v, p, vv, 8, 80)
            qq = 0.4 * vv + w[p, rows] * near
            q[p, rows] = qq
            p0[p] = qq + OMEGA * vv
        return carry

    lax.fori_loop(0, 7, smooth, 0)
    for n, p, inner in ((0, 0, 1), (3, 15, 14)):
        vv, ww = v[p, rows], w[p, rows]
        edge[n] = 0.4 * vv + ww * (v[inner, rows] + beside(v, p, vv, 8, 80))
        edge[n + 1] = ww
        edge[n + 2] = vv

    def sums(k, p):
        cx[k, rows] = cx[p, rows] + cx[p + 1, rows]
        return 0.04 * (bx[p, rows] + bx[p + 1, rows])

    def coarse(k, carry):
        p = 2 * k
        both = q[p, rows] + q[p + 1, rows]
        own1[k, rows] = both
        rest1[k] = sums(k, p) + (both + (q[p - 1, rows] + q[p + 2, rows]))
        return carry

    own1[0, rows] = q[1, rows]
    rest1[0] = sums(0, 0) + (q[1, rows] + q[2, rows])
    lax.fori_loop(1, 7, coarse, 0)
    own1[7, rows] = q[14, rows]
    rest1[7] = sums(7, 14) + (q[14, rows] + q[13, rows])

    pairs, sides = pick("pairs"), pick("beside")

    def products(n, carry):
        ends, mids, csums = [], [], []
        for k in (2 * n, 2 * n + 1):
            end, mid = gather(own1, rest1, k, 8, 0, 40)
            ends.append(end)
            mids.append(mid)
            csums.append(row_pairs(cx, k, 8, 40))
        bb = dot((jnp.concatenate(ends, axis=0), pairs), (jnp.concatenate(mids, axis=0), sides))
        cc = dot((jnp.concatenate(csums, axis=0), pairs))
        for i in (0, 1):
            b1[2 * n + i] = 0.5 * bb[40 * i : 40 * i + 40]
            c1[2 * n + i] = 0.5 * cc[40 * i : 40 * i + 40]
        return carry

    lax.fori_loop(0, 4, products, 0)
    for ref, up in ((se, x_even), (so, jnp.logical_not(x_even))):
        for i in range(3):
            ref[2 * i] = jnp.where(up, edge[3 + i, 0:40], edge[i, 0:40])
            ref[2 * i + 1] = jnp.where(up, edge[3 + i, 40:80], edge[i, 40:80])
            ref[6 + i] = jnp.where(up, b1[5 + i], b1[i]) + turn(jnp.where(up, c1[5 + i], c1[i]), 64, 1)


def mid_kernel(
    blocks, aggs,
    at, b1in, c1in, edge, xe, xo,
    pe, e1out, w1out, bc2, se, so,
    s4, r4, b1, c1, e1, own2, rest2,
):
    bi, ai = at[0], at[1]
    x_even, y_even = (bi & 1) == 0, (ai & 1) == 0
    pairs, sides = pick("pairs"), pick("beside")
    has_lo, has_hi = bi > 0, bi < blocks - 1
    lane1 = iota(40, 1) < 64

    def fetch(lo, n):
        first = x_even if lo else jnp.logical_not(x_even)
        return jnp.where(first, xo[n], xe[n])

    for i, (lo, there) in enumerate(((True, has_lo), (False, has_hi))):
        gb, wb, vb = [
            jnp.where(there, jnp.concatenate([fetch(lo, 2 * n), fetch(lo, 2 * n + 1)], axis=0), 0.0)
            for n in range(3)
        ]
        g, w, v = [edge[3 * i + n] for n in range(3)]
        mine, other = g + w * vb, gb + wb * v
        near, far = (1, 0) if lo else (2, 3)
        pe[near] = mine + OMEGA * v
        pe[far] = other + OMEGA * vb
        s4[2 * i, pl.ds(8, 80)] = mine
        s4[2 * i + 1, pl.ds(8, 80)] = other
        r4[2 * i] = mine + other
        r4[2 * i + 1] = mine + other
        for n in range(3):
            mix = fetch(lo, 6 + n)
            k = n if lo else 11 + n
            b1[k] = jnp.where(lane1, mix, 0.0)
            c1[k] = jnp.where(lane1, turn(mix, -64, 1), 0.0)
    for k in range(8):
        b1[k + 3] = b1in[k]
        c1[k + 3] = c1in[k]
    ends, mids = [], []
    for i in range(4):
        end, mid = gather(s4, r4, i, 8, 0, 40)
        ends.append(end)
        mids.append(mid)
    more = dot((jnp.concatenate(ends, axis=0), pairs), (jnp.concatenate(mids, axis=0), sides))
    for i, k in enumerate((3, 2, 10, 11)):
        b1[k] = b1[k] + 0.5 * more[40 * i : 40 * i + 40]

    row1 = ai * 32 - 4 + iota(40, 0)
    keep1 = inside(row1, 32 * aggs) & lane1
    for k in range(14):
        ok = keep1 & inside(bi * 8 + k - 3, 8 * blocks)
        ww = jnp.where(ok, OMEGA / (6.0 + c1[k]), 0.0)
        ee = jnp.where(ok, ww * b1[k], 0.0)
        e1[k] = ee
        if 0 < k < 13:
            w1out[k - 1], e1out[k - 1] = ww, ee

    at2 = (ai * 16 + iota(16, 0)) & (WINDOW // 2 - 1)
    lane16 = iota(16, 1)
    ends, mids, csums = [], [], []
    for k in range(6):
        p = 1 + 2 * k
        both = e1[p] + e1[p + 1]
        own2[k] = both
        rest2[k] = 0.2 * (b1[p] + b1[p + 1]) + (both + (e1[p - 1] + e1[p + 2]))
        end, mid = gather(own2, rest2, k, 4, 4, 16, at2)
        ends.append(end)
        mids.append(mid)
        csums.append(row_pairs(c1, p, 4, 16) + row_pairs(c1, p + 1, 4, 16))
    bb2 = dot((jnp.concatenate(ends, axis=0), pairs), (jnp.concatenate(mids, axis=0), sides))
    cc2 = dot((jnp.concatenate(csums, axis=0), pairs))
    for k in range(6):
        bb = jnp.where(lane16 < 32, 0.5 * bb2[16 * k : 16 * k + 16], 0.0)
        cc = jnp.where(lane16 < 32, 0.5 * cc2[16 * k : 16 * k + 16], 0.0)
        mix = bb + turn(cc, 32, 1)
        bc2[k] = mix
        for ref, lo_side in ((se, jnp.logical_not(y_even)), (so, y_even)):
            ref[k, 0:5] = jnp.where(lo_side, mix[0:5], mix[11:16])
            for j in (0, 1):
                n = 3 + (2 * k + j) % 8
                ref[k, 5 + j : 6 + j] = jnp.where(lo_side, e1[n, 5:6], e1[n, 34:35])
            ref[k, 7:8] = jnp.zeros((1, 128), F32)


def join_kernel(at, bc2, ye, yo, wide, se, so):
    bi, ai = at[0], at[1]
    x_even, y_even = (bi & 1) == 0, (ai & 1) == 0
    for k in range(6):
        wide[k] = jnp.zeros((32, 128), F32)
        wide[k, 3:8] = jnp.where(y_even, yo[k, 0:5], ye[k, 0:5])
        wide[k, 8:24] = bc2[k]
        wide[k, 24:29] = jnp.where(y_even, ye[k, 0:5], yo[k, 0:5])
    for k in range(5):
        se[k] = jnp.where(x_even, wide[k], wide[k + 1])
        so[k] = jnp.where(x_even, wide[k + 1], wide[k])


def up_kernel(
    blocks, aggs,
    at, p0, pe, vown, wown, e1in, w1, wide, ye, yo, xe, xo,
    out,
    bc, e2, w2, b2, c2, own2, rest2, m2, t2, e1, m1, mf,
):
    bi, ai = at[0], at[1]
    x_even, y_even = (bi & 1) == 0, (ai & 1) == 0
    pairs, sides, copies = pick("pairs"), pick("beside"), pick("copies")

    for k in range(5):
        bc[k] = jnp.where(x_even, xo[k], xe[k])
        bc[9 + k] = jnp.where(x_even, xe[k], xo[k])
    for k in range(4):
        bc[5 + k] = wide[1 + k]

    row2 = ai * 16 - 8 + iota(32, 0)
    lane2 = iota(32, 1) < 32
    keep2 = inside(row2, 16 * aggs) & lane2
    for k in range(14):
        mix = bc[k]
        bb = jnp.where(lane2, mix, 0.0)
        cc = jnp.where(lane2, turn(mix, -32, 1), 0.0)
        ww = jnp.where(keep2 & inside(bi * 4 + k - 5, 4 * blocks), OMEGA / (6.0 + cc), 0.0)
        b2[k], c2[k], w2[k], e2[k] = bb, cc, ww, ww * bb

    row3 = ai * 8 - 4 + iota(16, 0)
    at3 = row3 & (WINDOW // 2 - 1)
    ends, mids, sums = [], [], []
    for j in range(6):
        k = 1 + 2 * j
        both = e2[k] + e2[k + 1]
        own2[j, 8:40] = both
        rest2[j] = 0.2 * (b2[k] + b2[k + 1]) + (both + (e2[k - 1] + e2[k + 2]))
        end, mid = gather(own2, rest2, j, 8, 0, 16, at3)
        ends.append(end)
        mids.append(mid)
        sums.append(row_pairs(c2, k, 0, 16) + row_pairs(c2, k + 1, 0, 16))
    bb3 = dot((jnp.concatenate(ends, axis=0), pairs), (jnp.concatenate(mids, axis=0), sides))
    cc3 = dot((jnp.concatenate(sums, axis=0), pairs))
    keep3 = inside(row3, 8 * aggs) & (iota(16, 1) < 16)
    e3, w3 = [], []
    for j in range(6):
        bb, cc = 0.5 * bb3[16 * j : 16 * j + 16], 0.5 * cc3[16 * j : 16 * j + 16]
        ok = keep3 & inside(bi * 2 + j - 2, 2 * blocks)
        ww = jnp.where(ok, OMEGA / (6.0 + cc), 0.0)
        w3.append(ww)
        e3.append(jnp.where(ok, ww * bb, 0.0))
    solved = []
    for j in range(1, 5):
        v = e3[j]
        near = e3[j - 1] + e3[j + 1] + turn(v, 1, 0) + turn(v, -1, 0) + turn(v, 1, 1) + turn(v, -1, 1)
        solved.append(1.2 * v + w3[j] * near)
    wider = dot((jnp.concatenate(solved, axis=0), copies))
    for k in range(3, 11):
        j = (k - 3) // 2
        for r in (0, 1):
            m2[k, pl.ds(8 + r, 16, stride=2), :] = every_other(e2, k, r, 16) + wider[16 * j : 16 * j + 16]
    at2 = row2 & (WINDOW - 1)
    rows = pl.ds(8, 32)
    solved = []
    for k in range(4, 10):
        v = m2[k, rows]
        near = m2[k - 1, rows] + m2[k + 1, rows] + windowed(m2, k, v, 32, at2)
        solved.append(0.2 * v + e2[k] + w2[k] * near)
    wider = dot((jnp.concatenate(solved, axis=0), copies))
    for k in range(6):
        t2[k] = wider[32 * k : 32 * k + 32]

    for k in range(12):
        e1[k] = e1in[k]
    for n in range(8):
        k, j = n // 2, n % 2
        mine, other = ye[k, 5 + j : 6 + j], yo[k, 5 + j : 6 + j]
        e1[n + 2, 2:3] = jnp.where(y_even, other, mine)
        e1[n + 2, 37:38] = jnp.where(y_even, mine, other)
    for k in range(12):
        for r in (0, 1):
            m1[k, pl.ds(8 + r, 20, stride=2), :] = every_other(e1, k, r, 20) + t2[k // 2, 6:26]
    at1 = (ai * 32 - 4 + iota(40, 0)) & (WINDOW - 1)

    def fine(n, first):
        rows = pl.ds(8, 40)
        solved = []
        for k in (2 * n, 2 * n + 1):
            v = m1[k + 1, rows]
            near = m1[k, rows] + m1[k + 2, rows] + windowed(m1, k + 1, v, 40, at1)
            solved.append(0.2 * v + e1[k + 1] + w1[k + 1] * near)
        wider = dot((jnp.concatenate(solved, axis=0), copies))
        for k, (ref, p) in enumerate(first(4 * n)):
            for r in (0, 1):
                if ref is not None:
                    old = ref[p, pl.ds(r, 40, stride=2), :]
                    i = 40 * (k // 2)
                    mf[4 * n + k, pl.ds(8 + r, 40, stride=2), :] = old + wider[i : i + 40]

    def inner(n, carry):
        fine(n, lambda k: [(p0, k - 2), (p0, k - 1), (p0, k), (p0, k + 1)])
        return carry

    fine(0, lambda k: [(None, 0), (pe, 0), (pe, 1), (p0, 1)])
    lax.fori_loop(1, 4, inner, 0)
    fine(4, lambda k: [(p0, 14), (pe, 2), (pe, 3), (None, 0)])

    def last(n, carry):
        rows = pl.ds(16, 64)
        for k in (2 * n, 2 * n + 1):
            m = mf[k + 2, rows]
            near = mf[k + 1, rows] + mf[k + 3, rows] + beside(mf, k + 2, m, 16, 64)
            out[k] = 0.2 * m + vown[k] + wown[k] * near
        return carry

    lax.fori_loop(0, 8, last, 0)


def swaps(size, apart):
    inner, outer = [], []
    for i in range(size):
        inner.append((i, i ^ apart))
        outer.append((i, (i + apart) % size if i & apart else (i - apart) % size))
    return inner, outer


def shards(b, c):
    blocks, aggs = lax.axis_size("blk"), lax.axis_size("agg")
    bi, ai = lax.axis_index("blk"), lax.axis_index("agg")
    at = jnp.stack([bi, ai]).astype(jnp.int32)
    y_even = (ai & 1) == 0
    near_in, near_out = swaps(blocks, 1)
    side_in, side_out = swaps(aggs, 1)

    first = jnp.stack([b[:, :4], c[:, :4]])
    last = jnp.stack([b[:, 60:], c[:, 60:]])
    ye = lax.ppermute(jnp.where(y_even, last, first), "agg", side_in)
    yo = lax.ppermute(jnp.where(y_even, first, last), "agg", side_out)

    big, mid, own = (16, 96, 128), (12, 40, 128), (16, 64, 128)
    p0, vown, wown, b1, c1, edge, se, so = call(
        lambda *refs: head_kernel(aggs, *refs),
        (shape(16, 80, 128), shape(*own), shape(*own), shape(8, 40, 128), shape(8, 40, 128),
         shape(6, 80, 128), shape(9, 40, 128), shape(9, 40, 128)),
        [big] * 5 + [(8, 96, 128), (8, 80, 128)],
        at, b, c, ye, yo,
    )
    xe = lax.ppermute(se, "blk", near_in)
    xo = lax.ppermute(so, "blk", near_out)
    tall = (14, 40, 128)
    pe, e1, w1, bc2, se, so = call(
        lambda *refs: mid_kernel(blocks, aggs, *refs),
        (shape(4, 80, 128), shape(*mid), shape(*mid), shape(6, 16, 128), shape(6, 8, 128), shape(6, 8, 128)),
        [(4, 96, 128), (4, 80, 128), tall, tall, tall, (6, 40, 128), (6, 40, 128)],
        at, b1, c1, edge, xe, xo,
    )
    ye = lax.ppermute(se, "agg", side_in)
    yo = lax.ppermute(so, "agg", side_out)
    wide, se, so = call(
        join_kernel,
        (shape(6, 32, 128), shape(5, 32, 128), shape(5, 32, 128)),
        [],
        at, bc2, ye, yo,
    )
    xe = lax.ppermute(se, "blk", near_in)
    xo = lax.ppermute(so, "blk", near_out)
    small = (14, 32, 128)
    (out,) = call(
        lambda *refs: up_kernel(blocks, aggs, *refs),
        (shape(*own),),
        [small] * 5 + [(6, 48, 128), (6, 32, 128), (14, 48, 128), (6, 32, 128), mid, (12, 56, 128), (20, 96, 128)],
        at, p0, pe, vown, wown, e1, w1, wide, ye, yo, xe, xo,
    )
    return out


def solution(mesh):
    placed = (P("blk", "agg", None), P("blk", "agg", None))
    return jax.shard_map(
        shards, mesh=mesh, in_specs=placed, out_specs=P("blk", "agg", None), check_vma=False
    )
```

```python
import jax
import jax.numpy as jnp
from jax import lax
from jax.experimental import pallas as pl
from jax.experimental.pallas import tpu as pltpu
from jax.sharding import PartitionSpec as P

OMEGA = 0.8
F32 = jnp.float32
WINDOW = 64
STEPS = (4, 7, 3, 2, 4)
VM = pl.BlockSpec(memory_space=pltpu.VMEM)
SM = pl.BlockSpec(memory_space=pltpu.SMEM)


def shape(*dims):
    return jax.ShapeDtypeStruct(dims, F32)


def call(body, outs, scratch, *args, specs=None):
    return pl.pallas_call(
        body,
        out_shape=outs,
        in_specs=specs or [SM] + [VM] * (len(args) - 1),
        out_specs=tuple(VM for _ in outs),
        scratch_shapes=[pltpu.VMEM(s, F32) if isinstance(s, tuple) else s for s in scratch],
        compiler_params=pltpu.CompilerParams(vmem_limit_bytes=16 << 20),
    )(*args)


def loop(start, stop, step, body):
    def trip(n, carry):
        for i in range(step):
            body(start + n * step + i)
        return carry

    lax.fori_loop(0, (stop - start) // step, trip, 0)


def iota(rows, axis):
    return lax.broadcasted_iota(jnp.int32, (rows, 128), axis)


def pick(kind):
    i, j = iota(128, 0), iota(128, 1)
    if kind == "pairs":
        at = (i >> 1) == j
    elif kind == "beside":
        at = (i >= 2 * j - 1) & (i <= 2 * j + 2) & (j < 64)
    else:
        at = i == (j >> 1)
    return jnp.where(at, 1.0, 0.0).astype(jnp.bfloat16)


def halves(a):
    high = a.astype(jnp.bfloat16)
    return [high, (a - high.astype(F32)).astype(jnp.bfloat16)]


def dot(*terms):
    left = jnp.concatenate([h for a, _ in terms for h in halves(a)], axis=1)
    right = jnp.concatenate([m for _, m in terms for _ in (0, 1)], axis=0)
    return jnp.dot(left, right, preferred_element_type=F32)


def turn(v, by, axis):
    return pltpu.roll(v, by % v.shape[axis], axis)


def z_sum(v):
    lane = iota(v.shape[0], 1)
    below = jnp.where(lane == 0, 0.0, turn(v, 1, 1))
    return below + jnp.where(lane == 127, 0.0, turn(v, -1, 1))


def beside(ref, k, v, start, rows):
    return ref[k, pl.ds(start - 1, rows)] + ref[k, pl.ds(start + 1, rows)] + z_sum(v)


def windowed(ref, k, v, rows, at):
    below = jnp.where(at == 0, 0.0, ref[k, pl.ds(7, rows)])
    above = jnp.where(at == WINDOW - 1, 0.0, ref[k, pl.ds(9, rows)])
    return below + above + turn(v, 1, 1) + turn(v, -1, 1)


def inside(at, size):
    return (at >= 0) & (at < size)


def every_other(ref, k, start, rows):
    return ref[k, pl.ds(start, rows, stride=2), :]


def row_pairs(ref, k, start, rows):
    return every_other(ref, k, start, rows) + every_other(ref, k, start + 1, rows)


def gather(both, rest, k, at_both, at_rest, rows, at=None):
    below, above = every_other(both, k, at_both - 1, rows), every_other(both, k, at_both + 2, rows)
    if at is not None:
        below = jnp.where(at == 0, 0.0, below)
        above = jnp.where(at == WINDOW // 2 - 1, 0.0, above)
    own = row_pairs(both, k, at_both, rows)
    return row_pairs(rest, k, at_rest, rows) + own + below + above, own


def pack_kernel(b, c, se, so, first, last, sem):
    copies = []
    for n, ref in enumerate((b, c)):
        copies.append(pltpu.make_async_copy(ref.at[:, pl.ds(0, 8)], first.at[n], sem.at[2 * n]))
        copies.append(pltpu.make_async_copy(ref.at[:, pl.ds(56, 8)], last.at[n], sem.at[2 * n + 1]))
    for copy in copies:
        copy.start()
    y_even = (lax.axis_index("agg") & 1) == 0
    for copy in copies:
        copy.wait()
    for n in (0, 1):
        se[n] = jnp.where(y_even, last[n, :, 4:8], first[n, :, 0:4])
        so[n] = jnp.where(y_even, first[n, :, 0:4], last[n, :, 4:8])


def load_kernel(b, c, bv, cv, sem):
    copies = []
    for n in range(4):
        part = pl.ds(4 * n, 4)
        for i, (x, y) in enumerate(((b, bv), (c, cv))):
            copies.append(pltpu.make_async_copy(x.at[part], y.at[part], sem.at[2 * n + i]))
    for copy in copies:
        copy.start()
    for copy in copies:
        copy.wait()


def head_kernel(
    aggs,
    at, b, c, ye, yo,
    p0, v, w, b1, c1, edge, se, so,
    q, bx, cx, own1, rest1,
):
    bi, ai = at[0], at[1]
    x_even, y_even = (bi & 1) == 0, (ai & 1) == 0
    y_lo = jnp.where(ai > 0, OMEGA, 0.0)
    y_hi = jnp.where(ai < aggs - 1, OMEGA, 0.0)
    rows = pl.ds(8, 80)

    def put(p, rows, bb, cc, scale):
        ww = scale / (6.0 + cc)
        vv = ww * bb
        w[p, rows], v[p, rows], bx[p, rows], cx[p, rows] = ww, vv, bb, cc

    def plane(p):
        put(p, pl.ds(16, 64), b[p], c[p], OMEGA)
        lo = [jnp.where(y_even, yo[k, p], ye[k, p]) for k in (0, 1)]
        hi = [jnp.where(y_even, ye[k, p], yo[k, p]) for k in (0, 1)]
        put(p, pl.ds(12, 4), *lo, y_lo)
        put(p, pl.ds(80, 4), *hi, y_hi)

    loop(0, 16, STEPS[0], plane)

    def smooth(p):
        vv = v[p, rows]
        near = v[p - 1, rows] + v[p + 1, rows] + beside(v, p, vv, 8, 80)
        qq = 0.4 * vv + w[p, rows] * near
        q[p, rows] = qq
        p0[p] = qq + OMEGA * vv

    loop(1, 15, STEPS[1], smooth)
    for n, p, inner in ((0, 0, 1), (3, 15, 14)):
        vv, ww = v[p, rows], w[p, rows]
        edge[n] = 0.4 * vv + ww * (v[inner, rows] + beside(v, p, vv, 8, 80))
        edge[n + 1] = ww
        edge[n + 2] = vv

    def sums(k, p):
        cx[k, rows] = cx[p, rows] + cx[p + 1, rows]
        return 0.04 * (bx[p, rows] + bx[p + 1, rows])

    def coarse(k):
        p = 2 * k
        both = q[p, rows] + q[p + 1, rows]
        own1[k, rows] = both
        rest1[k] = sums(k, p) + (both + (q[p - 1, rows] + q[p + 2, rows]))

    own1[0, rows] = q[1, rows]
    rest1[0] = sums(0, 0) + (q[1, rows] + q[2, rows])
    loop(1, 7, STEPS[2], coarse)
    own1[7, rows] = q[14, rows]
    rest1[7] = sums(7, 14) + (q[14, rows] + q[13, rows])

    pairs, sides = pick("pairs"), pick("beside")

    def products(n):
        ends, mids, csums = [], [], []
        for k in (2 * n, 2 * n + 1):
            end, mid = gather(own1, rest1, k, 8, 0, 40)
            ends.append(end)
            mids.append(mid)
            csums.append(row_pairs(cx, k, 8, 40))
        bb = dot((jnp.concatenate(ends, axis=0), pairs), (jnp.concatenate(mids, axis=0), sides))
        cc = dot((jnp.concatenate(csums, axis=0), pairs))
        for i in (0, 1):
            b1[2 * n + i] = 0.5 * bb[40 * i : 40 * i + 40]
            c1[2 * n + i] = 0.5 * cc[40 * i : 40 * i + 40]

    loop(0, 4, STEPS[3], products)
    for ref, up in ((se, x_even), (so, jnp.logical_not(x_even))):
        for i in range(3):
            ref[72 * i : 72 * i + 72] = jnp.where(up, edge[3 + i, 4:76], edge[i, 4:76])
            mix = jnp.where(up, b1[5 + i], b1[i]) + turn(jnp.where(up, c1[5 + i], c1[i]), 64, 1)
            ref[216 + 40 * i : 256 + 40 * i] = mix


def mid_kernel(
    blocks, aggs,
    at, b1in, c1in, edge, xe, xo,
    pe, e1out, w1out, bc2, se, so,
    far, s4, r4, b1, c1, e1, own2, rest2,
):
    bi, ai = at[0], at[1]
    x_even, y_even = (bi & 1) == 0, (ai & 1) == 0
    pairs, sides = pick("pairs"), pick("beside")
    has_lo, has_hi = bi > 0, bi < blocks - 1
    lane1 = iota(40, 1) < 64

    def fetch(lo, start, rows):
        first = x_even if lo else jnp.logical_not(x_even)
        return jnp.where(first, xo[start : start + rows], xe[start : start + rows])

    for i, (lo, there) in enumerate(((True, has_lo), (False, has_hi))):
        for n in range(3):
            far[3 * i + n, 4:76] = jnp.where(there, fetch(lo, 72 * n, 72), 0.0)
        gb, wb, vb = [far[3 * i + n] for n in range(3)]
        g, w, v = [edge[3 * i + n] for n in range(3)]
        mine, other = g + w * vb, gb + wb * v
        here, there = (1, 0) if lo else (2, 3)
        pe[here] = mine + OMEGA * v
        pe[there] = other + OMEGA * vb
        s4[2 * i, pl.ds(8, 80)] = mine
        s4[2 * i + 1, pl.ds(8, 80)] = other
        r4[2 * i] = mine + other
        r4[2 * i + 1] = mine + other
        for n in range(3):
            mix = fetch(lo, 216 + 40 * n, 40)
            k = n if lo else 11 + n
            b1[k] = jnp.where(lane1, mix, 0.0)
            c1[k] = jnp.where(lane1, turn(mix, -64, 1), 0.0)
    for k in range(8):
        b1[k + 3] = b1in[k]
        c1[k + 3] = c1in[k]
    ends, mids = [], []
    for i in range(4):
        end, mid = gather(s4, r4, i, 8, 0, 40)
        ends.append(end)
        mids.append(mid)
    more = dot((jnp.concatenate(ends, axis=0), pairs), (jnp.concatenate(mids, axis=0), sides))
    for i, k in enumerate((3, 2, 10, 11)):
        b1[k] = b1[k] + 0.5 * more[40 * i : 40 * i + 40]

    row1 = ai * 32 - 4 + iota(40, 0)
    keep1 = inside(row1, 32 * aggs) & lane1
    for k in range(14):
        ok = keep1 & inside(bi * 8 + k - 3, 8 * blocks)
        ww = jnp.where(ok, OMEGA / (6.0 + c1[k]), 0.0)
        ee = jnp.where(ok, ww * b1[k], 0.0)
        e1[k] = ee
        if 0 < k < 13:
            w1out[k - 1], e1out[k - 1] = ww, ee

    at2 = (ai * 16 + iota(16, 0)) & (WINDOW // 2 - 1)
    lane16 = iota(16, 1)
    ends, mids, csums = [], [], []
    for k in range(6):
        p = 1 + 2 * k
        both = e1[p] + e1[p + 1]
        own2[k] = both
        rest2[k] = 0.2 * (b1[p] + b1[p + 1]) + (both + (e1[p - 1] + e1[p + 2]))
        end, mid = gather(own2, rest2, k, 4, 4, 16, at2)
        ends.append(end)
        mids.append(mid)
        csums.append(row_pairs(c1, p, 4, 16) + row_pairs(c1, p + 1, 4, 16))
    bb2 = dot((jnp.concatenate(ends, axis=0), pairs), (jnp.concatenate(mids, axis=0), sides))
    cc2 = dot((jnp.concatenate(csums, axis=0), pairs))
    for k in range(6):
        bb = jnp.where(lane16 < 32, 0.5 * bb2[16 * k : 16 * k + 16], 0.0)
        cc = jnp.where(lane16 < 32, 0.5 * cc2[16 * k : 16 * k + 16], 0.0)
        mix = bb + turn(cc, 32, 1)
        bc2[k] = mix
        for ref, lo_side in ((se, jnp.logical_not(y_even)), (so, y_even)):
            ref[k, 0:5] = jnp.where(lo_side, mix[0:5], mix[11:16])
            for j in (0, 1):
                n = 3 + (2 * k + j) % 8
                ref[k, 5 + j : 6 + j] = jnp.where(lo_side, e1[n, 5:6], e1[n, 34:35])
            ref[k, 7:8] = jnp.zeros((1, 128), F32)


def join_kernel(at, bc2, ye, yo, wide, se, so):
    bi, ai = at[0], at[1]
    x_even, y_even = (bi & 1) == 0, (ai & 1) == 0
    for k in range(6):
        wide[k] = jnp.zeros((32, 128), F32)
        wide[k, 3:8] = jnp.where(y_even, yo[k, 0:5], ye[k, 0:5])
        wide[k, 8:24] = bc2[k]
        wide[k, 24:29] = jnp.where(y_even, ye[k, 0:5], yo[k, 0:5])
    for k in range(3):
        low, high = wide[2 * k], wide[2 * k + 1]
        if k < 2:
            low, high = low + turn(high, 64, 1), high + turn(wide[2 * k + 2], 64, 1)
        se[k] = jnp.where(x_even, low, high)
        so[k] = jnp.where(x_even, high, low)


def up_kernel(
    blocks, aggs,
    at, p0, pe, v0, w0, e1in, w1, wide, ye, yo, xe, xo,
    out,
    e2, w2, b2, c2, own2, rest2, m2, t2, e1, m1, mf,
):
    bi, ai = at[0], at[1]
    x_even, y_even = (bi & 1) == 0, (ai & 1) == 0
    pairs, sides, copies = pick("pairs"), pick("beside"), pick("copies")

    def source(k):
        if 5 <= k < 9:
            return wide[k - 4], 0
        n = k if k < 5 else k - 9
        first = x_even if k < 5 else jnp.logical_not(x_even)
        return jnp.where(first, xo[n // 2], xe[n // 2]), 64 * (n % 2)

    row2 = ai * 16 - 8 + iota(32, 0)
    lane2 = iota(32, 1) < 32
    keep2 = inside(row2, 16 * aggs) & lane2
    for k in range(14):
        mix, lane = source(k)
        bb = jnp.where(lane2, turn(mix, -lane, 1) if lane else mix, 0.0)
        cc = jnp.where(lane2, turn(mix, -lane - 32, 1), 0.0)
        ww = jnp.where(keep2 & inside(bi * 4 + k - 5, 4 * blocks), OMEGA / (6.0 + cc), 0.0)
        b2[k], c2[k], w2[k], e2[k] = bb, cc, ww, ww * bb

    row3 = ai * 8 - 4 + iota(16, 0)
    at3 = row3 & (WINDOW // 2 - 1)
    ends, mids, sums = [], [], []
    for j in range(6):
        k = 1 + 2 * j
        both = e2[k] + e2[k + 1]
        own2[j, 8:40] = both
        rest2[j] = 0.2 * (b2[k] + b2[k + 1]) + (both + (e2[k - 1] + e2[k + 2]))
        end, mid = gather(own2, rest2, j, 8, 0, 16, at3)
        ends.append(end)
        mids.append(mid)
        sums.append(row_pairs(c2, k, 0, 16) + row_pairs(c2, k + 1, 0, 16))
    bb3 = dot((jnp.concatenate(ends, axis=0), pairs), (jnp.concatenate(mids, axis=0), sides))
    cc3 = dot((jnp.concatenate(sums, axis=0), pairs))
    keep3 = inside(row3, 8 * aggs) & (iota(16, 1) < 16)
    e3, w3 = [], []
    for j in range(6):
        bb, cc = 0.5 * bb3[16 * j : 16 * j + 16], 0.5 * cc3[16 * j : 16 * j + 16]
        ok = keep3 & inside(bi * 2 + j - 2, 2 * blocks)
        ww = jnp.where(ok, OMEGA / (6.0 + cc), 0.0)
        w3.append(ww)
        e3.append(jnp.where(ok, ww * bb, 0.0))
    solved = []
    for j in range(1, 5):
        v = e3[j]
        near = e3[j - 1] + e3[j + 1] + turn(v, 1, 0) + turn(v, -1, 0) + turn(v, 1, 1) + turn(v, -1, 1)
        solved.append(1.2 * v + w3[j] * near)
    wider = dot((jnp.concatenate(solved, axis=0), copies))
    for k in range(3, 11):
        j = (k - 3) // 2
        for r in (0, 1):
            m2[k, pl.ds(8 + r, 16, stride=2), :] = every_other(e2, k, r, 16) + wider[16 * j : 16 * j + 16]
    at2 = row2 & (WINDOW - 1)
    rows = pl.ds(8, 32)
    solved = []
    for k in range(4, 10):
        v = m2[k, rows]
        near = m2[k - 1, rows] + m2[k + 1, rows] + windowed(m2, k, v, 32, at2)
        solved.append(0.2 * v + e2[k] + w2[k] * near)
    wider = dot((jnp.concatenate(solved, axis=0), copies))
    for k in range(6):
        t2[k] = wider[32 * k : 32 * k + 32]

    for k in range(12):
        e1[k] = e1in[k]
    for n in range(8):
        k, j = n // 2, n % 2
        mine, other = ye[k, 5 + j : 6 + j], yo[k, 5 + j : 6 + j]
        e1[n + 2, 2:3] = jnp.where(y_even, other, mine)
        e1[n + 2, 37:38] = jnp.where(y_even, mine, other)
    for k in range(12):
        for r in (0, 1):
            m1[k, pl.ds(8 + r, 20, stride=2), :] = every_other(e1, k, r, 20) + t2[k // 2, 6:26]
    at1 = (ai * 32 - 4 + iota(40, 0)) & (WINDOW - 1)

    def fine(n, first):
        rows = pl.ds(8, 40)
        solved = []
        for k in (2 * n, 2 * n + 1):
            v = m1[k + 1, rows]
            near = m1[k, rows] + m1[k + 2, rows] + windowed(m1, k + 1, v, 40, at1)
            solved.append(0.2 * v + e1[k + 1] + w1[k + 1] * near)
        wider = dot((jnp.concatenate(solved, axis=0), copies))
        for k, (ref, p) in enumerate(first(4 * n)):
            for r in (0, 1):
                if ref is not None:
                    old = ref[p, pl.ds(r, 40, stride=2), :]
                    i = 40 * (k // 2)
                    mf[4 * n + k, pl.ds(8 + r, 40, stride=2), :] = old + wider[i : i + 40]

    def inner(n, carry):
        fine(n, lambda k: [(p0, k - 2), (p0, k - 1), (p0, k), (p0, k + 1)])
        return carry

    fine(0, lambda k: [(None, 0), (pe, 0), (pe, 1), (p0, 1)])
    lax.fori_loop(1, 4, inner, 0)
    fine(4, lambda k: [(p0, 14), (pe, 2), (pe, 3), (None, 0)])

    def last(k):
        rows = pl.ds(16, 64)
        m = mf[k + 2, rows]
        near = mf[k + 1, rows] + mf[k + 3, rows] + beside(mf, k + 2, m, 16, 64)
        out[k] = 0.2 * m + v0[k, rows] + w0[k, rows] * near

    loop(0, 16, STEPS[4], last)


def swaps(size, apart):
    inner, outer = [], []
    for i in range(size):
        inner.append((i, i ^ apart))
        outer.append((i, (i + apart) % size if i & apart else (i - apart) % size))
    return inner, outer


def shards(b, c):
    blocks, aggs = lax.axis_size("blk"), lax.axis_size("agg")
    bi, ai = lax.axis_index("blk"), lax.axis_index("agg")
    at = jnp.stack([bi, ai]).astype(jnp.int32)
    near_in, near_out = swaps(blocks, 1)
    side_in, side_out = swaps(aggs, 1)

    hbm = pl.BlockSpec(memory_space=pltpu.HBM)
    b, c = [pltpu.with_memory_space_constraint(x, pltpu.HBM) for x in (b, c)]
    own, faces = shape(16, 64, 128), shape(2, 16, 4, 128)
    se, so = call(
        pack_kernel,
        (faces, faces),
        [(2, 16, 8, 128), (2, 16, 8, 128), pltpu.SemaphoreType.DMA((4,))],
        b, c,
        specs=[hbm, hbm],
    )
    ye = lax.ppermute(se, "agg", side_in)
    yo = lax.ppermute(so, "agg", side_out)
    b, c = call(
        load_kernel,
        (own, own),
        [pltpu.SemaphoreType.DMA((8,))],
        b, c,
        specs=[hbm, hbm],
    )

    big, mid = (16, 96, 128), (12, 40, 128)
    p0, v, w, b1, c1, edge, se, so = call(
        lambda *refs: head_kernel(aggs, *refs),
        (shape(16, 80, 128), shape(*big), shape(*big), shape(8, 40, 128), shape(8, 40, 128),
         shape(6, 80, 128), shape(336, 128), shape(336, 128)),
        [big] * 3 + [(8, 96, 128), (8, 80, 128)],
        at, b, c, ye, yo,
    )
    xe = lax.ppermute(se, "blk", near_in)
    xo = lax.ppermute(so, "blk", near_out)
    tall = (14, 40, 128)
    pe, e1, w1, bc2, se, so = call(
        lambda *refs: mid_kernel(blocks, aggs, *refs),
        (shape(4, 80, 128), shape(*mid), shape(*mid), shape(6, 16, 128), shape(6, 8, 128), shape(6, 8, 128)),
        [(6, 80, 128), (4, 96, 128), (4, 80, 128), tall, tall, tall, (6, 40, 128), (6, 40, 128)],
        at, b1, c1, edge, xe, xo,
    )
    ye = lax.ppermute(se, "agg", side_in)
    yo = lax.ppermute(so, "agg", side_out)
    wide, se, so = call(
        join_kernel,
        (shape(6, 32, 128), shape(3, 32, 128), shape(3, 32, 128)),
        [],
        at, bc2, ye, yo,
    )
    xe = lax.ppermute(se, "blk", near_in)
    xo = lax.ppermute(so, "blk", near_out)
    small = (14, 32, 128)
    (out,) = call(
        lambda *refs: up_kernel(blocks, aggs, *refs),
        (own,),
        [small] * 4 + [(6, 48, 128), (6, 32, 128), (14, 48, 128), (6, 32, 128), mid, (12, 56, 128), (20, 96, 128)],
        at, p0, pe, v, w, e1, w1, wide, ye, yo, xe, xo,
    )
    return out


def solution(mesh):
    placed = (P("blk", "agg", None), P("blk", "agg", None))
    return jax.shard_map(
        shards, mesh=mesh, in_specs=placed, out_specs=P("blk", "agg", None), check_vma=False
    )
```

```python
import jax
import jax.numpy as jnp
from jax import lax
from jax.experimental import pallas as pl
from jax.experimental.pallas import tpu as pltpu
from jax.sharding import PartitionSpec as P

OMEGA = 0.8
F32 = jnp.float32
WINDOW = 64
STEPS = (4, 7, 3, 2, 4)
VM = pl.BlockSpec(memory_space=pltpu.VMEM)


def shape(*dims):
    return jax.ShapeDtypeStruct(dims, F32)


def call(body, outs, scratch, *args, specs=None):
    return pl.pallas_call(
        body,
        out_shape=outs,
        in_specs=specs or [VM] * len(args),
        out_specs=tuple(VM for _ in outs),
        scratch_shapes=[pltpu.VMEM(s, F32) if isinstance(s, tuple) else s for s in scratch],
        compiler_params=pltpu.CompilerParams(vmem_limit_bytes=16 << 20),
    )(*args)


def loop(start, stop, step, body):
    def trip(n, carry):
        for i in range(step):
            body(start + n * step + i)
        return carry

    lax.fori_loop(0, (stop - start) // step, trip, 0)


def iota(rows, axis):
    return lax.broadcasted_iota(jnp.int32, (rows, 128), axis)


def pick(kind):
    i, j = iota(128, 0), iota(128, 1)
    if kind == "pairs":
        at = (i >> 1) == j
    elif kind == "beside":
        at = (i >= 2 * j - 1) & (i <= 2 * j + 2) & (j < 64)
    else:
        at = i == (j >> 1)
    return jnp.where(at, 1.0, 0.0).astype(jnp.bfloat16)


def halves(a):
    high = a.astype(jnp.bfloat16)
    return [high, (a - high.astype(F32)).astype(jnp.bfloat16)]


def dot(*terms):
    left = jnp.concatenate([h for a, _ in terms for h in halves(a)], axis=1)
    right = jnp.concatenate([m for _, m in terms for _ in (0, 1)], axis=0)
    return jnp.dot(left, right, preferred_element_type=F32)


def turn(v, by, axis):
    return pltpu.roll(v, by % v.shape[axis], axis)


def z_sum(v):
    lane = iota(v.shape[0], 1)
    below = jnp.where(lane == 0, 0.0, turn(v, 1, 1))
    return below + jnp.where(lane == 127, 0.0, turn(v, -1, 1))


def beside(ref, k, v, start, rows):
    return ref[k, pl.ds(start - 1, rows)] + ref[k, pl.ds(start + 1, rows)] + z_sum(v)


def windowed(ref, k, v, rows, at):
    below = jnp.where(at == 0, 0.0, ref[k, pl.ds(7, rows)])
    above = jnp.where(at == WINDOW - 1, 0.0, ref[k, pl.ds(9, rows)])
    return below + above + turn(v, 1, 1) + turn(v, -1, 1)


def inside(at, size):
    return (at >= 0) & (at < size)


def every_other(ref, k, start, rows):
    return ref[k, pl.ds(start, rows, stride=2), :]


def row_pairs(ref, k, start, rows):
    return every_other(ref, k, start, rows) + every_other(ref, k, start + 1, rows)


def gather(both, rest, k, at_both, at_rest, rows, at=None):
    below, above = every_other(both, k, at_both - 1, rows), every_other(both, k, at_both + 2, rows)
    if at is not None:
        below = jnp.where(at == 0, 0.0, below)
        above = jnp.where(at == WINDOW // 2 - 1, 0.0, above)
    own = row_pairs(both, k, at_both, rows)
    return row_pairs(rest, k, at_rest, rows) + own + below + above, own


def pack_kernel(b, c, se, so, first, last, sem):
    copies = []
    for n, ref in enumerate((b, c)):
        copies.append(pltpu.make_async_copy(ref.at[:, pl.ds(0, 8)], first.at[n], sem.at[2 * n]))
        copies.append(pltpu.make_async_copy(ref.at[:, pl.ds(56, 8)], last.at[n], sem.at[2 * n + 1]))
    for copy in copies:
        copy.start()
    y_even = (lax.axis_index("agg") & 1) == 0
    for copy in copies:
        copy.wait()
    for n in (0, 1):
        se[n] = jnp.where(y_even, last[n, :, 4:8], first[n, :, 0:4])
        so[n] = jnp.where(y_even, first[n, :, 0:4], last[n, :, 4:8])


def load_kernel(b, c, bv, cv, sem):
    copies = []
    for n in range(4):
        part = pl.ds(4 * n, 4)
        for i, (x, y) in enumerate(((b, bv), (c, cv))):
            copies.append(pltpu.make_async_copy(x.at[part], y.at[part], sem.at[2 * n + i]))
    for copy in copies:
        copy.start()
    for copy in copies:
        copy.wait()


def head_kernel(
    aggs,
    b, c, ye, yo,
    p0, v, w, b1, c1, edge, se, so,
    q, bx, cx, own1, rest1,
):
    bi, ai = lax.axis_index("blk"), lax.axis_index("agg")
    x_even, y_even = (bi & 1) == 0, (ai & 1) == 0
    y_lo = jnp.where(ai > 0, OMEGA, 0.0)
    y_hi = jnp.where(ai < aggs - 1, OMEGA, 0.0)
    rows = pl.ds(8, 80)

    def put(p, rows, bb, cc, scale):
        ww = scale / (6.0 + cc)
        vv = ww * bb
        w[p, rows], v[p, rows], bx[p, rows], cx[p, rows] = ww, vv, bb, cc

    def plane(p):
        put(p, pl.ds(16, 64), b[p], c[p], OMEGA)
        lo = [jnp.where(y_even, yo[k, p], ye[k, p]) for k in (0, 1)]
        hi = [jnp.where(y_even, ye[k, p], yo[k, p]) for k in (0, 1)]
        put(p, pl.ds(12, 4), *lo, y_lo)
        put(p, pl.ds(80, 4), *hi, y_hi)

    loop(0, 16, STEPS[0], plane)

    def smooth(p):
        vv = v[p, rows]
        near = v[p - 1, rows] + v[p + 1, rows] + beside(v, p, vv, 8, 80)
        qq = 0.4 * vv + w[p, rows] * near
        q[p, rows] = qq
        p0[p] = qq + OMEGA * vv

    loop(1, 15, STEPS[1], smooth)
    for n, p, inner in ((0, 0, 1), (3, 15, 14)):
        vv, ww = v[p, rows], w[p, rows]
        edge[n] = 0.4 * vv + ww * (v[inner, rows] + beside(v, p, vv, 8, 80))
        edge[n + 1] = ww
        edge[n + 2] = vv

    def sums(k, p):
        cx[k, rows] = cx[p, rows] + cx[p + 1, rows]
        return 0.04 * (bx[p, rows] + bx[p + 1, rows])

    def coarse(k):
        p = 2 * k
        both = q[p, rows] + q[p + 1, rows]
        own1[k, rows] = both
        rest1[k] = sums(k, p) + (both + (q[p - 1, rows] + q[p + 2, rows]))

    own1[0, rows] = q[1, rows]
    rest1[0] = sums(0, 0) + (q[1, rows] + q[2, rows])
    loop(1, 7, STEPS[2], coarse)
    own1[7, rows] = q[14, rows]
    rest1[7] = sums(7, 14) + (q[14, rows] + q[13, rows])

    pairs, sides = pick("pairs"), pick("beside")

    def products(n):
        ends, mids, csums = [], [], []
        for k in (2 * n, 2 * n + 1):
            end, mid = gather(own1, rest1, k, 8, 0, 40)
            ends.append(end)
            mids.append(mid)
            csums.append(row_pairs(cx, k, 8, 40))
        bb = dot((jnp.concatenate(ends, axis=0), pairs), (jnp.concatenate(mids, axis=0), sides))
        cc = dot((jnp.concatenate(csums, axis=0), pairs))
        for i in (0, 1):
            b1[2 * n + i] = 0.5 * bb[40 * i : 40 * i + 40]
            c1[2 * n + i] = 0.5 * cc[40 * i : 40 * i + 40]

    loop(0, 4, STEPS[3], products)
    for ref, up in ((se, x_even), (so, jnp.logical_not(x_even))):
        for i in range(3):
            ref[72 * i : 72 * i + 72] = jnp.where(up, edge[3 + i, 4:76], edge[i, 4:76])
            mix = jnp.where(up, b1[5 + i], b1[i]) + turn(jnp.where(up, c1[5 + i], c1[i]), 64, 1)
            ref[216 + 40 * i : 256 + 40 * i] = mix


def mid_kernel(
    blocks, aggs,
    b1in, c1in, edge, xe, xo,
    pe, e1out, w1out, bc2, se, so,
    far, s4, r4, b1, c1, e1, own2, rest2,
):
    bi, ai = lax.axis_index("blk"), lax.axis_index("agg")
    x_even, y_even = (bi & 1) == 0, (ai & 1) == 0
    pairs, sides = pick("pairs"), pick("beside")
    has_lo, has_hi = bi > 0, bi < blocks - 1
    lane1 = iota(40, 1) < 64

    def fetch(lo, start, rows):
        first = x_even if lo else jnp.logical_not(x_even)
        return jnp.where(first, xo[start : start + rows], xe[start : start + rows])

    for i, (lo, there) in enumerate(((True, has_lo), (False, has_hi))):
        for n in range(3):
            far[3 * i + n, 4:76] = jnp.where(there, fetch(lo, 72 * n, 72), 0.0)
        gb, wb, vb = [far[3 * i + n] for n in range(3)]
        g, w, v = [edge[3 * i + n] for n in range(3)]
        mine, other = g + w * vb, gb + wb * v
        here, there = (1, 0) if lo else (2, 3)
        pe[here] = mine + OMEGA * v
        pe[there] = other + OMEGA * vb
        s4[2 * i, pl.ds(8, 80)] = mine
        s4[2 * i + 1, pl.ds(8, 80)] = other
        r4[2 * i] = mine + other
        r4[2 * i + 1] = mine + other
        for n in range(3):
            mix = fetch(lo, 216 + 40 * n, 40)
            k = n if lo else 11 + n
            b1[k] = jnp.where(lane1, mix, 0.0)
            c1[k] = jnp.where(lane1, turn(mix, -64, 1), 0.0)
    for k in range(8):
        b1[k + 3] = b1in[k]
        c1[k + 3] = c1in[k]
    ends, mids = [], []
    for i in range(4):
        end, mid = gather(s4, r4, i, 8, 0, 40)
        ends.append(end)
        mids.append(mid)
    more = dot((jnp.concatenate(ends, axis=0), pairs), (jnp.concatenate(mids, axis=0), sides))
    for i, k in enumerate((3, 2, 10, 11)):
        b1[k] = b1[k] + 0.5 * more[40 * i : 40 * i + 40]

    row1 = ai * 32 - 4 + iota(40, 0)
    keep1 = inside(row1, 32 * aggs) & lane1
    for k in range(14):
        ok = keep1 & inside(bi * 8 + k - 3, 8 * blocks)
        ww = jnp.where(ok, OMEGA / (6.0 + c1[k]), 0.0)
        ee = jnp.where(ok, ww * b1[k], 0.0)
        e1[k] = ee
        if 0 < k < 13:
            w1out[k - 1], e1out[k - 1] = ww, ee

    at2 = (ai * 16 + iota(16, 0)) & (WINDOW // 2 - 1)
    lane16 = iota(16, 1)
    ends, mids, csums = [], [], []
    for k in range(6):
        p = 1 + 2 * k
        both = e1[p] + e1[p + 1]
        own2[k] = both
        rest2[k] = 0.2 * (b1[p] + b1[p + 1]) + (both + (e1[p - 1] + e1[p + 2]))
        end, mid = gather(own2, rest2, k, 4, 4, 16, at2)
        ends.append(end)
        mids.append(mid)
        csums.append(row_pairs(c1, p, 4, 16) + row_pairs(c1, p + 1, 4, 16))
    bb2 = dot((jnp.concatenate(ends, axis=0), pairs), (jnp.concatenate(mids, axis=0), sides))
    cc2 = dot((jnp.concatenate(csums, axis=0), pairs))
    for k in range(6):
        bb = jnp.where(lane16 < 32, 0.5 * bb2[16 * k : 16 * k + 16], 0.0)
        cc = jnp.where(lane16 < 32, 0.5 * cc2[16 * k : 16 * k + 16], 0.0)
        mix = bb + turn(cc, 32, 1)
        bc2[k] = mix
        for ref, lo_side in ((se, jnp.logical_not(y_even)), (so, y_even)):
            ref[k, 0:5] = jnp.where(lo_side, mix[0:5], mix[11:16])
            for j in (0, 1):
                n = 3 + (2 * k + j) % 8
                ref[k, 5 + j : 6 + j] = jnp.where(lo_side, e1[n, 5:6], e1[n, 34:35])
            ref[k, 7:8] = jnp.zeros((1, 128), F32)


def join_kernel(bc2, ye, yo, wide, se, so):
    bi, ai = lax.axis_index("blk"), lax.axis_index("agg")
    x_even, y_even = (bi & 1) == 0, (ai & 1) == 0
    for k in range(6):
        wide[k] = jnp.zeros((32, 128), F32)
        wide[k, 3:8] = jnp.where(y_even, yo[k, 0:5], ye[k, 0:5])
        wide[k, 8:24] = bc2[k]
        wide[k, 24:29] = jnp.where(y_even, ye[k, 0:5], yo[k, 0:5])
    for k in range(3):
        low, high = wide[2 * k], wide[2 * k + 1]
        if k < 2:
            low, high = low + turn(high, 64, 1), high + turn(wide[2 * k + 2], 64, 1)
        se[k] = jnp.where(x_even, low, high)
        so[k] = jnp.where(x_even, high, low)


def up_kernel(
    blocks, aggs,
    p0, pe, v0, w0, e1in, w1, wide, ye, yo, xe, xo,
    out,
    e2, w2, b2, c2, own2, rest2, m2, t2, e1, m1, mf,
):
    bi, ai = lax.axis_index("blk"), lax.axis_index("agg")
    x_even, y_even = (bi & 1) == 0, (ai & 1) == 0
    pairs, sides, copies = pick("pairs"), pick("beside"), pick("copies")

    def source(k):
        if 5 <= k < 9:
            return wide[k - 4], 0
        n = k if k < 5 else k - 9
        first = x_even if k < 5 else jnp.logical_not(x_even)
        return jnp.where(first, xo[n // 2], xe[n // 2]), 64 * (n % 2)

    row2 = ai * 16 - 8 + iota(32, 0)
    lane2 = iota(32, 1) < 32
    keep2 = inside(row2, 16 * aggs) & lane2
    for k in range(14):
        mix, lane = source(k)
        bb = jnp.where(lane2, turn(mix, -lane, 1) if lane else mix, 0.0)
        cc = jnp.where(lane2, turn(mix, -lane - 32, 1), 0.0)
        ww = jnp.where(keep2 & inside(bi * 4 + k - 5, 4 * blocks), OMEGA / (6.0 + cc), 0.0)
        b2[k], c2[k], w2[k], e2[k] = bb, cc, ww, ww * bb

    row3 = ai * 8 - 4 + iota(16, 0)
    at3 = row3 & (WINDOW // 2 - 1)
    ends, mids, sums = [], [], []
    for j in range(6):
        k = 1 + 2 * j
        both = e2[k] + e2[k + 1]
        own2[j, 8:40] = both
        rest2[j] = 0.2 * (b2[k] + b2[k + 1]) + (both + (e2[k - 1] + e2[k + 2]))
        end, mid = gather(own2, rest2, j, 8, 0, 16, at3)
        ends.append(end)
        mids.append(mid)
        sums.append(row_pairs(c2, k, 0, 16) + row_pairs(c2, k + 1, 0, 16))
    bb3 = dot((jnp.concatenate(ends, axis=0), pairs), (jnp.concatenate(mids, axis=0), sides))
    cc3 = dot((jnp.concatenate(sums, axis=0), pairs))
    keep3 = inside(row3, 8 * aggs) & (iota(16, 1) < 16)
    e3, w3 = [], []
    for j in range(6):
        bb, cc = 0.5 * bb3[16 * j : 16 * j + 16], 0.5 * cc3[16 * j : 16 * j + 16]
        ok = keep3 & inside(bi * 2 + j - 2, 2 * blocks)
        ww = jnp.where(ok, OMEGA / (6.0 + cc), 0.0)
        w3.append(ww)
        e3.append(jnp.where(ok, ww * bb, 0.0))
    solved = []
    for j in range(1, 5):
        v = e3[j]
        near = e3[j - 1] + e3[j + 1] + turn(v, 1, 0) + turn(v, -1, 0) + turn(v, 1, 1) + turn(v, -1, 1)
        solved.append(1.2 * v + w3[j] * near)
    wider = dot((jnp.concatenate(solved, axis=0), copies))
    for k in range(3, 11):
        j = (k - 3) // 2
        for r in (0, 1):
            m2[k, pl.ds(8 + r, 16, stride=2), :] = every_other(e2, k, r, 16) + wider[16 * j : 16 * j + 16]
    at2 = row2 & (WINDOW - 1)
    rows = pl.ds(8, 32)
    solved = []
    for k in range(4, 10):
        v = m2[k, rows]
        near = m2[k - 1, rows] + m2[k + 1, rows] + windowed(m2, k, v, 32, at2)
        solved.append(0.2 * v + e2[k] + w2[k] * near)
    wider = dot((jnp.concatenate(solved, axis=0), copies))
    for k in range(6):
        t2[k] = wider[32 * k : 32 * k + 32]

    for k in range(12):
        e1[k] = e1in[k]
    for n in range(8):
        k, j = n // 2, n % 2
        mine, other = ye[k, 5 + j : 6 + j], yo[k, 5 + j : 6 + j]
        e1[n + 2, 2:3] = jnp.where(y_even, other, mine)
        e1[n + 2, 37:38] = jnp.where(y_even, mine, other)
    for k in range(12):
        for r in (0, 1):
            m1[k, pl.ds(8 + r, 20, stride=2), :] = every_other(e1, k, r, 20) + t2[k // 2, 6:26]
    at1 = (ai * 32 - 4 + iota(40, 0)) & (WINDOW - 1)

    def fine(n, first):
        rows = pl.ds(8, 40)
        solved = []
        for k in (2 * n, 2 * n + 1):
            v = m1[k + 1, rows]
            near = m1[k, rows] + m1[k + 2, rows] + windowed(m1, k + 1, v, 40, at1)
            solved.append(0.2 * v + e1[k + 1] + w1[k + 1] * near)
        wider = dot((jnp.concatenate(solved, axis=0), copies))
        for k, (ref, p) in enumerate(first(4 * n)):
            for r in (0, 1):
                if ref is not None:
                    old = ref[p, pl.ds(r, 40, stride=2), :]
                    i = 40 * (k // 2)
                    mf[4 * n + k, pl.ds(8 + r, 40, stride=2), :] = old + wider[i : i + 40]

    def inner(n, carry):
        fine(n, lambda k: [(p0, k - 2), (p0, k - 1), (p0, k), (p0, k + 1)])
        return carry

    fine(0, lambda k: [(None, 0), (pe, 0), (pe, 1), (p0, 1)])
    lax.fori_loop(1, 4, inner, 0)
    fine(4, lambda k: [(p0, 14), (pe, 2), (pe, 3), (None, 0)])

    def last(k):
        rows = pl.ds(16, 64)
        m = mf[k + 2, rows]
        near = mf[k + 1, rows] + mf[k + 3, rows] + beside(mf, k + 2, m, 16, 64)
        out[k] = 0.2 * m + v0[k, rows] + w0[k, rows] * near

    loop(0, 16, STEPS[4], last)


def swaps(size, apart):
    inner, outer = [], []
    for i in range(size):
        inner.append((i, i ^ apart))
        outer.append((i, (i + apart) % size if i & apart else (i - apart) % size))
    return inner, outer


def shards(b, c):
    blocks, aggs = lax.axis_size("blk"), lax.axis_size("agg")
    near_in, near_out = swaps(blocks, 1)
    side_in, side_out = swaps(aggs, 1)

    hbm = pl.BlockSpec(memory_space=pltpu.HBM)
    b, c = [pltpu.with_memory_space_constraint(x, pltpu.HBM) for x in (b, c)]
    own, faces = shape(16, 64, 128), shape(2, 16, 4, 128)
    se, so = call(
        pack_kernel,
        (faces, faces),
        [(2, 16, 8, 128), (2, 16, 8, 128), pltpu.SemaphoreType.DMA((4,))],
        b, c,
        specs=[hbm, hbm],
    )
    ye = lax.ppermute(se, "agg", side_in)
    yo = lax.ppermute(so, "agg", side_out)
    b, c = call(
        load_kernel,
        (own, own),
        [pltpu.SemaphoreType.DMA((8,))],
        b, c,
        specs=[hbm, hbm],
    )

    big, mid = (16, 96, 128), (12, 40, 128)
    p0, v, w, b1, c1, edge, se, so = call(
        lambda *refs: head_kernel(aggs, *refs),
        (shape(16, 80, 128), shape(*big), shape(*big), shape(8, 40, 128), shape(8, 40, 128),
         shape(6, 80, 128), shape(336, 128), shape(336, 128)),
        [big] * 3 + [(8, 96, 128), (8, 80, 128)],
        b, c, ye, yo,
    )
    xe = lax.ppermute(se, "blk", near_in)
    xo = lax.ppermute(so, "blk", near_out)
    tall = (14, 40, 128)
    pe, e1, w1, bc2, se, so = call(
        lambda *refs: mid_kernel(blocks, aggs, *refs),
        (shape(4, 80, 128), shape(*mid), shape(*mid), shape(6, 16, 128), shape(6, 8, 128), shape(6, 8, 128)),
        [(6, 80, 128), (4, 96, 128), (4, 80, 128), tall, tall, tall, (6, 40, 128), (6, 40, 128)],
        b1, c1, edge, xe, xo,
    )
    ye = lax.ppermute(se, "agg", side_in)
    yo = lax.ppermute(so, "agg", side_out)
    wide, se, so = call(
        join_kernel,
        (shape(6, 32, 128), shape(3, 32, 128), shape(3, 32, 128)),
        [],
        bc2, ye, yo,
    )
    xe = lax.ppermute(se, "blk", near_in)
    xo = lax.ppermute(so, "blk", near_out)
    small = (14, 32, 128)
    (out,) = call(
        lambda *refs: up_kernel(blocks, aggs, *refs),
        (own,),
        [small] * 4 + [(6, 48, 128), (6, 32, 128), (14, 48, 128), (6, 32, 128), mid, (12, 56, 128), (20, 96, 128)],
        p0, pe, v, w, e1, w1, wide, ye, yo, xe, xo,
    )
    return out


def solution(mesh):
    placed = (P("blk", "agg", None), P("blk", "agg", None))
    return jax.shard_map(
        shards, mesh=mesh, in_specs=placed, out_specs=P("blk", "agg", None), check_vma=False
    )
```

```python
import jax
import jax.numpy as jnp
from jax import lax
from jax.experimental import pallas as pl
from jax.experimental.pallas import tpu as pltpu
from jax.sharding import PartitionSpec as P

OMEGA = 0.8
F32 = jnp.float32
WINDOW = 64
STEPS = (4, 7, 3, 2)
VM = pl.BlockSpec(memory_space=pltpu.VMEM)


def shape(*dims):
    return jax.ShapeDtypeStruct(dims, F32)


def call(body, outs, scratch, *args, specs=None, out_specs=None):
    return pl.pallas_call(
        body,
        out_shape=outs,
        in_specs=specs or [VM] * len(args),
        out_specs=out_specs or tuple(VM for _ in outs),
        scratch_shapes=[pltpu.VMEM(s, F32) if isinstance(s, tuple) else s for s in scratch],
        compiler_params=pltpu.CompilerParams(vmem_limit_bytes=16 << 20),
    )(*args)


def loop(start, stop, step, body):
    def trip(n, carry):
        for i in range(step):
            body(start + n * step + i)
        return carry

    lax.fori_loop(0, (stop - start) // step, trip, 0)


def iota(rows, axis):
    return lax.broadcasted_iota(jnp.int32, (rows, 128), axis)


def pick(kind):
    i, j = iota(128, 0), iota(128, 1)
    if kind == "pairs":
        at = (i >> 1) == j
    elif kind == "beside":
        at = (i >= 2 * j - 1) & (i <= 2 * j + 2) & (j < 64)
    else:
        at = i == (j >> 1)
    return jnp.where(at, 1.0, 0.0).astype(jnp.bfloat16)


def halves(a):
    high = a.astype(jnp.bfloat16)
    return [high, (a - high.astype(F32)).astype(jnp.bfloat16)]


def dot(*terms):
    left = jnp.concatenate([h for a, _ in terms for h in halves(a)], axis=1)
    right = jnp.concatenate([m for _, m in terms for _ in (0, 1)], axis=0)
    return jnp.dot(left, right, preferred_element_type=F32)


def turn(v, by, axis):
    return pltpu.roll(v, by % v.shape[axis], axis)


def z_sum(v):
    lane = iota(v.shape[0], 1)
    below = jnp.where(lane == 0, 0.0, turn(v, 1, 1))
    return below + jnp.where(lane == 127, 0.0, turn(v, -1, 1))


def beside(ref, k, v, start, rows):
    return ref[k, pl.ds(start - 1, rows)] + ref[k, pl.ds(start + 1, rows)] + z_sum(v)


def windowed(ref, k, v, rows, at):
    below = jnp.where(at == 0, 0.0, ref[k, pl.ds(7, rows)])
    above = jnp.where(at == WINDOW - 1, 0.0, ref[k, pl.ds(9, rows)])
    return below + above + turn(v, 1, 1) + turn(v, -1, 1)


def inside(at, size):
    return (at >= 0) & (at < size)


def every_other(ref, k, start, rows):
    return ref[k, pl.ds(start, rows, stride=2), :]


def row_pairs(ref, k, start, rows):
    return every_other(ref, k, start, rows) + every_other(ref, k, start + 1, rows)


def gather(both, rest, k, at_both, at_rest, rows, at=None):
    below, above = every_other(both, k, at_both - 1, rows), every_other(both, k, at_both + 2, rows)
    if at is not None:
        below = jnp.where(at == 0, 0.0, below)
        above = jnp.where(at == WINDOW // 2 - 1, 0.0, above)
    own = row_pairs(both, k, at_both, rows)
    return row_pairs(rest, k, at_rest, rows) + own + below + above, own


def pack_kernel(b, c, se, so, first, last, sem):
    copies = []
    for n, ref in enumerate((b, c)):
        copies.append(pltpu.make_async_copy(ref.at[:, pl.ds(0, 8)], first.at[n], sem.at[2 * n]))
        copies.append(pltpu.make_async_copy(ref.at[:, pl.ds(56, 8)], last.at[n], sem.at[2 * n + 1]))
    for copy in copies:
        copy.start()
    y_even = (lax.axis_index("agg") & 1) == 0
    for copy in copies:
        copy.wait()
    for n in (0, 1):
        se[n] = jnp.where(y_even, last[n, :, 4:8], first[n, :, 0:4])
        so[n] = jnp.where(y_even, first[n, :, 0:4], last[n, :, 4:8])


def load_kernel(b, c, bv, cv, sem):
    copies = []
    for n in range(4):
        part = pl.ds(4 * n, 4)
        for i, (x, y) in enumerate(((b, bv), (c, cv))):
            copies.append(pltpu.make_async_copy(x.at[part], y.at[part], sem.at[2 * n + i]))
    for copy in copies:
        copy.start()
    for copy in copies:
        copy.wait()


def head_kernel(
    aggs,
    b, c, ye, yo,
    p0, v, w, b1, c1, edge, se, so,
    q, bx, cx, own1, rest1,
):
    bi, ai = lax.axis_index("blk"), lax.axis_index("agg")
    x_even, y_even = (bi & 1) == 0, (ai & 1) == 0
    y_lo = jnp.where(ai > 0, OMEGA, 0.0)
    y_hi = jnp.where(ai < aggs - 1, OMEGA, 0.0)
    rows = pl.ds(8, 80)

    def put(p, rows, bb, cc, scale):
        ww = scale / (6.0 + cc)
        vv = ww * bb
        w[p, rows], v[p, rows], bx[p, rows], cx[p, rows] = ww, vv, bb, cc

    def plane(p):
        put(p, pl.ds(16, 64), b[p], c[p], OMEGA)
        lo = [jnp.where(y_even, yo[k, p], ye[k, p]) for k in (0, 1)]
        hi = [jnp.where(y_even, ye[k, p], yo[k, p]) for k in (0, 1)]
        put(p, pl.ds(12, 4), *lo, y_lo)
        put(p, pl.ds(80, 4), *hi, y_hi)

    loop(0, 16, STEPS[0], plane)

    def smooth(p):
        vv = v[p, rows]
        near = v[p - 1, rows] + v[p + 1, rows] + beside(v, p, vv, 8, 80)
        qq = 0.4 * vv + w[p, rows] * near
        q[p, rows] = qq
        p0[p] = qq + OMEGA * vv

    loop(1, 15, STEPS[1], smooth)
    for n, p, inner in ((0, 0, 1), (3, 15, 14)):
        vv, ww = v[p, rows], w[p, rows]
        edge[n] = 0.4 * vv + ww * (v[inner, rows] + beside(v, p, vv, 8, 80))
        edge[n + 1] = ww
        edge[n + 2] = vv

    def sums(k, p):
        cx[k, rows] = cx[p, rows] + cx[p + 1, rows]
        return 0.04 * (bx[p, rows] + bx[p + 1, rows])

    def coarse(k):
        p = 2 * k
        both = q[p, rows] + q[p + 1, rows]
        own1[k, rows] = both
        rest1[k] = sums(k, p) + (both + (q[p - 1, rows] + q[p + 2, rows]))

    own1[0, rows] = q[1, rows]
    rest1[0] = sums(0, 0) + (q[1, rows] + q[2, rows])
    loop(1, 7, STEPS[2], coarse)
    own1[7, rows] = q[14, rows]
    rest1[7] = sums(7, 14) + (q[14, rows] + q[13, rows])

    pairs, sides = pick("pairs"), pick("beside")

    def products(n):
        ends, mids, csums = [], [], []
        for k in (2 * n, 2 * n + 1):
            end, mid = gather(own1, rest1, k, 8, 0, 40)
            ends.append(end)
            mids.append(mid)
            csums.append(row_pairs(cx, k, 8, 40))
        bb = dot((jnp.concatenate(ends, axis=0), pairs), (jnp.concatenate(mids, axis=0), sides))
        cc = dot((jnp.concatenate(csums, axis=0), pairs))
        for i in (0, 1):
            b1[2 * n + i] = 0.5 * bb[40 * i : 40 * i + 40]
            c1[2 * n + i] = 0.5 * cc[40 * i : 40 * i + 40]

    loop(0, 4, STEPS[3], products)
    for ref, up in ((se, x_even), (so, jnp.logical_not(x_even))):
        for i in range(3):
            ref[72 * i : 72 * i + 72] = jnp.where(up, edge[3 + i, 4:76], edge[i, 4:76])
            mix = jnp.where(up, b1[5 + i], b1[i]) + turn(jnp.where(up, c1[5 + i], c1[i]), 64, 1)
            ref[216 + 40 * i : 256 + 40 * i] = mix


def mid_kernel(
    blocks, aggs,
    b1in, c1in, edge, xe, xo,
    pe, e1out, w1out, bc2, se, so,
    far, s4, r4, b1, c1, e1, own2, rest2,
):
    bi, ai = lax.axis_index("blk"), lax.axis_index("agg")
    x_even, y_even = (bi & 1) == 0, (ai & 1) == 0
    pairs, sides = pick("pairs"), pick("beside")
    has_lo, has_hi = bi > 0, bi < blocks - 1
    lane1 = iota(40, 1) < 64

    def fetch(lo, start, rows):
        first = x_even if lo else jnp.logical_not(x_even)
        return jnp.where(first, xo[start : start + rows], xe[start : start + rows])

    for i, (lo, there) in enumerate(((True, has_lo), (False, has_hi))):
        for n in range(3):
            far[3 * i + n, 4:76] = jnp.where(there, fetch(lo, 72 * n, 72), 0.0)
        gb, wb, vb = [far[3 * i + n] for n in range(3)]
        g, w, v = [edge[3 * i + n] for n in range(3)]
        mine, other = g + w * vb, gb + wb * v
        here, there = (1, 0) if lo else (2, 3)
        pe[here] = mine + OMEGA * v
        pe[there] = other + OMEGA * vb
        s4[2 * i, pl.ds(8, 80)] = mine
        s4[2 * i + 1, pl.ds(8, 80)] = other
        r4[2 * i] = mine + other
        r4[2 * i + 1] = mine + other
        for n in range(3):
            mix = fetch(lo, 216 + 40 * n, 40)
            k = n if lo else 11 + n
            b1[k] = jnp.where(lane1, mix, 0.0)
            c1[k] = jnp.where(lane1, turn(mix, -64, 1), 0.0)
    for k in range(8):
        b1[k + 3] = b1in[k]
        c1[k + 3] = c1in[k]
    ends, mids = [], []
    for i in range(4):
        end, mid = gather(s4, r4, i, 8, 0, 40)
        ends.append(end)
        mids.append(mid)
    more = dot((jnp.concatenate(ends, axis=0), pairs), (jnp.concatenate(mids, axis=0), sides))
    for i, k in enumerate((3, 2, 10, 11)):
        b1[k] = b1[k] + 0.5 * more[40 * i : 40 * i + 40]

    row1 = ai * 32 - 4 + iota(40, 0)
    keep1 = inside(row1, 32 * aggs) & lane1
    for k in range(14):
        ok = keep1 & inside(bi * 8 + k - 3, 8 * blocks)
        ww = jnp.where(ok, OMEGA / (6.0 + c1[k]), 0.0)
        ee = jnp.where(ok, ww * b1[k], 0.0)
        e1[k] = ee
        if 0 < k < 13:
            w1out[k - 1], e1out[k - 1] = ww, ee

    at2 = (ai * 16 + iota(16, 0)) & (WINDOW // 2 - 1)
    lane16 = iota(16, 1)
    ends, mids, csums = [], [], []
    for k in range(6):
        p = 1 + 2 * k
        both = e1[p] + e1[p + 1]
        own2[k] = both
        rest2[k] = 0.2 * (b1[p] + b1[p + 1]) + (both + (e1[p - 1] + e1[p + 2]))
        end, mid = gather(own2, rest2, k, 4, 4, 16, at2)
        ends.append(end)
        mids.append(mid)
        csums.append(row_pairs(c1, p, 4, 16) + row_pairs(c1, p + 1, 4, 16))
    bb2 = dot((jnp.concatenate(ends, axis=0), pairs), (jnp.concatenate(mids, axis=0), sides))
    cc2 = dot((jnp.concatenate(csums, axis=0), pairs))
    for k in range(6):
        bb = jnp.where(lane16 < 32, 0.5 * bb2[16 * k : 16 * k + 16], 0.0)
        cc = jnp.where(lane16 < 32, 0.5 * cc2[16 * k : 16 * k + 16], 0.0)
        mix = bb + turn(cc, 32, 1)
        bc2[k] = mix
        for ref, lo_side in ((se, jnp.logical_not(y_even)), (so, y_even)):
            ref[k, 0:5] = jnp.where(lo_side, mix[0:5], mix[11:16])
            for j in (0, 1):
                n = 3 + (2 * k + j) % 8
                ref[k, 5 + j : 6 + j] = jnp.where(lo_side, e1[n, 5:6], e1[n, 34:35])
            ref[k, 7:8] = jnp.zeros((1, 128), F32)


def join_kernel(bc2, ye, yo, wide, se, so):
    bi, ai = lax.axis_index("blk"), lax.axis_index("agg")
    x_even, y_even = (bi & 1) == 0, (ai & 1) == 0
    for k in range(6):
        wide[k] = jnp.zeros((32, 128), F32)
        wide[k, 3:8] = jnp.where(y_even, yo[k, 0:5], ye[k, 0:5])
        wide[k, 8:24] = bc2[k]
        wide[k, 24:29] = jnp.where(y_even, ye[k, 0:5], yo[k, 0:5])
    for k in range(3):
        low, high = wide[2 * k], wide[2 * k + 1]
        if k < 2:
            low, high = low + turn(high, 64, 1), high + turn(wide[2 * k + 2], 64, 1)
        se[k] = jnp.where(x_even, low, high)
        so[k] = jnp.where(x_even, high, low)


def up_kernel(
    blocks, aggs,
    p0, pe, v0, w0, e1in, w1, wide, ye, yo, xe, xo,
    out,
    e2, w2, b2, c2, own2, rest2, m2, t2, e1, m1, mf, made, sem,
):
    bi, ai = lax.axis_index("blk"), lax.axis_index("agg")
    x_even, y_even = (bi & 1) == 0, (ai & 1) == 0
    pairs, sides, copies = pick("pairs"), pick("beside"), pick("copies")

    def source(k):
        if 5 <= k < 9:
            return wide[k - 4], 0
        n = k if k < 5 else k - 9
        first = x_even if k < 5 else jnp.logical_not(x_even)
        return jnp.where(first, xo[n // 2], xe[n // 2]), 64 * (n % 2)

    row2 = ai * 16 - 8 + iota(32, 0)
    lane2 = iota(32, 1) < 32
    keep2 = inside(row2, 16 * aggs) & lane2
    for k in range(14):
        mix, lane = source(k)
        bb = jnp.where(lane2, turn(mix, -lane, 1) if lane else mix, 0.0)
        cc = jnp.where(lane2, turn(mix, -lane - 32, 1), 0.0)
        ww = jnp.where(keep2 & inside(bi * 4 + k - 5, 4 * blocks), OMEGA / (6.0 + cc), 0.0)
        b2[k], c2[k], w2[k], e2[k] = bb, cc, ww, ww * bb

    row3 = ai * 8 - 4 + iota(16, 0)
    at3 = row3 & (WINDOW // 2 - 1)
    ends, mids, sums = [], [], []
    for j in range(6):
        k = 1 + 2 * j
        both = e2[k] + e2[k + 1]
        own2[j, 8:40] = both
        rest2[j] = 0.2 * (b2[k] + b2[k + 1]) + (both + (e2[k - 1] + e2[k + 2]))
        end, mid = gather(own2, rest2, j, 8, 0, 16, at3)
        ends.append(end)
        mids.append(mid)
        sums.append(row_pairs(c2, k, 0, 16) + row_pairs(c2, k + 1, 0, 16))
    bb3 = dot((jnp.concatenate(ends, axis=0), pairs), (jnp.concatenate(mids, axis=0), sides))
    cc3 = dot((jnp.concatenate(sums, axis=0), pairs))
    keep3 = inside(row3, 8 * aggs) & (iota(16, 1) < 16)
    e3, w3 = [], []
    for j in range(6):
        bb, cc = 0.5 * bb3[16 * j : 16 * j + 16], 0.5 * cc3[16 * j : 16 * j + 16]
        ok = keep3 & inside(bi * 2 + j - 2, 2 * blocks)
        ww = jnp.where(ok, OMEGA / (6.0 + cc), 0.0)
        w3.append(ww)
        e3.append(jnp.where(ok, ww * bb, 0.0))
    solved = []
    for j in range(1, 5):
        v = e3[j]
        near = e3[j - 1] + e3[j + 1] + turn(v, 1, 0) + turn(v, -1, 0) + turn(v, 1, 1) + turn(v, -1, 1)
        solved.append(1.2 * v + w3[j] * near)
    wider = dot((jnp.concatenate(solved, axis=0), copies))
    for k in range(3, 11):
        j = (k - 3) // 2
        for r in (0, 1):
            m2[k, pl.ds(8 + r, 16, stride=2), :] = every_other(e2, k, r, 16) + wider[16 * j : 16 * j + 16]
    at2 = row2 & (WINDOW - 1)
    rows = pl.ds(8, 32)
    solved = []
    for k in range(4, 10):
        v = m2[k, rows]
        near = m2[k - 1, rows] + m2[k + 1, rows] + windowed(m2, k, v, 32, at2)
        solved.append(0.2 * v + e2[k] + w2[k] * near)
    wider = dot((jnp.concatenate(solved, axis=0), copies))
    for k in range(6):
        t2[k] = wider[32 * k : 32 * k + 32]

    for k in range(12):
        e1[k] = e1in[k]
    for n in range(8):
        k, j = n // 2, n % 2
        mine, other = ye[k, 5 + j : 6 + j], yo[k, 5 + j : 6 + j]
        e1[n + 2, 2:3] = jnp.where(y_even, other, mine)
        e1[n + 2, 37:38] = jnp.where(y_even, mine, other)
    for k in range(12):
        for r in (0, 1):
            m1[k, pl.ds(8 + r, 20, stride=2), :] = every_other(e1, k, r, 20) + t2[k // 2, 6:26]
    at1 = (ai * 32 - 4 + iota(40, 0)) & (WINDOW - 1)

    def fine(n, first):
        rows = pl.ds(8, 40)
        solved = []
        for k in (2 * n, 2 * n + 1):
            v = m1[k + 1, rows]
            near = m1[k, rows] + m1[k + 2, rows] + windowed(m1, k + 1, v, 40, at1)
            solved.append(0.2 * v + e1[k + 1] + w1[k + 1] * near)
        wider = dot((jnp.concatenate(solved, axis=0), copies))
        for k, (ref, p) in enumerate(first(4 * n)):
            for r in (0, 1):
                if ref is not None:
                    old = ref[p, pl.ds(r, 40, stride=2), :]
                    i = 40 * (k // 2)
                    mf[4 * n + k, pl.ds(8 + r, 40, stride=2), :] = old + wider[i : i + 40]

    rows = pl.ds(16, 64)
    writes = []
    for n in range(5):
        old = [(p0, 4 * n - 2 + k) for k in range(4)]
        if n == 0:
            old[:3] = (None, 0), (pe, 0), (pe, 1)
        if n == 4:
            old[1:] = (pe, 2), (pe, 3), (None, 0)
        fine(n, lambda _: old)
        for k in range(max(4 * n - 3, 0), min(4 * n + 1, 16)):
            m = mf[k + 2, rows]
            near = mf[k + 1, rows] + mf[k + 3, rows] + beside(mf, k + 2, m, 16, 64)
            made[k] = 0.2 * m + v0[k, rows] + w0[k, rows] * near
            writes.append(pltpu.make_async_copy(made.at[k], out.at[k], sem.at[k]))
            writes[-1].start()
    for copy in writes:
        copy.wait()


def swaps(size, apart):
    inner, outer = [], []
    for i in range(size):
        inner.append((i, i ^ apart))
        outer.append((i, (i + apart) % size if i & apart else (i - apart) % size))
    return inner, outer


def shards(b, c):
    blocks, aggs = lax.axis_size("blk"), lax.axis_size("agg")
    near_in, near_out = swaps(blocks, 1)
    side_in, side_out = swaps(aggs, 1)

    hbm = pl.BlockSpec(memory_space=pltpu.HBM)
    b, c = [pltpu.with_memory_space_constraint(x, pltpu.HBM) for x in (b, c)]
    own, faces = shape(16, 64, 128), shape(2, 16, 4, 128)
    se, so = call(
        pack_kernel,
        (faces, faces),
        [(2, 16, 8, 128), (2, 16, 8, 128), pltpu.SemaphoreType.DMA((4,))],
        b, c,
        specs=[hbm, hbm],
    )
    ye = lax.ppermute(se, "agg", side_in)
    yo = lax.ppermute(so, "agg", side_out)
    b, c = call(
        load_kernel,
        (own, own),
        [pltpu.SemaphoreType.DMA((8,))],
        b, c,
        specs=[hbm, hbm],
    )

    big, mid = (16, 96, 128), (12, 40, 128)
    p0, v, w, b1, c1, edge, se, so = call(
        lambda *refs: head_kernel(aggs, *refs),
        (shape(16, 80, 128), shape(*big), shape(*big), shape(8, 40, 128), shape(8, 40, 128),
         shape(6, 80, 128), shape(336, 128), shape(336, 128)),
        [big] * 3 + [(8, 96, 128), (8, 80, 128)],
        b, c, ye, yo,
    )
    xe = lax.ppermute(se, "blk", near_in)
    xo = lax.ppermute(so, "blk", near_out)
    tall = (14, 40, 128)
    pe, e1, w1, bc2, se, so = call(
        lambda *refs: mid_kernel(blocks, aggs, *refs),
        (shape(4, 80, 128), shape(*mid), shape(*mid), shape(6, 16, 128), shape(6, 8, 128), shape(6, 8, 128)),
        [(6, 80, 128), (4, 96, 128), (4, 80, 128), tall, tall, tall, (6, 40, 128), (6, 40, 128)],
        b1, c1, edge, xe, xo,
    )
    ye = lax.ppermute(se, "agg", side_in)
    yo = lax.ppermute(so, "agg", side_out)
    wide, se, so = call(
        join_kernel,
        (shape(6, 32, 128), shape(3, 32, 128), shape(3, 32, 128)),
        [],
        bc2, ye, yo,
    )
    xe = lax.ppermute(se, "blk", near_in)
    xo = lax.ppermute(so, "blk", near_out)
    small = (14, 32, 128)
    (out,) = call(
        lambda *refs: up_kernel(blocks, aggs, *refs),
        (own,),
        [small] * 4 + [(6, 48, 128), (6, 32, 128), (14, 48, 128), (6, 32, 128), mid, (12, 56, 128), (20, 96, 128),
                       (16, 64, 128), pltpu.SemaphoreType.DMA((16,))],
        p0, pe, v, w, e1, w1, wide, ye, yo, xe, xo,
        out_specs=(hbm,),
    )
    return out


def solution(mesh):
    placed = (P("blk", "agg", None), P("blk", "agg", None))
    return jax.shard_map(
        shards, mesh=mesh, in_specs=placed, out_specs=P("blk", "agg", None), check_vma=False
    )
```

```python
import jax
import jax.numpy as jnp
from jax import lax
from jax.experimental import pallas as pl
from jax.experimental.pallas import tpu as pltpu
from jax.sharding import PartitionSpec as P

OMEGA = 0.8
F32 = jnp.float32
WINDOW = 64
STEPS = (4, 7, 3, 2)
VM = pl.BlockSpec(memory_space=pltpu.VMEM)


def shape(*dims):
    return jax.ShapeDtypeStruct(dims, F32)


def call(body, outs, scratch, *args, specs=None, out_specs=None, aliases={}):
    return pl.pallas_call(
        body,
        out_shape=outs,
        in_specs=specs or [VM] * len(args),
        out_specs=out_specs or tuple(VM for _ in outs),
        scratch_shapes=[pltpu.VMEM(s, F32) if isinstance(s, tuple) else s for s in scratch],
        input_output_aliases=aliases,
        compiler_params=pltpu.CompilerParams(vmem_limit_bytes=16 << 20),
    )(*args)


def loop(start, stop, step, body):
    def trip(n, carry):
        for i in range(step):
            body(start + n * step + i)
        return carry

    lax.fori_loop(0, (stop - start) // step, trip, 0)


def iota(rows, axis):
    return lax.broadcasted_iota(jnp.int32, (rows, 128), axis)


def pick(kind):
    i, j = iota(128, 0), iota(128, 1)
    if kind == "pairs":
        at = (i >> 1) == j
    elif kind == "beside":
        at = (i >= 2 * j - 1) & (i <= 2 * j + 2) & (j < 64)
    else:
        at = i == (j >> 1)
    return jnp.where(at, 1.0, 0.0).astype(jnp.bfloat16)


def halves(a):
    high = a.astype(jnp.bfloat16)
    return [high, (a - high.astype(F32)).astype(jnp.bfloat16)]


def dot(*terms):
    left = jnp.concatenate([h for a, _ in terms for h in halves(a)], axis=1)
    right = jnp.concatenate([m for _, m in terms for _ in (0, 1)], axis=0)
    return jnp.dot(left, right, preferred_element_type=F32)


def turn(v, by, axis):
    return pltpu.roll(v, by % v.shape[axis], axis)


def z_sum(v):
    lane = iota(v.shape[0], 1)
    below = jnp.where(lane == 0, 0.0, turn(v, 1, 1))
    return below + jnp.where(lane == 127, 0.0, turn(v, -1, 1))


def beside(ref, k, v, start, rows):
    return ref[k, pl.ds(start - 1, rows)] + ref[k, pl.ds(start + 1, rows)] + z_sum(v)


def windowed(ref, k, v, rows, at):
    below = jnp.where(at == 0, 0.0, ref[k, pl.ds(7, rows)])
    above = jnp.where(at == WINDOW - 1, 0.0, ref[k, pl.ds(9, rows)])
    return below + above + turn(v, 1, 1) + turn(v, -1, 1)


def inside(at, size):
    return (at >= 0) & (at < size)


def every_other(ref, k, start, rows):
    return ref[k, pl.ds(start, rows, stride=2), :]


def row_pairs(ref, k, start, rows):
    return every_other(ref, k, start, rows) + every_other(ref, k, start + 1, rows)


def gather(both, rest, k, at_both, at_rest, rows, at=None):
    below, above = every_other(both, k, at_both - 1, rows), every_other(both, k, at_both + 2, rows)
    if at is not None:
        below = jnp.where(at == 0, 0.0, below)
        above = jnp.where(at == WINDOW // 2 - 1, 0.0, above)
    own = row_pairs(both, k, at_both, rows)
    return row_pairs(rest, k, at_rest, rows) + own + below + above, own


def pack_kernel(b, c, se, so, sides, first, last, sem):
    copies = []
    for n, ref in enumerate((b, c)):
        copies.append(pltpu.make_async_copy(ref.at[:, pl.ds(0, 8)], first.at[n], sem.at[2 * n]))
        copies.append(pltpu.make_async_copy(ref.at[:, pl.ds(56, 8)], last.at[n], sem.at[2 * n + 1]))
    for copy in copies:
        copy.start()
    y_even = (lax.axis_index("agg") & 1) == 0
    for copy in copies:
        copy.wait()
    for n in (0, 1):
        se[n] = jnp.where(y_even, last[n, :, 4:8], first[n, :, 0:4])
        so[n] = jnp.where(y_even, first[n, :, 0:4], last[n, :, 4:8])
    sides[0], sides[1] = first[0], last[0]


def smoothed(v, w, q, p0, p, start, rows):
    at = pl.ds(start, rows)
    vv = v[p, at]
    near = v[p - 1, at] + v[p + 1, at] + beside(v, p, vv, start, rows)
    qq = 0.4 * vv + w[p, at] * near
    q[p, at] = qq
    p0[p, pl.ds(start - 8, rows)] = qq + OMEGA * vv


def child_sums(q, own1, rest1, k, start, rows, bb, end=None):
    at, p = pl.ds(start, rows), 2 * k
    if end is not None:
        both, outer = q[end[0], at], q[end[1], at]
    else:
        both, outer = q[p, at] + q[p + 1, at], q[p - 1, at] + q[p + 2, at]
    own1[k, at] = both
    rest1[k, pl.ds(start - 8, rows)] = 0.04 * bb + (both + outer)


def own_kernel(b, c, v, w, p0, own1, rest1, c1, q, bv, cv, cs, sem):
    copies = []
    for n in range(4):
        part = pl.ds(4 * n, 4)
        for i, (x, y) in enumerate(((b, bv), (c, cv))):
            copies.append(pltpu.make_async_copy(x.at[part], y.at[part], sem.at[2 * n + i]))
    for copy in copies:
        copy.start()
    for n in range(4):
        for copy in copies[2 * n : 2 * n + 2]:
            copy.wait()
        for p in range(4 * n, 4 * n + 4):
            ww = OMEGA / (6.0 + cv[p])
            w[p, 16:80] = ww
            v[p, 16:80] = ww * bv[p]
        for k in (2 * n, 2 * n + 1):
            cs[k] = cv[2 * k] + cv[2 * k + 1]
    loop(1, 15, STEPS[1], lambda p: smoothed(v, w, q, p0, p, 24, 48))

    def sums(k, end=None):
        child_sums(q, own1, rest1, k, 24, 48, bv[2 * k, 8:56] + bv[2 * k + 1, 8:56], end)

    sums(0, (1, 2))
    loop(1, 7, STEPS[2], sums)
    sums(7, (14, 13))
    pairs = pick("pairs")
    for n in range(2):
        some = range(4 * n, 4 * n + 4)
        cc = 0.5 * dot((jnp.concatenate([row_pairs(cs, k, 0, 32) for k in some], axis=0), pairs))
        for i, k in enumerate(some):
            c1[k, 4:36] = cc[32 * i : 32 * i + 32]


def head_kernel(
    aggs,
    ye, yo, sides, v_in, w_in, p0_in, own_in, rest_in, c_in,
    v, w, p0, own1, rest1, c1, b1, edge, se, so,
    q, bl, bh, cs,
):
    bi, ai = lax.axis_index("blk"), lax.axis_index("agg")
    x_even, y_even = (bi & 1) == 0, (ai & 1) == 0
    y_lo = jnp.where(ai > 0, OMEGA, 0.0)
    y_hi = jnp.where(ai < aggs - 1, OMEGA, 0.0)
    rows = pl.ds(8, 80)

    def halo(k):
        csum = []
        for first, scale, start in ((jnp.logical_not(y_even), y_lo, 12), (y_even, y_hi, 80)):
            got = []
            for p in (2 * k, 2 * k + 1):
                bb, cc = [jnp.where(first, ye[n, p], yo[n, p]) for n in (0, 1)]
                ww = scale / (6.0 + cc)
                w[p, pl.ds(start, 4)] = ww
                v[p, pl.ds(start, 4)] = ww * bb
                got.append((bb, cc))
            csum.append(got[0][1] + got[1][1])
            bsum = got[0][0] + got[1][0]
            if start == 12:
                bl[k, 4:8] = bsum
            else:
                bh[k, 8:12] = bsum
        bl[k, 8:16] = sides[0, 2 * k] + sides[0, 2 * k + 1]
        bh[k, 0:8] = sides[1, 2 * k] + sides[1, 2 * k + 1]
        cs[k, 0:4] = csum[0]
        cs[k, 4:8] = csum[1]

    loop(0, 8, STEPS[0], halo)

    def smooth(p):
        for start in (8, 72):
            smoothed(v, w, q, p0, p, start, 16)

    loop(1, 15, STEPS[1], smooth)
    for n, p, inner in ((0, 0, 1), (3, 15, 14)):
        vv, ww = v[p, rows], w[p, rows]
        edge[n] = 0.4 * vv + ww * (v[inner, rows] + beside(v, p, vv, 8, 80))
        edge[n + 1] = ww
        edge[n + 2] = vv

    def sums(k, end=None):
        child_sums(q, own1, rest1, k, 8, 16, bl[k], end)
        child_sums(q, own1, rest1, k, 72, 16, bh[k], end)

    sums(0, (1, 2))
    loop(1, 7, STEPS[2], sums)
    sums(7, (14, 13))
    pairs, near = pick("pairs"), pick("beside")
    cc = 0.5 * dot((jnp.concatenate([row_pairs(cs, k, 0, 4) for k in range(8)], axis=0), pairs))
    for k in range(8):
        c1[k, 4:36] = c_in[k, 4:36]
        c1[k, 2:4] = cc[4 * k : 4 * k + 2]
        c1[k, 36:38] = cc[4 * k + 2 : 4 * k + 4]

    def products(n):
        ends, mids = [], []
        for k in (2 * n, 2 * n + 1):
            end, mid = gather(own1, rest1, k, 8, 0, 40)
            ends.append(end)
            mids.append(mid)
        bb = dot((jnp.concatenate(ends, axis=0), pairs), (jnp.concatenate(mids, axis=0), near))
        for i in (0, 1):
            b1[2 * n + i] = 0.5 * bb[40 * i : 40 * i + 40]

    loop(0, 4, STEPS[3], products)
    for ref, up in ((se, x_even), (so, jnp.logical_not(x_even))):
        for i in range(3):
            ref[72 * i : 72 * i + 72] = jnp.where(up, edge[3 + i, 4:76], edge[i, 4:76])
        for i in (0, 1):
            mix = jnp.where(up, b1[6 + i], b1[i]) + turn(jnp.where(up, c1[6 + i], c1[i]), 64, 1)
            ref[216 + 34 * i : 250 + 34 * i] = mix[3:37]
        third = OMEGA / (6.0 + jnp.where(up, c1[5], c1[2])) * jnp.where(up, b1[5], b1[2])
        ref[284:301] = third[3:20] + turn(third, 64, 1)[20:37]
        ref[301:304] = jnp.zeros((3, 128), F32)


def mid_kernel(
    blocks, aggs,
    b1in, c1in, edge, xe, xo,
    pe, e1out, w1out, bc2, se, so,
    far, s4, r4, b1, c1, e1, own2, rest2,
):
    bi, ai = lax.axis_index("blk"), lax.axis_index("agg")
    x_even, y_even = (bi & 1) == 0, (ai & 1) == 0
    pairs, sides = pick("pairs"), pick("beside")
    has_lo, has_hi = bi > 0, bi < blocks - 1
    lane1 = iota(40, 1) < 64

    def fetch(lo, start, rows):
        first = x_even if lo else jnp.logical_not(x_even)
        return jnp.where(first, xo[start : start + rows], xe[start : start + rows])

    for i, (lo, there) in enumerate(((True, has_lo), (False, has_hi))):
        for n in range(3):
            far[3 * i + n, 4:76] = jnp.where(there, fetch(lo, 72 * n, 72), 0.0)
        gb, wb, vb = [far[3 * i + n] for n in range(3)]
        g, w, v = [edge[3 * i + n] for n in range(3)]
        mine, other = g + w * vb, gb + wb * v
        here, there = (1, 0) if lo else (2, 3)
        pe[here] = mine + OMEGA * v
        pe[there] = other + OMEGA * vb
        s4[2 * i, pl.ds(8, 80)] = mine
        s4[2 * i + 1, pl.ds(8, 80)] = other
        r4[2 * i] = mine + other
        r4[2 * i + 1] = mine + other
        for n in (0, 1):
            mix = fetch(lo, 216 + 34 * n, 34)
            k = 1 + n if lo else 11 + n
            b1[k, 3:37] = jnp.where(lane1[:34], mix, 0.0)
            c1[k, 3:37] = jnp.where(lane1[:34], turn(mix, -64, 1), 0.0)
        k = 0 if lo else 13
        there = inside(bi * 8 + k - 3, 8 * blocks) & lane1[:17]
        mix = fetch(lo, 284, 17)
        for start, part in ((3, mix), (20, turn(mix, -64, 1))):
            e1[k, start : start + 17] = jnp.where(there & inside(ai * 32 - 4 + start + iota(17, 0), 32 * aggs), part, 0.0)
    for k in range(8):
        b1[k + 3] = b1in[k]
        c1[k + 3] = c1in[k]
    ends, mids = [], []
    for i in range(4):
        end, mid = gather(s4, r4, i, 8, 0, 40)
        ends.append(end)
        mids.append(mid)
    more = dot((jnp.concatenate(ends, axis=0), pairs), (jnp.concatenate(mids, axis=0), sides))
    for i, k in enumerate((3, 2, 10, 11)):
        b1[k] = b1[k] + 0.5 * more[40 * i : 40 * i + 40]

    row1 = ai * 32 - 4 + iota(40, 0)
    keep1 = inside(row1, 32 * aggs) & lane1
    for k in range(1, 13):
        ok = keep1 & inside(bi * 8 + k - 3, 8 * blocks)
        ww = jnp.where(ok, OMEGA / (6.0 + c1[k]), 0.0)
        ee = jnp.where(ok, ww * b1[k], 0.0)
        e1[k] = ee
        w1out[k - 1], e1out[k - 1] = ww, ee

    at2 = (ai * 16 + iota(16, 0)) & (WINDOW // 2 - 1)
    lane16 = iota(16, 1)
    ends, mids, csums = [], [], []
    for k in range(6):
        p = 1 + 2 * k
        both = e1[p] + e1[p + 1]
        own2[k] = both
        rest2[k] = 0.2 * (b1[p] + b1[p + 1]) + (both + (e1[p - 1] + e1[p + 2]))
        end, mid = gather(own2, rest2, k, 4, 4, 16, at2)
        ends.append(end)
        mids.append(mid)
        csums.append(row_pairs(c1, p, 4, 16) + row_pairs(c1, p + 1, 4, 16))
    bb2 = dot((jnp.concatenate(ends, axis=0), pairs), (jnp.concatenate(mids, axis=0), sides))
    cc2 = dot((jnp.concatenate(csums, axis=0), pairs))
    for k in range(6):
        bb = jnp.where(lane16 < 32, 0.5 * bb2[16 * k : 16 * k + 16], 0.0)
        cc = jnp.where(lane16 < 32, 0.5 * cc2[16 * k : 16 * k + 16], 0.0)
        mix = bb + turn(cc, 32, 1)
        bc2[k] = mix
        for ref, lo_side in ((se, jnp.logical_not(y_even)), (so, y_even)):
            ref[k, 0:5] = jnp.where(lo_side, mix[0:5], mix[11:16])
            for j in (0, 1):
                n = 3 + (2 * k + j) % 8
                ref[k, 5 + j : 6 + j] = jnp.where(lo_side, e1[n, 5:6], e1[n, 34:35])
            ref[k, 7:8] = jnp.zeros((1, 128), F32)


def join_kernel(bc2, ye, yo, wide, se, so):
    bi, ai = lax.axis_index("blk"), lax.axis_index("agg")
    x_even, y_even = (bi & 1) == 0, (ai & 1) == 0
    for k in range(6):
        wide[k] = jnp.zeros((32, 128), F32)
        wide[k, 3:8] = jnp.where(y_even, yo[k, 0:5], ye[k, 0:5])
        wide[k, 8:24] = bc2[k]
        wide[k, 24:29] = jnp.where(y_even, ye[k, 0:5], yo[k, 0:5])
    for k in range(3):
        low, high = wide[2 * k], wide[2 * k + 1]
        if k < 2:
            low, high = low + turn(high, 64, 1), high + turn(wide[2 * k + 2], 64, 1)
        se[k] = jnp.where(x_even, low, high)
        so[k] = jnp.where(x_even, high, low)


def up_kernel(
    blocks, aggs,
    p0, pe, v0, w0, e1in, w1, wide, ye, yo, xe, xo,
    out,
    e2, w2, b2, c2, own2, rest2, m2, t2, e1, m1, mf, made, sem,
):
    bi, ai = lax.axis_index("blk"), lax.axis_index("agg")
    x_even, y_even = (bi & 1) == 0, (ai & 1) == 0
    pairs, sides, copies = pick("pairs"), pick("beside"), pick("copies")

    def source(k):
        if 5 <= k < 9:
            return wide[k - 4], 0
        n = k if k < 5 else k - 9
        first = x_even if k < 5 else jnp.logical_not(x_even)
        return jnp.where(first, xo[n // 2], xe[n // 2]), 64 * (n % 2)

    row2 = ai * 16 - 8 + iota(32, 0)
    lane2 = iota(32, 1) < 32
    keep2 = inside(row2, 16 * aggs) & lane2
    for k in range(14):
        mix, lane = source(k)
        bb = jnp.where(lane2, turn(mix, -lane, 1) if lane else mix, 0.0)
        cc = jnp.where(lane2, turn(mix, -lane - 32, 1), 0.0)
        ww = jnp.where(keep2 & inside(bi * 4 + k - 5, 4 * blocks), OMEGA / (6.0 + cc), 0.0)
        b2[k], c2[k], w2[k], e2[k] = bb, cc, ww, ww * bb

    row3 = ai * 8 - 4 + iota(16, 0)
    at3 = row3 & (WINDOW // 2 - 1)
    ends, mids, sums = [], [], []
    for j in range(6):
        k = 1 + 2 * j
        both = e2[k] + e2[k + 1]
        own2[j, 8:40] = both
        rest2[j] = 0.2 * (b2[k] + b2[k + 1]) + (both + (e2[k - 1] + e2[k + 2]))
        end, mid = gather(own2, rest2, j, 8, 0, 16, at3)
        ends.append(end)
        mids.append(mid)
        sums.append(row_pairs(c2, k, 0, 16) + row_pairs(c2, k + 1, 0, 16))
    bb3 = dot((jnp.concatenate(ends, axis=0), pairs), (jnp.concatenate(mids, axis=0), sides))
    cc3 = dot((jnp.concatenate(sums, axis=0), pairs))
    keep3 = inside(row3, 8 * aggs) & (iota(16, 1) < 16)
    e3, w3 = [], []
    for j in range(6):
        bb, cc = 0.5 * bb3[16 * j : 16 * j + 16], 0.5 * cc3[16 * j : 16 * j + 16]
        ok = keep3 & inside(bi * 2 + j - 2, 2 * blocks)
        ww = jnp.where(ok, OMEGA / (6.0 + cc), 0.0)
        w3.append(ww)
        e3.append(jnp.where(ok, ww * bb, 0.0))
    solved = []
    for j in range(1, 5):
        v = e3[j]
        near = e3[j - 1] + e3[j + 1] + turn(v, 1, 0) + turn(v, -1, 0) + turn(v, 1, 1) + turn(v, -1, 1)
        solved.append(1.2 * v + w3[j] * near)
    wider = dot((jnp.concatenate(solved, axis=0), copies))
    for k in range(3, 11):
        j = (k - 3) // 2
        for r in (0, 1):
            m2[k, pl.ds(8 + r, 16, stride=2), :] = every_other(e2, k, r, 16) + wider[16 * j : 16 * j + 16]
    at2 = row2 & (WINDOW - 1)
    rows = pl.ds(8, 32)
    solved = []
    for k in range(4, 10):
        v = m2[k, rows]
        near = m2[k - 1, rows] + m2[k + 1, rows] + windowed(m2, k, v, 32, at2)
        solved.append(0.2 * v + e2[k] + w2[k] * near)
    wider = dot((jnp.concatenate(solved, axis=0), copies))
    for k in range(6):
        t2[k] = wider[32 * k : 32 * k + 32]

    for k in range(12):
        e1[k] = e1in[k]
    for n in range(8):
        k, j = n // 2, n % 2
        mine, other = ye[k, 5 + j : 6 + j], yo[k, 5 + j : 6 + j]
        e1[n + 2, 2:3] = jnp.where(y_even, other, mine)
        e1[n + 2, 37:38] = jnp.where(y_even, mine, other)
    for k in range(12):
        for r in (0, 1):
            m1[k, pl.ds(8 + r, 20, stride=2), :] = every_other(e1, k, r, 20) + t2[k // 2, 6:26]
    at1 = (ai * 32 - 4 + iota(40, 0)) & (WINDOW - 1)

    def fine(n, first):
        rows = pl.ds(8, 40)
        solved = []
        for k in (2 * n, 2 * n + 1):
            v = m1[k + 1, rows]
            near = m1[k, rows] + m1[k + 2, rows] + windowed(m1, k + 1, v, 40, at1)
            solved.append(0.2 * v + e1[k + 1] + w1[k + 1] * near)
        wider = dot((jnp.concatenate(solved, axis=0), copies))
        for k, (ref, p) in enumerate(first(4 * n)):
            for r in (0, 1):
                if ref is not None:
                    old = ref[p, pl.ds(r, 40, stride=2), :]
                    i = 40 * (k // 2)
                    mf[4 * n + k, pl.ds(8 + r, 40, stride=2), :] = old + wider[i : i + 40]

    rows = pl.ds(16, 64)
    writes = []
    for n in range(5):
        old = [(p0, 4 * n - 2 + k) for k in range(4)]
        if n == 0:
            old[:3] = (None, 0), (pe, 0), (pe, 1)
        if n == 4:
            old[1:] = (pe, 2), (pe, 3), (None, 0)
        fine(n, lambda _: old)
        for k in range(max(4 * n - 3, 0), min(4 * n + 1, 16)):
            m = mf[k + 2, rows]
            near = mf[k + 1, rows] + mf[k + 3, rows] + beside(mf, k + 2, m, 16, 64)
            made[k] = 0.2 * m + v0[k, rows] + w0[k, rows] * near
            writes.append(pltpu.make_async_copy(made.at[k], out.at[k], sem.at[k]))
            writes[-1].start()
    for copy in writes:
        copy.wait()


def swaps(size, apart):
    inner, outer = [], []
    for i in range(size):
        inner.append((i, i ^ apart))
        outer.append((i, (i + apart) % size if i & apart else (i - apart) % size))
    return inner, outer


def shards(b, c):
    blocks, aggs = lax.axis_size("blk"), lax.axis_size("agg")
    near_in, near_out = swaps(blocks, 1)
    side_in, side_out = swaps(aggs, 1)

    hbm = pl.BlockSpec(memory_space=pltpu.HBM)
    b, c = [pltpu.with_memory_space_constraint(x, pltpu.HBM) for x in (b, c)]
    faces = shape(2, 16, 4, 128)
    se, so, sides = call(
        pack_kernel,
        (faces, faces, shape(2, 16, 8, 128)),
        [(2, 16, 8, 128), (2, 16, 8, 128), pltpu.SemaphoreType.DMA((4,))],
        b, c,
        specs=[hbm, hbm],
    )
    ye = lax.ppermute(se, "agg", side_in)
    yo = lax.ppermute(so, "agg", side_out)

    mid, big = (12, 40, 128), shape(16, 96, 128)
    fields = (big, big, shape(16, 80, 128), shape(8, 96, 128), shape(8, 80, 128))
    v, w, p0, own1, rest1, c1 = call(
        own_kernel,
        fields + (shape(8, 40, 128),),
        [(16, 96, 128), (16, 64, 128), (16, 64, 128), (8, 64, 128), pltpu.SemaphoreType.DMA((8,))],
        b, c,
        specs=[hbm, hbm],
    )
    v, w, p0, _, _, c1, b1, edge, se, so = call(
        lambda *refs: head_kernel(aggs, *refs),
        fields + (shape(8, 40, 128), shape(8, 40, 128), shape(6, 80, 128), shape(304, 128), shape(304, 128)),
        [(16, 96, 128), (8, 16, 128), (8, 16, 128), (8, 8, 128)],
        ye, yo, sides, v, w, p0, own1, rest1, c1,
        aliases={3 + i: i for i in range(5)},
    )
    xe = lax.ppermute(se, "blk", near_in)
    xo = lax.ppermute(so, "blk", near_out)
    tall = (14, 40, 128)
    pe, e1, w1, bc2, se, so = call(
        lambda *refs: mid_kernel(blocks, aggs, *refs),
        (shape(4, 80, 128), shape(*mid), shape(*mid), shape(6, 16, 128), shape(6, 8, 128), shape(6, 8, 128)),
        [(6, 80, 128), (4, 96, 128), (4, 80, 128), tall, tall, tall, (6, 40, 128), (6, 40, 128)],
        b1, c1, edge, xe, xo,
    )
    ye = lax.ppermute(se, "agg", side_in)
    yo = lax.ppermute(so, "agg", side_out)
    wide, se, so = call(
        join_kernel,
        (shape(6, 32, 128), shape(3, 32, 128), shape(3, 32, 128)),
        [],
        bc2, ye, yo,
    )
    xe = lax.ppermute(se, "blk", near_in)
    xo = lax.ppermute(so, "blk", near_out)
    small = (14, 32, 128)
    (out,) = call(
        lambda *refs: up_kernel(blocks, aggs, *refs),
        (shape(16, 64, 128),),
        [small] * 4 + [(6, 48, 128), (6, 32, 128), (14, 48, 128), (6, 32, 128), mid, (12, 56, 128), (20, 96, 128),
                       (16, 64, 128), pltpu.SemaphoreType.DMA((16,))],
        p0, pe, v, w, e1, w1, wide, ye, yo, xe, xo,
        out_specs=(hbm,),
    )
    return out


def solution(mesh):
    placed = (P("blk", "agg", None), P("blk", "agg", None))
    return jax.shard_map(
        shards, mesh=mesh, in_specs=placed, out_specs=P("blk", "agg", None), check_vma=False
    )
```

```python
import jax
import jax.numpy as jnp
from jax import lax
from jax.experimental import pallas as pl
from jax.experimental.pallas import tpu as pltpu
from jax.sharding import PartitionSpec as P


OMEGA = 0.8
F32 = jnp.float32
WINDOW = 64
STEPS = (8, 14, 6, 4)
VM = pl.BlockSpec(memory_space=pltpu.VMEM)


def shape(*dims):
    return jax.ShapeDtypeStruct(dims, F32)


def call(body, outs, scratch, *args, specs=None, out_specs=None, aliases={}):
    return pl.pallas_call(
        body,
        out_shape=outs,
        in_specs=specs or [VM] * len(args),
        out_specs=out_specs or tuple(VM for _ in outs),
        scratch_shapes=[pltpu.VMEM(s, F32) if isinstance(s, tuple) else s for s in scratch],
        input_output_aliases=aliases,
        compiler_params=pltpu.CompilerParams(vmem_limit_bytes=16 << 20),
    )(*args)


def loop(start, stop, step, body):
    def trip(n, carry):
        for i in range(step):
            body(start + n * step + i)
        return carry

    lax.fori_loop(0, (stop - start) // step, trip, 0)


def iota(rows, axis):
    return lax.broadcasted_iota(jnp.int32, (rows, 128), axis)


def pick(kind):
    i, j = iota(128, 0), iota(128, 1)
    if kind == "pairs":
        at = (i >> 1) == j
    elif kind == "beside":
        at = (i >= 2 * j - 1) & (i <= 2 * j + 2) & (j < 64)
    else:
        at = i == (j >> 1)
    return jnp.where(at, 1.0, 0.0).astype(jnp.bfloat16)


def halves(a):
    high = a.astype(jnp.bfloat16)
    return [high, (a - high.astype(F32)).astype(jnp.bfloat16)]


def dot(*terms):
    left = jnp.concatenate([h for a, _ in terms for h in halves(a)], axis=1)
    right = jnp.concatenate([m for _, m in terms for _ in (0, 1)], axis=0)
    return jnp.dot(left, right, preferred_element_type=F32)


def turn(v, by, axis):
    return pltpu.roll(v, by % v.shape[axis], axis)


def z_sum(v):
    lane = iota(v.shape[0], 1)
    below = jnp.where(lane == 0, 0.0, turn(v, 1, 1))
    return below + jnp.where(lane == 127, 0.0, turn(v, -1, 1))


def beside(ref, k, v, start, rows):
    return ref[k, pl.ds(start - 1, rows)] + ref[k, pl.ds(start + 1, rows)] + z_sum(v)


def windowed(ref, k, v, rows, at):
    below = jnp.where(at == 0, 0.0, ref[k, pl.ds(7, rows)])
    above = jnp.where(at == WINDOW - 1, 0.0, ref[k, pl.ds(9, rows)])
    return below + above + turn(v, 1, 1) + turn(v, -1, 1)


def inside(at, size):
    return (at >= 0) & (at < size)


def every_other(ref, k, start, rows):
    return ref[k, pl.ds(start, rows, stride=2), :]


def row_pairs(ref, k, start, rows):
    return every_other(ref, k, start, rows) + every_other(ref, k, start + 1, rows)


def gather(both, rest, k, at_both, at_rest, rows, at=None):
    below, above = every_other(both, k, at_both - 1, rows), every_other(both, k, at_both + 2, rows)
    if at is not None:
        below = jnp.where(at == 0, 0.0, below)
        above = jnp.where(at == WINDOW // 2 - 1, 0.0, above)
    own = row_pairs(both, k, at_both, rows)
    return row_pairs(rest, k, at_rest, rows) + own + below + above, own


def pack_kernel(b, c, se, so, sides, first, last, sem):
    copies = []
    for n, ref in enumerate((b, c)):
        copies.append(pltpu.make_async_copy(ref.at[:, pl.ds(0, 8)], first.at[n], sem.at[2 * n]))
        copies.append(pltpu.make_async_copy(ref.at[:, pl.ds(56, 8)], last.at[n], sem.at[2 * n + 1]))
    for copy in copies:
        copy.start()
    y_even = (lax.axis_index("agg") & 1) == 0
    for n in (0, 1):
        for copy in copies[2 * n : 2 * n + 2]:
            copy.wait()
        se[n] = jnp.where(y_even, last[n, :, 4:8], first[n, :, 0:4])
        so[n] = jnp.where(y_even, first[n, :, 0:4], last[n, :, 4:8])
    sides[0], sides[1] = first[0], last[0]


def smoothed(v, w, q, p0, p, start, rows):
    at = pl.ds(start, rows)
    vv = v[p, at]
    near = v[p - 1, at] + v[p + 1, at] + beside(v, p, vv, start, rows)
    qq = 0.4 * vv + w[p, at] * near
    q[p, at] = qq
    p0[p, pl.ds(start - 8, rows)] = qq + OMEGA * vv


def child_sums(q, own1, rest1, k, start, rows, bb, end=None):
    at, p = pl.ds(start, rows), 2 * k
    if end is not None:
        both, outer = q[end[0], at], q[end[1], at]
    else:
        both, outer = q[p, at] + q[p + 1, at], q[p - 1, at] + q[p + 2, at]
    own1[k, at] = both
    rest1[k, pl.ds(start - 8, rows)] = 0.04 * bb + (both + outer)


def own_kernel(b, c, v, w, p0, own1, rest1, c1, q, bv, cv, cs, sem):
    copies = []
    for n in range(4):
        part = pl.ds(4 * n, 4)
        for i, (x, y) in enumerate(((b, bv), (c, cv))):
            copies.append(pltpu.make_async_copy(x.at[part], y.at[part], sem.at[2 * n + i]))
    for copy in copies:
        copy.start()
    for n in range(4):
        for copy in copies[2 * n : 2 * n + 2]:
            copy.wait()
        for p in range(4 * n, 4 * n + 4):
            ww = OMEGA / (6.0 + cv[p])
            w[p, 16:80] = ww
            v[p, 16:80] = ww * bv[p]
        for k in (2 * n, 2 * n + 1):
            cs[k] = cv[2 * k] + cv[2 * k + 1]
    loop(1, 15, STEPS[1], lambda p: smoothed(v, w, q, p0, p, 24, 48))

    def sums(k, end=None):
        child_sums(q, own1, rest1, k, 24, 48, bv[2 * k, 8:56] + bv[2 * k + 1, 8:56], end)

    sums(0, (1, 2))
    loop(1, 7, STEPS[2], sums)
    sums(7, (14, 13))
    pairs = pick("pairs")
    for n in range(2):
        some = range(4 * n, 4 * n + 4)
        cc = 0.5 * dot((jnp.concatenate([row_pairs(cs, k, 0, 32) for k in some], axis=0), pairs))
        for i, k in enumerate(some):
            c1[k, 4:36] = cc[32 * i : 32 * i + 32]


def head_kernel(
    aggs,
    ye, yo, sides, v_in, w_in, p0_in, own_in, rest_in, c_in,
    v, w, p0, own1, rest1, c1, b1, edge, se, so,
    q, bl, bh, cs,
):
    bi, ai = lax.axis_index("blk"), lax.axis_index("agg")
    x_even, y_even = (bi & 1) == 0, (ai & 1) == 0
    y_lo = jnp.where(ai > 0, OMEGA, 0.0)
    y_hi = jnp.where(ai < aggs - 1, OMEGA, 0.0)
    rows = pl.ds(8, 80)

    def halo(k):
        csum = []
        for first, scale, start in ((jnp.logical_not(y_even), y_lo, 12), (y_even, y_hi, 80)):
            got = []
            for p in (2 * k, 2 * k + 1):
                bb, cc = [jnp.where(first, ye[n, p], yo[n, p]) for n in (0, 1)]
                ww = scale / (6.0 + cc)
                w[p, pl.ds(start, 4)] = ww
                v[p, pl.ds(start, 4)] = ww * bb
                got.append((bb, cc))
            csum.append(got[0][1] + got[1][1])
            bsum = got[0][0] + got[1][0]
            if start == 12:
                bl[k, 4:8] = bsum
            else:
                bh[k, 8:12] = bsum
        bl[k, 8:16] = sides[0, 2 * k] + sides[0, 2 * k + 1]
        bh[k, 0:8] = sides[1, 2 * k] + sides[1, 2 * k + 1]
        cs[k, 0:4] = csum[0]
        cs[k, 4:8] = csum[1]

    loop(0, 8, STEPS[0], halo)

    def smooth(p):
        for start in (8, 72):
            smoothed(v, w, q, p0, p, start, 16)

    loop(1, 15, STEPS[1], smooth)
    for n, p, inner in ((0, 0, 1), (3, 15, 14)):
        vv, ww = v[p, rows], w[p, rows]
        edge[n] = 0.4 * vv + ww * (v[inner, rows] + beside(v, p, vv, 8, 80))
        edge[n + 1] = ww
        edge[n + 2] = vv

    def sums(k, end=None):
        child_sums(q, own1, rest1, k, 8, 16, bl[k], end)
        child_sums(q, own1, rest1, k, 72, 16, bh[k], end)

    sums(0, (1, 2))
    loop(1, 7, STEPS[2], sums)
    sums(7, (14, 13))
    pairs, near = pick("pairs"), pick("beside")
    cc = 0.5 * dot((jnp.concatenate([row_pairs(cs, k, 0, 4) for k in range(8)], axis=0), pairs))
    for k in range(8):
        c1[k, 4:36] = c_in[k, 4:36]
        c1[k, 2:4] = cc[4 * k : 4 * k + 2]
        c1[k, 36:38] = cc[4 * k + 2 : 4 * k + 4]

    def products(n):
        ends, mids = [], []
        for k in (2 * n, 2 * n + 1):
            end, mid = gather(own1, rest1, k, 8, 0, 40)
            ends.append(end)
            mids.append(mid)
        bb = dot((jnp.concatenate(ends, axis=0), pairs), (jnp.concatenate(mids, axis=0), near))
        for i in (0, 1):
            b1[2 * n + i] = 0.5 * bb[40 * i : 40 * i + 40]

    loop(0, 4, STEPS[3], products)
    for ref, up in ((se, x_even), (so, jnp.logical_not(x_even))):
        for i in range(3):
            ref[88 + 72 * i : 160 + 72 * i] = jnp.where(up, edge[3 + i, 4:76], edge[i, 4:76])
        for i in (0, 1):
            mix = jnp.where(up, b1[6 + i], b1[i]) + turn(jnp.where(up, c1[6 + i], c1[i]), 64, 1)
            ref[34 * i : 34 * i + 34] = mix[3:37]
        third = OMEGA / (6.0 + jnp.where(up, c1[5], c1[2])) * jnp.where(up, b1[5], b1[2])
        ref[68:85] = third[3:20] + turn(third, 64, 1)[20:37]
        ref[85:88] = jnp.zeros((3, 128), F32)


def mid_kernel(
    blocks, aggs,
    b1in, c1in, edge, xe, xo,
    pe, e1out, w1out, bc2, se, so,
    far, s4, r4, b1, c1, e1, own2, rest2,
):
    bi, ai = lax.axis_index("blk"), lax.axis_index("agg")
    x_even, y_even = (bi & 1) == 0, (ai & 1) == 0
    pairs, sides = pick("pairs"), pick("beside")
    has_lo, has_hi = bi > 0, bi < blocks - 1
    lane1 = iota(40, 1) < 64

    def fetch(lo, start, rows):
        first = x_even if lo else jnp.logical_not(x_even)
        return jnp.where(first, xo[start : start + rows], xe[start : start + rows])

    for i, (lo, there) in enumerate(((True, has_lo), (False, has_hi))):
        for n in range(3):
            far[3 * i + n, 4:76] = jnp.where(there, fetch(lo, 88 + 72 * n, 72), 0.0)
        gb, wb, vb = [far[3 * i + n] for n in range(3)]
        g, w, v = [edge[3 * i + n] for n in range(3)]
        mine, other = g + w * vb, gb + wb * v
        here, there = (1, 0) if lo else (2, 3)
        pe[here] = mine + OMEGA * v
        pe[there] = other + OMEGA * vb
        s4[2 * i, pl.ds(8, 80)] = mine
        s4[2 * i + 1, pl.ds(8, 80)] = other
        r4[2 * i] = mine + other
        r4[2 * i + 1] = mine + other
        for n in (0, 1):
            mix = fetch(lo, 34 * n, 34)
            k = 1 + n if lo else 11 + n
            b1[k, 3:37] = jnp.where(lane1[:34], mix, 0.0)
            c1[k, 3:37] = jnp.where(lane1[:34], turn(mix, -64, 1), 0.0)
        k = 0 if lo else 13
        there = inside(bi * 8 + k - 3, 8 * blocks) & lane1[:17]
        mix = fetch(lo, 68, 17)
        for start, part in ((3, mix), (20, turn(mix, -64, 1))):
            e1[k, start : start + 17] = jnp.where(there & inside(ai * 32 - 4 + start + iota(17, 0), 32 * aggs), part, 0.0)
    for k in range(8):
        b1[k + 3] = b1in[k]
        c1[k + 3] = c1in[k]
    ends, mids = [], []
    for i in range(4):
        end, mid = gather(s4, r4, i, 8, 0, 40)
        ends.append(end)
        mids.append(mid)
    more = dot((jnp.concatenate(ends, axis=0), pairs), (jnp.concatenate(mids, axis=0), sides))
    for i, k in enumerate((3, 2, 10, 11)):
        b1[k] = b1[k] + 0.5 * more[40 * i : 40 * i + 40]

    row1 = ai * 32 - 4 + iota(40, 0)
    keep1 = inside(row1, 32 * aggs) & lane1
    for k in range(1, 13):
        ok = keep1 & inside(bi * 8 + k - 3, 8 * blocks)
        ww = jnp.where(ok, OMEGA / (6.0 + c1[k]), 0.0)
        ee = jnp.where(ok, ww * b1[k], 0.0)
        e1[k] = ee
        w1out[k - 1], e1out[k - 1] = ww, ee

    at2 = (ai * 16 + iota(16, 0)) & (WINDOW // 2 - 1)
    lane16 = iota(16, 1)
    ends, mids, csums = [], [], []
    for k in range(6):
        p = 1 + 2 * k
        both = e1[p] + e1[p + 1]
        own2[k] = both
        rest2[k] = 0.2 * (b1[p] + b1[p + 1]) + (both + (e1[p - 1] + e1[p + 2]))
        end, mid = gather(own2, rest2, k, 4, 4, 16, at2)
        ends.append(end)
        mids.append(mid)
        csums.append(row_pairs(c1, p, 4, 16) + row_pairs(c1, p + 1, 4, 16))
    bb2 = dot((jnp.concatenate(ends, axis=0), pairs), (jnp.concatenate(mids, axis=0), sides))
    cc2 = dot((jnp.concatenate(csums, axis=0), pairs))
    for k in range(6):
        bb = jnp.where(lane16 < 32, 0.5 * bb2[16 * k : 16 * k + 16], 0.0)
        cc = jnp.where(lane16 < 32, 0.5 * cc2[16 * k : 16 * k + 16], 0.0)
        bc2[k] = bb + turn(cc, 32, 1)
    for ref, lo_side in ((se, jnp.logical_not(y_even)), (so, y_even)):
        for k in range(3):
            both = bc2[2 * k] + turn(bc2[2 * k + 1], 64, 1)
            ref[k, 0:5] = jnp.where(lo_side, both[0:5], both[11:16])
            ref[k, 5:8] = jnp.zeros((3, 128), F32)
        for n in range(4):
            both = jnp.where(lane1, e1[3 + 2 * n], 0.0) + turn(jnp.where(lane1, e1[4 + 2 * n], 0.0), 64, 1)
            ref[n // 2, 5 + n % 2 : 6 + n % 2] = jnp.where(lo_side, both[5:6], both[34:35])


def halves_of(v, h):
    return jnp.where(iota(v.shape[0], 1) < 64, turn(v, -64, 1) if h else v, 0.0)


def join_kernel(bc2, ye, yo, wide, se, so):
    bi, ai = lax.axis_index("blk"), lax.axis_index("agg")
    x_even, y_even = (bi & 1) == 0, (ai & 1) == 0
    for k in range(6):
        lo = halves_of(jnp.where(y_even, yo[k // 2], ye[k // 2]), k % 2)
        hi = halves_of(jnp.where(y_even, ye[k // 2], yo[k // 2]), k % 2)
        wide[k] = jnp.zeros((32, 128), F32)
        wide[k, 3:8] = lo[0:5]
        wide[k, 8:24] = bc2[k]
        wide[k, 24:29] = hi[0:5]
    for k in range(2):
        low, high = wide[2 * k] + turn(wide[2 * k + 1], 64, 1), wide[2 * k + 1] + turn(wide[2 * k + 2], 64, 1)
        se[26 * k : 26 * k + 26] = jnp.where(x_even, low, high)[3:29]
        so[26 * k : 26 * k + 26] = jnp.where(x_even, high, low)[3:29]
    for ref, k in ((se, (4, 5)), (so, (5, 4))):
        end = jnp.where(x_even, wide[k[0]], wide[k[1]])
        ref[52:65] = end[3:16] + turn(end, 64, 1)[16:29]
        ref[65:72] = jnp.zeros((7, 128), F32)


def up_kernel(
    blocks, aggs,
    p0, pe, v0, w0, e1in, w1, wide, ye, yo, xe, xo,
    out,
    bc, e2, w2, b2, c2, own2, rest2, m2, t2, e1, m1, mf, made, sem,
):
    bi, ai = lax.axis_index("blk"), lax.axis_index("agg")
    x_even, y_even = (bi & 1) == 0, (ai & 1) == 0
    pairs, sides, copies = pick("pairs"), pick("beside"), pick("copies")

    for lo in (0, 1):
        first = jnp.logical_not(x_even) if lo else x_even
        for n in range(2):
            both = jnp.where(first, xo[26 * n : 26 * n + 26], xe[26 * n : 26 * n + 26])
            for h in (0, 1):
                bc[5 * lo + 2 * n + h, 3:29] = halves_of(both, h)
        both = jnp.where(first, xo[52:65], xe[52:65])
        for h in (0, 1):
            bc[5 * lo + 4, 3 + 13 * h : 16 + 13 * h] = halves_of(both, h)

    def source(k):
        return wide[k - 4] if 5 <= k < 9 else bc[k if k < 5 else k - 4]

    row2 = ai * 16 - 8 + iota(32, 0)
    lane2 = iota(32, 1) < 32
    keep2 = inside(row2, 16 * aggs) & lane2
    for k in range(14):
        mix = source(k)
        bb = jnp.where(lane2, mix, 0.0)
        cc = jnp.where(lane2, turn(mix, -32, 1), 0.0)
        ww = jnp.where(keep2 & inside(bi * 4 + k - 5, 4 * blocks), OMEGA / (6.0 + cc), 0.0)
        b2[k], c2[k], w2[k], e2[k] = bb, cc, ww, ww * bb

    row3 = ai * 8 - 4 + iota(16, 0)
    at3 = row3 & (WINDOW // 2 - 1)
    ends, mids, sums = [], [], []
    for j in range(6):
        k = 1 + 2 * j
        both = e2[k] + e2[k + 1]
        own2[j, 8:40] = both
        rest2[j] = 0.2 * (b2[k] + b2[k + 1]) + (both + (e2[k - 1] + e2[k + 2]))
        end, mid = gather(own2, rest2, j, 8, 0, 16, at3)
        ends.append(end)
        mids.append(mid)
        sums.append(row_pairs(c2, k, 0, 16) + row_pairs(c2, k + 1, 0, 16))
    bb3 = dot((jnp.concatenate(ends, axis=0), pairs), (jnp.concatenate(mids, axis=0), sides))
    cc3 = dot((jnp.concatenate(sums, axis=0), pairs))
    keep3 = inside(row3, 8 * aggs) & (iota(16, 1) < 16)
    e3, w3 = [], []
    for j in range(6):
        bb, cc = 0.5 * bb3[16 * j : 16 * j + 16], 0.5 * cc3[16 * j : 16 * j + 16]
        ok = keep3 & inside(bi * 2 + j - 2, 2 * blocks)
        ww = jnp.where(ok, OMEGA / (6.0 + cc), 0.0)
        w3.append(ww)
        e3.append(jnp.where(ok, ww * bb, 0.0))
    solved = []
    for j in range(1, 5):
        v = e3[j]
        near = e3[j - 1] + e3[j + 1] + turn(v, 1, 0) + turn(v, -1, 0) + turn(v, 1, 1) + turn(v, -1, 1)
        solved.append(1.2 * v + w3[j] * near)
    wider = dot((jnp.concatenate(solved, axis=0), copies))
    for k in range(3, 11):
        j = (k - 3) // 2
        for r in (0, 1):
            m2[k, pl.ds(8 + r, 16, stride=2), :] = every_other(e2, k, r, 16) + wider[16 * j : 16 * j + 16]
    at2 = row2 & (WINDOW - 1)
    rows = pl.ds(8, 32)
    solved = []
    for k in range(4, 10):
        v = m2[k, rows]
        near = m2[k - 1, rows] + m2[k + 1, rows] + windowed(m2, k, v, 32, at2)
        solved.append(0.2 * v + e2[k] + w2[k] * near)
    wider = dot((jnp.concatenate(solved, axis=0), copies))
    for k in range(6):
        t2[k] = wider[32 * k : 32 * k + 32]

    for k in range(12):
        e1[k] = e1in[k]
    for n in range(8):
        k, j = n // 4, 5 + n % 4 // 2
        mine, other = halves_of(ye[k], n % 2)[j : j + 1], halves_of(yo[k], n % 2)[j : j + 1]
        e1[n + 2, 2:3] = jnp.where(y_even, other, mine)
        e1[n + 2, 37:38] = jnp.where(y_even, mine, other)
    for k in range(12):
        for r in (0, 1):
            m1[k, pl.ds(8 + r, 20, stride=2), :] = every_other(e1, k, r, 20) + t2[k // 2, 6:26]
    at1 = (ai * 32 - 4 + iota(40, 0)) & (WINDOW - 1)

    def fine(n, first):
        rows = pl.ds(8, 40)
        solved = []
        for k in (2 * n, 2 * n + 1):
            v = m1[k + 1, rows]
            near = m1[k, rows] + m1[k + 2, rows] + windowed(m1, k + 1, v, 40, at1)
            solved.append(0.2 * v + e1[k + 1] + w1[k + 1] * near)
        wider = dot((jnp.concatenate(solved, axis=0), copies))
        for k, (ref, p) in enumerate(first(4 * n)):
            for r in (0, 1):
                if ref is not None:
                    old = ref[p, pl.ds(r, 40, stride=2), :]
                    i = 40 * (k // 2)
                    mf[4 * n + k, pl.ds(8 + r, 40, stride=2), :] = old + wider[i : i + 40]

    rows = pl.ds(16, 64)
    writes = []
    for n in range(5):
        old = [(p0, 4 * n - 2 + k) for k in range(4)]
        if n == 0:
            old[:3] = (None, 0), (pe, 0), (pe, 1)
        if n == 4:
            old[1:] = (pe, 2), (pe, 3), (None, 0)
        fine(n, lambda _: old)
        for k in range(max(4 * n - 3, 0), min(4 * n + 1, 16)):
            m = mf[k + 2, rows]
            near = mf[k + 1, rows] + mf[k + 3, rows] + beside(mf, k + 2, m, 16, 64)
            made[k] = 0.2 * m + v0[k, rows] + w0[k, rows] * near
            writes.append(pltpu.make_async_copy(made.at[k], out.at[k], sem.at[k]))
            writes[-1].start()
    for copy in writes:
        copy.wait()


def swaps(size, apart):
    inner, outer = [], []
    for i in range(size):
        inner.append((i, i ^ apart))
        outer.append((i, (i + apart) % size if i & apart else (i - apart) % size))
    return inner, outer


def shards(b, c):
    blocks, aggs = lax.axis_size("blk"), lax.axis_size("agg")
    near_in, near_out = swaps(blocks, 1)
    side_in, side_out = swaps(aggs, 1)

    hbm = pl.BlockSpec(memory_space=pltpu.HBM)
    b, c = [pltpu.with_memory_space_constraint(x, pltpu.HBM) for x in (b, c)]
    faces = shape(2, 16, 4, 128)
    se, so, sides = call(
        pack_kernel,
        (faces, faces, shape(2, 16, 8, 128)),
        [(2, 16, 8, 128), (2, 16, 8, 128), pltpu.SemaphoreType.DMA((4,))],
        b, c,
        specs=[hbm, hbm],
    )
    yo = lax.ppermute(so, "agg", side_out)
    ye = lax.ppermute(se, "agg", side_in)

    mid, big = (12, 40, 128), shape(16, 96, 128)
    fields = (big, big, shape(16, 80, 128), shape(8, 96, 128), shape(8, 80, 128))
    v, w, p0, own1, rest1, c1 = call(
        own_kernel,
        fields + (shape(8, 40, 128),),
        [(16, 96, 128), (16, 64, 128), (16, 64, 128), (8, 64, 128), pltpu.SemaphoreType.DMA((8,))],
        b, c,
        specs=[hbm, hbm],
    )
    v, w, p0, _, _, c1, b1, edge, se, so = call(
        lambda *refs: head_kernel(aggs, *refs),
        fields + (shape(8, 40, 128), shape(8, 40, 128), shape(6, 80, 128), shape(304, 128), shape(304, 128)),
        [(16, 96, 128), (8, 16, 128), (8, 16, 128), (8, 8, 128)],
        ye, yo, sides, v, w, p0, own1, rest1, c1,
        aliases={3 + i: i for i in range(5)},
    )
    xo = lax.ppermute(so, "blk", near_out)
    xe = lax.ppermute(se, "blk", near_in)
    tall = (14, 40, 128)
    pe, e1, w1, bc2, se, so = call(
        lambda *refs: mid_kernel(blocks, aggs, *refs),
        (shape(4, 80, 128), shape(*mid), shape(*mid), shape(6, 16, 128), shape(3, 8, 128), shape(3, 8, 128)),
        [(6, 80, 128), (4, 96, 128), (4, 80, 128), tall, tall, tall, (6, 40, 128), (6, 40, 128)],
        b1, c1, edge, xe, xo,
    )
    yo = lax.ppermute(so, "agg", side_out)
    ye = lax.ppermute(se, "agg", side_in)
    wide, se, so = call(
        join_kernel,
        (shape(6, 32, 128), shape(72, 128), shape(72, 128)),
        [],
        bc2, ye, yo,
    )
    xo = lax.ppermute(so, "blk", near_out)
    xe = lax.ppermute(se, "blk", near_in)
    small = (14, 32, 128)
    (out,) = call(
        lambda *refs: up_kernel(blocks, aggs, *refs),
        (shape(16, 64, 128),),
        [(10, 32, 128)] + [small] * 4 + [(6, 48, 128), (6, 32, 128), (14, 48, 128), (6, 32, 128), mid, (12, 56, 128), (20, 96, 128),
                       (16, 64, 128), pltpu.SemaphoreType.DMA((16,))],
        p0, pe, v, w, e1, w1, wide, ye, yo, xe, xo,
        out_specs=(hbm,),
    )
    return out


def solution(mesh):
    placed = (P("blk", "agg", None), P("blk", "agg", None))
    return jax.shard_map(shards, mesh=mesh, in_specs=placed, out_specs=P("blk", "agg", None), check_vma=False)
```
